32 devices in a mesh: dp: 8 (over z, x), tensor: 4 (over y, core).
Axes of the slice: x: 2, y: 2, z: 4, core: 2. Of those that a mesh axis runs over, the one named last changes fastest.
Arguments:
- layer_input: bfloat16 [5120, 2304], P(('dp', 'tensor')), may hold values from -6 to 6
- cotangent: bfloat16 [5120, 2304], P(('dp', 'tensor')), may hold values from -6 to 6
- norm_gains: bfloat16 [4, 2304], replicated, may hold values from 0.25 to 1.75
- w_query: bfloat16 [2304, 2048], P('dp', 'tensor'), may hold values from -0.125 to 0.125
- w_key: bfloat16 [2304, 1024], P('dp', 'tensor'), may hold values from -0.125 to 0.125
- w_value: bfloat16 [2304, 1024], P('dp', 'tensor'), may hold values from -0.125 to 0.125
- w_output: bfloat16 [2048, 2304], P('tensor', 'dp'), may hold values from -0.125 to 0.125
- w_gate: bfloat16 [2304, 9216], P('dp', 'tensor'), may hold values from -0.125 to 0.125
- w_up: bfloat16 [2304, 9216], P('dp', 'tensor'), may hold values from -0.125 to 0.125
- w_down: bfloat16 [9216, 2304], P('tensor', 'dp'), may hold values from -0.0625 to 0.0625
- query_shrink: bfloat16 [8, 16, 2304], replicated, may hold values from -0.125 to 0.125
- key_shrink: bfloat16 [8, 16, 2304], replicated, may hold values from -0.125 to 0.125
- value_shrink: bfloat16 [8, 16, 2304], replicated, may hold values from -0.125 to 0.125
- output_shrink: bfloat16 [8, 16, 2048], P(None, None, 'tensor'), may hold values from -0.125 to 0.125
- gate_shrink: bfloat16 [8, 16, 2304], replicated, may hold values from -0.125 to 0.125
- up_shrink: bfloat16 [8, 16, 2304], replicated, may hold values from -0.125 to 0.125
- down_shrink: bfloat16 [8, 16, 9216], P(None, None, 'tensor'), may hold values from -0.0625 to 0.0625
- query_expand: bfloat16 [8, 16, 2048], P(None, None, 'tensor'), may hold values from -0.75 to 0.75
- key_expand: bfloat16 [8, 16, 1024], P(None, None, 'tensor'), may hold values from -0.75 to 0.75
- value_expand: bfloat16 [8, 16, 1024], P(None, None, 'tensor'), may hold values from -0.75 to 0.75
- output_expand: bfloat16 [8, 16, 2304], replicated, may hold values from -0.75 to 0.75
- gate_expand: bfloat16 [8, 16, 9216], P(None, None, 'tensor'), may hold values from -0.75 to 0.75
- up_expand: bfloat16 [8, 16, 9216], P(None, None, 'tensor'), may hold values from -0.75 to 0.75
- down_expand: bfloat16 [8, 16, 2304], replicated, may hold values from -0.75 to 0.75
- adapter_ids: int32 [8], P('dp'), may hold values from 0 to 7
- parent_segments: int32 [8, 13], P('dp'), may hold values from 0 to 4, as said below
- segment_ids: int32 [5120], P('dp'), may hold values from 0 to 12, as said below
Outputs:
- layer_output: bfloat16 [5120, 2304], P(('dp', 'tensor'))
- input_grad: float32 [5120, 2304], P(('dp', 'tensor'))
- shrink_query: float32 [8, 16, 2304], replicated
- shrink_key: float32 [8, 16, 2304], replicated
- shrink_value: float32 [8, 16, 2304], replicated
- shrink_output: float32 [8, 16, 2048], P(None, None, 'tensor')
- shrink_gate: float32 [8, 16, 2304], replicated
- shrink_up: float32 [8, 16, 2304], replicated
- shrink_down: float32 [8, 16, 9216], P(None, None, 'tensor')
- expand_query: float32 [8, 16, 2048], P(None, None, 'tensor')
- expand_key: float32 [8, 16, 1024], P(None, None, 'tensor')
- expand_value: float32 [8, 16, 1024], P(None, None, 'tensor')
- expand_output: float32 [8, 16, 2304], replicated
- expand_gate: float32 [8, 16, 9216], P(None, None, 'tensor')
- expand_up: float32 [8, 16, 9216], P(None, None, 'tensor')
- expand_down: float32 [8, 16, 2304], replicated
The draws below stay inside these ranges and needn't reach their ends.
Inputs may be any that keep to these rules, and one draw needn't show every extreme that they name: `parent_segments`: in each tree, segment 0 is the trunk and is its own parent; segments 1 to 4 have parent 0; each of the other segments has a branch (1 to 4) as parent, and every branch is the parent of exactly 2 of them. `segment_ids`: the first 256 tokens of each tree are segment 0; the rest are 12 contiguous runs of 32 tokens, one run for each other segment, in any order.
All inputs are finite; a program needn't handle non-finite values.
Results may differ from the reference program's by a relative error of at most 0.028.
Values may be sent and summed in bfloat16 or wider, within the bound.
No kernel may reach another device: no remote copies, remote signals or barrier semaphores. Data moves between devices by JAX's collectives and lax.ppermute only.
A program may use at most 256 MiB of HBM per device.

```python
import math
import jax
import jax.numpy as jnp
from jax import lax

D = 2304
QUERY_HEADS = 8
KEY_VALUE_HEADS = 4
HEAD_WIDTH = 256
FF = 9216
RANK = 16
ADAPTERS = 8
BRANCHES = 4
LEAVES = 8
NSEG = 13
TRUNK = 256
SEG = 32
TREE_LEN = 640
TREES = 8
TOKENS = 5120
QW = 2048
KW = 1024


def tree_shapes(key):
    base_key = jax.random.fold_in(key, 7)

    def one_tree(tree_index):
        tree_key = jax.random.fold_in(base_key, tree_index)
        order_key, leaf_key = jax.random.split(tree_key)
        slot_order = jax.random.permutation(order_key, NSEG - 1).astype(jnp.int32)
        leaf_parent = jax.random.permutation(leaf_key, LEAVES).astype(jnp.int32)
        return (slot_order, leaf_parent)
    return jax.vmap(one_tree)(jnp.arange(TREES, dtype=jnp.int32))


def draw_parent_segments(key, part):
    slot_order, leaf_parent = tree_shapes(key)
    top_parents = jnp.zeros((TREES, 1 + BRANCHES), jnp.int32)
    return jnp.concatenate([top_parents, 1 + leaf_parent // (LEAVES // BRANCHES)], axis=1).astype(jnp.int32)


def draw_segment_ids(key, part):
    slot_order, leaf_parent = tree_shapes(key)
    trunk_ids = jnp.zeros((TREES, TRUNK), jnp.int32)
    branch_ids = jnp.repeat(1 + slot_order, SEG, axis=1)
    return jnp.concatenate([trunk_ids, branch_ids], axis=1).reshape(TOKENS).astype(jnp.int32)


def place_ends(drawn, stream_key, low, high):
    index_at = [jax.random.randint(jax.random.fold_in(stream_key, axis), (), 0, length) for axis, length in enumerate(drawn.shape)]
    longest = drawn.shape.index(max(drawn.shape))
    next_to = index_at[:longest] + [(index_at[longest] + 1) % drawn.shape[longest]] + index_at[longest + 1:]
    return drawn.at[tuple(index_at)].set(low).at[tuple(next_to)].set(high)


def block_scale(stream_key, shape, shards, smallest, high):
    level = 1.0
    for axis_at, parts in shards:
        steps = jax.random.uniform(jax.random.fold_in(jax.random.fold_in(stream_key, 6), axis_at), (parts,), jnp.float32, smallest / len(shards), high / len(shards))
        level = level * jnp.repeat(jnp.exp(steps), shape[axis_at] // parts).reshape((-1,) + (1,) * (len(shape) - 1 - axis_at))
    return level


def noise(stream_key, shape, deviation, most, cuts=(), held_as=jnp.bfloat16):
    entries = jax.random.normal(stream_key, shape, jnp.float32) * deviation
    if len(cuts) > 0:
        entries = block_scale(stream_key, shape, cuts, -0.22, 0.18) * entries
    return jnp.clip(entries, min=-most, max=most).astype(held_as)


def setup_inputs(seed: int = 0) -> dict:
    key_of = jax.random.split(jax.random.key(seed), 28)
    layer_input = noise(key_of[0], (TOKENS, D), 1.0, 6.0, ((0, 32),))
    cotangent = noise(key_of[1], (TOKENS, D), 1.0, 6.0, ((0, 32),))
    norm_gains = jnp.clip(1.0 + 0.15 * jax.random.normal(key_of[2], (4, D), jnp.float32), 0.25, 1.75).astype(jnp.bfloat16)
    w_query = noise(key_of[3], (D, QW), D ** -0.5, 0.125, ((0, 8), (1, 4)))
    w_key = noise(key_of[4], (D, KW), D ** -0.5, 0.125, ((0, 8), (1, 4)))
    w_value = noise(key_of[5], (D, KW), D ** -0.5, 0.125, ((0, 8), (1, 4)))
    w_output = noise(key_of[6], (QW, D), QW ** -0.5, 0.125, ((0, 4), (1, 8)))
    w_gate = noise(key_of[7], (D, FF), D ** -0.5, 0.125, ((0, 8), (1, 4)))
    w_up = noise(key_of[8], (D, FF), D ** -0.5, 0.125, ((0, 8), (1, 4)))
    w_down = noise(key_of[9], (FF, D), FF ** -0.5, 0.0625, ((0, 4), (1, 8)))
    query_shrink = noise(key_of[10], (ADAPTERS, RANK, D), D ** -0.5, 0.125)
    key_shrink = noise(key_of[11], (ADAPTERS, RANK, D), D ** -0.5, 0.125)
    value_shrink = noise(key_of[12], (ADAPTERS, RANK, D), D ** -0.5, 0.125)
    output_shrink = noise(key_of[13], (ADAPTERS, RANK, QW), QW ** -0.5, 0.125, ((2, 4),))
    gate_shrink = noise(key_of[14], (ADAPTERS, RANK, D), D ** -0.5, 0.125)
    up_shrink = noise(key_of[15], (ADAPTERS, RANK, D), D ** -0.5, 0.125)
    down_shrink = noise(key_of[16], (ADAPTERS, RANK, FF), FF ** -0.5, 0.0625, ((2, 4),))
    query_expand = noise(key_of[17], (ADAPTERS, RANK, QW), (4 * RANK) ** -0.5, 0.75, ((2, 4),))
    key_expand = noise(key_of[18], (ADAPTERS, RANK, KW), (4 * RANK) ** -0.5, 0.75, ((2, 4),))
    value_expand = noise(key_of[19], (ADAPTERS, RANK, KW), (4 * RANK) ** -0.5, 0.75, ((2, 4),))
    output_expand = noise(key_of[20], (ADAPTERS, RANK, D), (4 * RANK) ** -0.5, 0.75)
    gate_expand = noise(key_of[21], (ADAPTERS, RANK, FF), (4 * RANK) ** -0.5, 0.75, ((2, 4),))
    up_expand = noise(key_of[22], (ADAPTERS, RANK, FF), (4 * RANK) ** -0.5, 0.75, ((2, 4),))
    down_expand = noise(key_of[23], (ADAPTERS, RANK, D), (4 * RANK) ** -0.5, 0.75)
    adapter_ids = place_ends(jax.random.randint(key_of[24], (TREES,), 0, ADAPTERS), jax.random.fold_in(key_of[24], 1), 0, ADAPTERS - 1).astype(jnp.int32)
    parent_segments = draw_parent_segments(jax.random.fold_in(key_of[27], 71), 0)
    segment_ids = draw_segment_ids(jax.random.fold_in(key_of[27], 71), 0)
    return {"layer_input": layer_input, "cotangent": cotangent, "norm_gains": norm_gains, "w_query": w_query, "w_key": w_key, "w_value": w_value, "w_output": w_output, "w_gate": w_gate, "w_up": w_up, "w_down": w_down, "query_shrink": query_shrink, "key_shrink": key_shrink, "value_shrink": value_shrink, "output_shrink": output_shrink, "gate_shrink": gate_shrink, "up_shrink": up_shrink, "down_shrink": down_shrink, "query_expand": query_expand, "key_expand": key_expand, "value_expand": value_expand, "output_expand": output_expand, "gate_expand": gate_expand, "up_expand": up_expand, "down_expand": down_expand, "adapter_ids": adapter_ids, "parent_segments": parent_segments, "segment_ids": segment_ids}


@jax.custom_vjp
def lower_triangle(v):
    return lax.optimization_barrier(v.astype(jnp.bfloat16)).astype(jnp.float32)

@jax.custom_vjp
def low_back(v):
    return v

def low_keep(v):
    return (lower_triangle(v), None)

def low_pass(kept, grad):
    return (grad,)

def back_keep(v):
    return (v, None)

def back_low(kept, grad):
    return (lower_triangle(grad),)
lower_triangle.defvjp(low_keep, low_pass)
low_back.defvjp(back_keep, back_low)
precise = lax.Precision.HIGHEST

def matmul(former, latter):
    return jnp.dot(former, latter, precision=precise)

def rms_scale(value_rows, gain_row):
    inverse = lax.rsqrt(lax.optimization_barrier(jnp.mean(value_rows * value_rows, axis=-1, keepdims=True)) + 1e-06)
    return value_rows * inverse * gain_row

def pick_from(lookup, indices, labels):
    return lax.optimization_barrier(jnp.sum(jnp.where(indices[:, None] == labels[None, :], lookup[None, :], 0), axis=1))

def tree_tables(segments, parents):
    count_seg = parents.shape[0]
    sequence_length = segments.shape[0]
    labels = jnp.arange(count_seg, dtype=jnp.int32)
    places = jnp.arange(sequence_length, dtype=jnp.int32)
    member = segments[None, :] == labels[:, None]
    starts = lax.optimization_barrier(jnp.min(jnp.where(member, places[None, :], sequence_length), axis=1)).astype(jnp.int32)
    counts = lax.optimization_barrier(jnp.sum(member.astype(jnp.int32), axis=1)).astype(jnp.int32)
    grands = pick_from(parents, parents, labels)
    offsets = jnp.where(parents != labels, pick_from(counts, parents, labels), 0) + jnp.where(grands != parents, pick_from(counts, grands, labels), 0)
    tok_start = pick_from(starts, segments, labels)
    tok_offset = pick_from(offsets, segments, labels)
    tok_parent = pick_from(parents, segments, labels)
    tok_grand = pick_from(grands, segments, labels)
    positions = (places - tok_start + tok_offset).astype(jnp.float32)
    same_seg = (segments[None, :] == segments[:, None]) & (places[None, :] <= places[:, None])
    from_parent = (segments[None, :] == tok_parent[:, None]) & (tok_parent != segments)[:, None]
    from_grand = (segments[None, :] == tok_grand[:, None]) & (tok_grand != tok_parent)[:, None]
    visible = same_seg | from_parent | from_grand
    inv_freq = jnp.exp(jnp.arange(HEAD_WIDTH // 2, dtype=jnp.float32) * (-2.0 * math.log(10000.0) / HEAD_WIDTH))
    angles = positions[:, None] * inv_freq[None, :]
    return (visible, jnp.cos(angles), jnp.sin(angles))

def apply_rotary(value_rows, cos_rows, sin_rows):
    half_size = value_rows.shape[-1] // 2
    front_half = value_rows[..., :half_size]
    back_half = value_rows[..., half_size:]
    return jnp.concatenate([front_half * cos_rows - back_half * sin_rows, back_half * cos_rows + front_half * sin_rows], axis=-1)

def select(onehot, stacked):
    return jnp.einsum('e,erc->rc', onehot, stacked, precision=precise)

def project(inputs, weight, shrink, expand):
    inner_rank = matmul(inputs, shrink.T)
    return matmul(inputs, weight) + matmul(inner_rank, expand)

def tree_layer(inputs, adapters, onehot, weights, norm_gain, visible, cos_rows, sin_rows):
    w_query, w_key, w_value, w_output, w_gate, w_up, w_down = weights
    chosen = [select(onehot, stacked) for stacked in adapters]
    s_query, s_key, s_value, s_output, s_gate, s_up, s_down = chosen[:7]
    e_query, e_key, e_value, e_output, e_gate, e_up, e_down = chosen[7:]
    sequence_length = inputs.shape[0]
    head_groups = QUERY_HEADS // KEY_VALUE_HEADS
    normed = lower_triangle(rms_scale(inputs, norm_gain[0]))
    query_pre = low_back(project(normed, w_query, s_query, e_query))
    key_before_rotation = low_back(project(normed, w_key, s_key, e_key))
    value_projected = low_back(project(normed, w_value, s_value, e_value))
    cosine_per_head = cos_rows[:, None, :]
    sine_per_head = sin_rows[:, None, :]
    query_rows = lower_triangle(apply_rotary(query_pre.reshape(sequence_length, QUERY_HEADS, HEAD_WIDTH), cosine_per_head, sine_per_head) * HEAD_WIDTH ** (-0.5))
    rotated_keys = lower_triangle(apply_rotary(key_before_rotation.reshape(sequence_length, KEY_VALUE_HEADS, HEAD_WIDTH), cosine_per_head, sine_per_head))
    value_rows = lower_triangle(value_projected).reshape(sequence_length, KEY_VALUE_HEADS, HEAD_WIDTH)
    grouped_heads = query_rows.reshape(sequence_length, KEY_VALUE_HEADS, head_groups, HEAD_WIDTH)
    scores = low_back(jnp.einsum('qngd,knd->ngqk', grouped_heads, rotated_keys, precision=precise))
    capped = 50.0 * jnp.tanh(scores / 50.0)
    masked = jnp.where(visible[None, None], capped, -1e+30)
    attn_probs = lower_triangle(jax.nn.softmax(masked, axis=-1))
    mixed_heads = jnp.einsum('ngqk,knd->qngd', attn_probs, value_rows, precision=precise).reshape(sequence_length, QUERY_HEADS * HEAD_WIDTH)
    mixed_heads = lower_triangle(low_back(mixed_heads))
    attended = low_back(project(mixed_heads, w_output, s_output, e_output))
    residual = inputs + rms_scale(attended, norm_gain[1])
    normed_ffn = lower_triangle(rms_scale(residual, norm_gain[2]))
    gate_pre = low_back(project(normed_ffn, w_gate, s_gate, e_gate))
    up_pre = low_back(project(normed_ffn, w_up, s_up, e_up))
    hidden = lower_triangle(jax.nn.gelu(gate_pre, approximate=True) * up_pre)
    ffn_out = low_back(project(hidden, w_down, s_down, e_down))
    return residual + rms_scale(ffn_out, norm_gain[3])

def reference(layer_input, cotangent, norm_gains, w_query, w_key, w_value, w_output, w_gate, w_up, w_down, query_shrink, key_shrink, value_shrink, output_shrink, gate_shrink, up_shrink, down_shrink, query_expand, key_expand, value_expand, output_expand, gate_expand, up_expand, down_expand, adapter_ids, parent_segments, segment_ids):
    weights = tuple((matrix.astype(jnp.float32) for matrix in (w_query, w_key, w_value, w_output, w_gate, w_up, w_down)))
    norm_gain = norm_gains.astype(jnp.float32)
    adapters = tuple((matrix.astype(jnp.float32) for matrix in (query_shrink, key_shrink, value_shrink, output_shrink, gate_shrink, up_shrink, down_shrink, query_expand, key_expand, value_expand, output_expand, gate_expand, up_expand, down_expand)))
    tree_inputs = layer_input.astype(jnp.float32).reshape(TREES, TREE_LEN, D)
    tree_cot = cotangent.astype(jnp.float32).reshape(TREES, TREE_LEN, D)
    tree_segs = segment_ids.reshape(TREES, TREE_LEN)
    labels = jnp.arange(ADAPTERS, dtype=jnp.int32)

    def one_tree(running, pieces):
        inputs, grad_out, segments, parents, chosen_id = pieces
        visible, cos_rows, sin_rows = tree_tables(segments, parents)
        onehot = (labels == chosen_id).astype(jnp.float32)

        def layer_fn(layer_rows, adapter_set):
            return tree_layer(layer_rows, adapter_set, onehot, weights, norm_gain, visible, cos_rows, sin_rows)
        output, pullback = jax.vjp(layer_fn, inputs, adapters)
        grad_in, grad_adapt = pullback(grad_out)
        running = tuple((kept_sum + added for kept_sum, added in zip(running, grad_adapt)))
        return (running, (output.astype(jnp.bfloat16), grad_in))
    zeros_start = tuple((jnp.zeros_like(matrix) for matrix in adapters))
    totals, (outputs, grads_in) = lax.scan(one_tree, zeros_start, (tree_inputs, tree_cot, tree_segs, parent_segments, adapter_ids))
    return (outputs.reshape(TOKENS, D), grads_in.reshape(TOKENS, D), totals[0], totals[1], totals[2], totals[3], totals[4], totals[5], totals[6], totals[7], totals[8], totals[9], totals[10], totals[11], totals[12], totals[13])
```

```python
import math

import jax
import jax.numpy as jnp
from jax import lax
from jax.experimental import pallas as pl
from jax.experimental.pallas import tpu as pltpu
from jax.sharding import PartitionSpec as P

HEAD_WIDTH = 256
ADAPTERS = 8


def rms_scale(value_rows, gain_row):
    inverse = lax.rsqrt(jnp.mean(value_rows * value_rows, axis=-1, keepdims=True) + 1e-06)
    return value_rows * inverse * gain_row


def rms_back(value_rows, gain_row, upstream):
    inverse = lax.rsqrt(jnp.mean(value_rows * value_rows, axis=-1, keepdims=True) + 1e-06)
    scaled = gain_row * upstream
    return inverse * scaled - value_rows * (inverse * inverse * inverse) * jnp.mean(
        value_rows * scaled, axis=-1, keepdims=True
    )


def pick_from(lookup, indices, labels):
    return jnp.sum(jnp.where(indices[:, None] == labels[None, :], lookup[None, :], 0), axis=1)


def tree_tables(segments, parents, order):
    count_seg = parents.shape[0]
    sequence_length = segments.shape[0]
    blocks = order.shape[0]
    labels = jnp.arange(count_seg, dtype=jnp.int32)
    ordered_places = jnp.arange(sequence_length, dtype=jnp.int32)
    member = segments[None, :] == labels[:, None]
    starts = jnp.min(jnp.where(member, ordered_places[None, :], sequence_length), axis=1)
    counts = jnp.sum(member.astype(jnp.int32), axis=1)
    grands = pick_from(parents, parents, labels)
    offsets = jnp.where(parents != labels, pick_from(counts, parents, labels), 0) + jnp.where(
        grands != parents, pick_from(counts, grands, labels), 0
    )
    block_rows = sequence_length // blocks
    chosen = order[:, None] == jnp.arange(blocks, dtype=jnp.int32)[None, :]
    segments = jnp.sum(
        jnp.where(chosen[:, :, None], segments.reshape(1, blocks, block_rows), 0), axis=1
    ).reshape(sequence_length)
    places = (
        order[:, None] * block_rows + jnp.arange(block_rows, dtype=jnp.int32)[None, :]
    ).reshape(sequence_length)
    tok_start = pick_from(starts, segments, labels)
    tok_offset = pick_from(offsets, segments, labels)
    tok_parent = pick_from(parents, segments, labels)
    tok_grand = pick_from(grands, segments, labels)
    positions = (places - tok_start + tok_offset).astype(jnp.float32)
    same_seg = (segments[None, :] == segments[:, None]) & (places[None, :] <= places[:, None])
    from_parent = (segments[None, :] == tok_parent[:, None]) & (tok_parent != segments)[:, None]
    from_grand = (segments[None, :] == tok_grand[:, None]) & (tok_grand != tok_parent)[:, None]
    visible = same_seg | from_parent | from_grand
    inv_freq = jnp.exp(
        jnp.arange(HEAD_WIDTH // 2, dtype=jnp.float32) * (-2.0 * math.log(10000.0) / HEAD_WIDTH)
    )
    angles = positions[:, None] * inv_freq[None, :]
    return (visible, jnp.cos(angles), jnp.sin(angles))


def apply_rotary(value_rows, cos_rows, sin_rows):
    half_size = value_rows.shape[-1] // 2
    front_half = value_rows[..., :half_size]
    back_half = value_rows[..., half_size:]
    return jnp.concatenate(
        [
            front_half * cos_rows - back_half * sin_rows,
            back_half * cos_rows + front_half * sin_rows,
        ],
        axis=-1,
    )


def rotate_back(value_rows, cos_rows, sin_rows):
    return apply_rotary(value_rows, cos_rows, -sin_rows)


def product(former, latter):
    return jnp.dot(former, latter, preferred_element_type=jnp.float32)


def times_rows(former, latter):
    return lax.dot_general(
        former, latter, (((1,), (1,)), ((), ())), preferred_element_type=jnp.float32
    )


def over_rows(former, latter):
    return lax.dot_general(
        former, latter, (((0,), (0,)), ((), ())), preferred_element_type=jnp.float32
    )


def low(values):
    return values.astype(jnp.bfloat16)


def select(onehot, stacked):
    return low(jnp.einsum("e,erc->rc", onehot, stacked, preferred_element_type=jnp.float32))


def score_block(query_rows, rotated_keys, visible):
    scores = jnp.einsum(
        "qngd,knd->ngqk", query_rows, rotated_keys, preferred_element_type=jnp.float32
    )
    bounded = jnp.tanh(scores / 50.0)
    masked = jnp.where(visible[None, None], 50.0 * bounded, -1e30)
    return (bounded, masked)


def activate(gate_in, up_in):
    return jax.nn.gelu(gate_in, approximate=True) * up_in


def flip(values, axis_name, bit):
    size = lax.axis_size(axis_name)
    return lax.ppermute(values, axis_name, [(i, i ^ bit) for i in range(size)])


def gather_blocks(pieces, columns_z):
    along_z, stacks, along_x = [], [], []
    for i, (mine, other) in enumerate(pieces):
        needs = []
        if i >= 1:
            needs += along_z[i - 1]
        if i >= 2:
            needs.append(along_x[i - 2])
        if needs:
            mine, other, *_ = lax.optimization_barrier((mine, other, *needs))
        got = [flip(other if k % 2 else mine, "dp", 2 * k) for k in range(1, columns_z)]
        along_z.append(got)
        stack = jnp.stack([mine] + got)
        stacks.append(stack)
        if i >= 1:
            stack, _ = lax.optimization_barrier((stack, along_x[i - 1]))
        along_x.append(flip(stack, "dp", 1))
    return stacks, along_x


def assemble(stacks, crossed, slots):
    columns_z, _, columns = stacks[0].shape
    rows = sum(stack.shape[1] for stack in stacks)
    count = len(stacks)

    def kernel(slots_ref, *refs):
        out_ref, sems = refs[2 * count], refs[2 * count + 1]
        copies = []
        for side in range(2):
            first = 0
            for i in range(count):
                source = refs[side * count + i]
                height = source.shape[1]
                for k in range(columns_z):
                    slot = slots_ref[side * columns_z + k]
                    copies.append(
                        pltpu.make_async_copy(
                            source.at[k],
                            out_ref.at[slot, pl.ds(first, height)],
                            sems.at[len(copies)],
                        )
                    )
                first += height
        for copy in copies:
            copy.start()
        for copy in copies:
            copy.wait()

    out = pl.pallas_call(
        kernel,
        out_shape=jax.ShapeDtypeStruct((2 * columns_z, rows, columns), stacks[0].dtype),
        in_specs=[pl.BlockSpec(memory_space=pltpu.SMEM)]
        + [pl.BlockSpec(memory_space=pl.ANY)] * (2 * count),
        out_specs=pl.BlockSpec(memory_space=pl.ANY),
        scratch_shapes=[pltpu.SemaphoreType.DMA((2 * count * columns_z,))],
        cost_estimate=pl.CostEstimate(
            flops=0,
            transcendentals=0,
            bytes_accessed=4 * 2 * columns_z * rows * columns,
        ),
    )(slots, *stacks, *crossed)
    return out.reshape(2 * columns_z * rows, columns)


def gather_pair(own):
    pair = jnp.concatenate([own, flip(own, "tensor", 2)])
    return jnp.concatenate([pair, flip(pair, "tensor", 1)])


def scatter_pair(part):
    rows = part.shape[0] // 4
    part = low(part)
    got = flip(part[2 * rows :], "tensor", 1).astype(jnp.float32)
    kept = part[: 2 * rows].astype(jnp.float32) + got
    last = flip(low(kept[rows:]), "tensor", 2)
    return kept[:rows] + last.astype(jnp.float32)


def gather_square(own):
    half = own.shape[0] // 2
    from_y = flip(own, "tensor", 2)
    from_z = flip(own, "dp", 2)
    three = jnp.concatenate([own, from_y, from_z])
    three_core = flip(three, "tensor", 1)
    diagonal = jnp.concatenate(
        [flip(from_y[:half], "dp", 2), flip(from_z[half:], "tensor", 2)]
    )
    diagonal_core = flip(diagonal, "tensor", 1)
    return jnp.concatenate([three, diagonal, three_core, diagonal_core])


def scatter_square(part):
    rows = part.shape[0] // 8
    half = rows // 2
    part = low(part)
    got = flip(part[4 * rows :], "tensor", 1).astype(jnp.float32)
    kept = part[: 4 * rows].astype(jnp.float32) + got
    kept_low = low(kept)
    mine, to_y, to_z, to_zy = (kept[i * rows : (i + 1) * rows] for i in range(4))
    low_y, low_z, low_zy = (kept_low[i * rows : (i + 1) * rows] for i in range(1, 4))
    got_y = flip(jnp.concatenate([low_y[:half], low_zy[:half]]), "tensor", 2)
    got_z = flip(jnp.concatenate([low_z[half:], low_zy[half:]]), "dp", 2)
    got_y, got_z = got_y.astype(jnp.float32), got_z.astype(jnp.float32)
    last_y = flip(low(to_y[half:] + got_z[half:]), "tensor", 2).astype(jnp.float32)
    last_z = flip(low(to_z[:half] + got_y[half:]), "dp", 2).astype(jnp.float32)
    return jnp.concatenate(
        [mine[:half] + got_y[:half] + last_z, mine[half:] + got_z[:half] + last_y]
    )


def on_device(
    layer_input,
    cotangent,
    norm_gains,
    w_query,
    w_key,
    w_value,
    w_output,
    w_gate,
    w_up,
    w_down,
    query_shrink,
    key_shrink,
    value_shrink,
    output_shrink,
    gate_shrink,
    up_shrink,
    down_shrink,
    query_expand,
    key_expand,
    value_expand,
    output_expand,
    gate_expand,
    up_expand,
    down_expand,
    adapter_ids,
    parent_segments,
    segment_ids,
):
    trees = lax.axis_size("dp")
    columns_z = trees // 2
    my_tree = lax.axis_index("dp")
    my_z, my_x = my_tree // 2, my_tree % 2
    my_part = lax.axis_index("tensor")
    odd = my_z % 2 == 1
    norm_gain = norm_gains.astype(jnp.float32)

    def my_half(values):
        half = values.shape[-1] // 2
        return jnp.where(odd, values[..., half:], values[..., :half])

    def other_half(values):
        half = values.shape[-1] // 2
        return jnp.where(odd, values[..., :half], values[..., half:])

    own_rows = layer_input.astype(jnp.float32)
    normed = low(rms_scale(own_rows, norm_gain[0]))
    normed_all = gather_pair(normed)

    w_qkv = jnp.concatenate([w_query, w_key, w_value], axis=1)
    w_out_t = w_output.T
    w_down_t = w_down.T
    depth = w_qkv.shape[0]
    cut = depth // 2 // 16 * 16
    pieces = [(w_qkv[:cut],) * 2, (w_qkv[cut:],) * 2, (w_out_t,) * 2]
    for matrix in (w_gate, w_up, w_down_t):
        mine, other = my_half(matrix), other_half(matrix)
        pieces += [(mine[:cut], other[:cut]), (mine[cut:], other[cut:])]
    stacks, crossed = gather_blocks(pieces, columns_z)
    slots = jnp.stack(
        [(my_z ^ k) * 2 + my_x for k in range(columns_z)]
        + [(my_z ^ k) * 2 + 1 - my_x for k in range(columns_z)]
    ).astype(jnp.int32)
    full_qkv = assemble(stacks[0:2], crossed[0:2], slots)
    full_out_t = assemble(stacks[2:3], crossed[2:3], slots)
    full_gate = assemble(stacks[3:5], crossed[3:5], slots)
    full_up = assemble(stacks[5:7], crossed[5:7], slots)
    full_down_t = assemble(stacks[7:9], crossed[7:9], slots)

    all_ids = lax.all_gather(adapter_ids, "dp", axis=0, tiled=True)
    labels = jnp.arange(ADAPTERS, dtype=jnp.int32)
    onehots = low(all_ids[:, None] == labels[None, :])
    onehot = low(labels == adapter_ids[0])
    near_id = jnp.sum(
        jnp.where(jnp.arange(trees, dtype=jnp.int32) == my_tree ^ 2, all_ids, 0)
    )
    onehot_near = low(labels == near_id)

    def both(stacked):
        return jnp.concatenate([select(onehot, stacked), select(onehot_near, stacked)])

    s_qkv = jnp.concatenate(
        [select(onehot, stacked) for stacked in (query_shrink, key_shrink, value_shrink)]
    )
    e_parts = [select(onehot, stacked) for stacked in (query_expand, key_expand, value_expand)]
    rank = e_parts[0].shape[0]
    widths = [part.shape[1] for part in e_parts]
    e_qkv = jnp.concatenate(
        [
            jnp.pad(part, ((0, 0), (sum(widths[:i]), sum(widths[i + 1 :]))))
            for i, part in enumerate(e_parts)
        ]
    )
    s_output, e_output = select(onehot, output_shrink), select(onehot, output_expand)
    s_gate_up = jnp.concatenate([both(gate_shrink), both(up_shrink)])
    e_gate, e_up = my_half(both(gate_expand)), my_half(both(up_expand))
    s_down, e_down = my_half(both(down_shrink)), both(down_expand)

    sequence_length = normed_all.shape[0]
    order = jnp.stack([my_part, my_part ^ 2, my_part ^ 1, my_part ^ 3]).astype(jnp.int32)
    visible, cos_rows, sin_rows = tree_tables(segment_ids, parent_segments[0], order)
    cosine_per_head = cos_rows[:, None, :]
    sine_per_head = sin_rows[:, None, :]
    inner_qkv = low(times_rows(normed_all, s_qkv))
    qkv_pre = product(normed_all, full_qkv) + product(inner_qkv, e_qkv)
    query_pre = qkv_pre[:, : widths[0]]
    key_before_rotation = qkv_pre[:, widths[0] : widths[0] + widths[1]]
    value_projected = qkv_pre[:, widths[0] + widths[1] :]
    heads_q = widths[0] // HEAD_WIDTH
    heads_kv = widths[1] // HEAD_WIDTH
    head_groups = heads_q // heads_kv
    query_rows = low(
        apply_rotary(
            query_pre.reshape(sequence_length, heads_q, HEAD_WIDTH),
            cosine_per_head,
            sine_per_head,
        )
        * HEAD_WIDTH ** (-0.5)
    ).reshape(sequence_length, heads_kv, head_groups, HEAD_WIDTH)
    rotated_keys = low(
        apply_rotary(
            key_before_rotation.reshape(sequence_length, heads_kv, HEAD_WIDTH),
            cosine_per_head,
            sine_per_head,
        )
    )
    value_rows = low(value_projected).reshape(sequence_length, heads_kv, HEAD_WIDTH)
    bounded, masked = score_block(query_rows, rotated_keys, visible)
    row_max = jnp.max(masked, axis=-1, keepdims=True)
    exponent = jnp.exp(masked - row_max)
    row_total = jnp.sum(exponent, axis=-1, keepdims=True)
    log_total = row_max + jnp.log(row_total)
    probs_low = low(exponent / row_total)
    mixed_heads = low(
        jnp.einsum(
            "ngqk,knd->qngd", probs_low, value_rows, preferred_element_type=jnp.float32
        ).reshape(sequence_length, heads_q * HEAD_WIDTH)
    )
    inner_output = low(times_rows(mixed_heads, s_output))
    attn_part = times_rows(mixed_heads, full_out_t) + product(inner_output, e_output)
    attended = scatter_pair(attn_part)
    residual = own_rows + rms_scale(attended, norm_gain[1])

    ffn_rows = gather_square(low(rms_scale(residual, norm_gain[2])))
    block_rows = residual.shape[0]
    row_block = jnp.arange(8 * block_rows, dtype=jnp.int32) // block_rows
    row_near = (row_block // 2 % 2)[:, None]
    rank_near = (jnp.arange(4 * rank, dtype=jnp.int32) // rank % 2)[None, :]
    keep_four = row_near == rank_near
    keep_two = keep_four[:, : 2 * rank]
    inner_gate_up = low(jnp.where(keep_four, times_rows(ffn_rows, s_gate_up), 0.0))
    inner_gate, inner_up = inner_gate_up[:, : 2 * rank], inner_gate_up[:, 2 * rank :]
    gate_pre = product(ffn_rows, full_gate) + product(inner_gate, e_gate)
    up_pre = product(ffn_rows, full_up) + product(inner_up, e_up)
    hidden_full, act_back = jax.vjp(activate, gate_pre, up_pre)
    hidden = low(hidden_full)
    inner_down = low(jnp.where(keep_two, times_rows(hidden, s_down), 0.0))
    ffn_part = times_rows(hidden, full_down_t) + product(inner_down, e_down)
    ffn_out = scatter_square(ffn_part)
    layer_output = low(residual + rms_scale(ffn_out, norm_gain[3]))

    grad_out = cotangent.astype(jnp.float32)
    grad_ffn = gather_square(low(rms_back(ffn_out, norm_gain[3], grad_out)))
    grad_inner_down = low(jnp.where(keep_two, times_rows(grad_ffn, e_down), 0.0))
    grad_hidden = product(grad_ffn, full_down_t) + product(grad_inner_down, s_down)
    grad_gate, grad_up = (low(grad) for grad in act_back(grad_hidden))
    grad_inner_gate = low(jnp.where(keep_two, times_rows(grad_gate, e_gate), 0.0))
    grad_inner_up = low(jnp.where(keep_two, times_rows(grad_up, e_up), 0.0))
    grad_inner_gate_up = jnp.concatenate([grad_inner_gate, grad_inner_up], axis=1)
    grad_normed_part = (
        times_rows(grad_gate, full_gate)
        + times_rows(grad_up, full_up)
        + product(grad_inner_gate_up, s_gate_up)
    )
    grad_normed_ffn = scatter_square(grad_normed_part)
    grad_expand_down = over_rows(inner_down, grad_ffn)
    grad_shrink_down = over_rows(grad_inner_down, hidden)
    grad_expand_gate = over_rows(inner_gate, grad_gate)
    grad_expand_up = over_rows(inner_up, grad_up)
    grad_shrink_gate_up = over_rows(grad_inner_gate_up, ffn_rows)

    grad_resid = grad_out + rms_back(residual, norm_gain[2], grad_normed_ffn)
    grad_attn = gather_pair(low(rms_back(attended, norm_gain[1], grad_resid)))

    grad_inner_output = low(times_rows(grad_attn, e_output))
    grad_mixed = low(
        product(grad_attn, full_out_t) + product(grad_inner_output, s_output)
    ).reshape(sequence_length, heads_kv, head_groups, HEAD_WIDTH)
    grad_expand_output = over_rows(inner_output, grad_attn)
    grad_shrink_output = over_rows(grad_inner_output, mixed_heads)
    bounded, masked = score_block(query_rows, rotated_keys, visible)
    attn_probs = jnp.exp(masked - log_total)
    probs_low = low(attn_probs)
    grad_values = low(
        jnp.einsum("ngqk,qngd->knd", probs_low, grad_mixed, preferred_element_type=jnp.float32)
    ).reshape(sequence_length, heads_kv * HEAD_WIDTH)
    grad_probs = jnp.einsum(
        "qngd,knd->ngqk", grad_mixed, value_rows, preferred_element_type=jnp.float32
    )
    grad_capped = attn_probs * (
        grad_probs - jnp.sum(attn_probs * grad_probs, axis=-1, keepdims=True)
    )
    grad_scores = low(grad_capped * (1.0 - bounded * bounded))
    grad_queries = jnp.einsum(
        "ngqk,knd->qngd", grad_scores, rotated_keys, preferred_element_type=jnp.float32
    ).reshape(sequence_length, heads_q, HEAD_WIDTH)
    grad_keys = jnp.einsum(
        "ngqk,qngd->knd", grad_scores, query_rows, preferred_element_type=jnp.float32
    )
    grad_qpre = low(
        rotate_back(grad_queries * HEAD_WIDTH ** (-0.5), cosine_per_head, sine_per_head)
    ).reshape(sequence_length, heads_q * HEAD_WIDTH)
    grad_kpre = low(rotate_back(grad_keys, cosine_per_head, sine_per_head)).reshape(
        sequence_length, heads_kv * HEAD_WIDTH
    )
    grad_qkv = jnp.concatenate([grad_qpre, grad_kpre, grad_values], axis=1)
    grad_inner_qkv = low(times_rows(grad_qkv, e_qkv))
    grad_normed = scatter_pair(
        times_rows(grad_qkv, full_qkv) + product(grad_inner_qkv, s_qkv)
    )
    grad_expand_qkv = over_rows(inner_qkv, grad_qkv)
    grad_shrink_qkv = over_rows(grad_inner_qkv, normed_all)
    input_grad = grad_resid + rms_back(own_rows, norm_gain[0], grad_normed)

    def by_adapter(hot, gathered):
        return lax.dot_general(
            hot, gathered, (((0,), (0,)), ((), ())), preferred_element_type=jnp.float32
        )

    local = low(
        jnp.concatenate([grad_expand_gate, grad_expand_up, grad_shrink_down], axis=1)
    )
    width = local.shape[1] // 3
    local_all = lax.all_gather(local, "dp", axis=0, tiled=False)
    local_all = local_all.reshape(columns_z // 2, 2, 2, 2, rank, 3 * width)
    hot_grid = onehots.reshape(columns_z // 2, 2, 2, ADAPTERS)
    sums = []
    for parity in range(2):
        hot = jnp.stack([hot_grid[:, parity], hot_grid[:, 1 - parity]], axis=2)
        sums.append(
            by_adapter(
                hot.reshape(2 * trees // 2, ADAPTERS),
                local_all[:, parity].reshape(2 * trees // 2, rank, 3 * width),
            )
        )
    out_expand_gate, out_expand_up, out_shrink_down = (
        jnp.concatenate([part[:, :, i * width : (i + 1) * width] for part in sums], axis=2)
        for i in range(3)
    )

    shared = low(
        jnp.concatenate([grad_shrink_gate_up, grad_expand_down]).reshape(3, 2, rank, -1)
    )
    shared = shared[:, 0].astype(jnp.float32) + flip(shared[:, 1], "dp", 2).astype(jnp.float32)
    shared = low(shared).reshape(3 * rank, -1)
    shared = lax.psum_scatter(shared, "tensor", scatter_dimension=0, tiled=True)
    shared_all = lax.all_gather(shared, ("dp", "tensor"), axis=0, tiled=True)
    shared_all = by_adapter(onehots, shared_all.reshape(trees, 3 * rank, -1))
    out_shrink_gate, out_shrink_up, out_expand_down = (
        shared_all[:, i * rank : (i + 1) * rank] for i in range(3)
    )

    starts = [sum(widths[:i]) for i in range(3)]
    local = low(
        jnp.concatenate(
            [
                grad_expand_qkv[i * rank : (i + 1) * rank, starts[i] : starts[i] + widths[i]]
                for i in range(3)
            ]
            + [grad_shrink_output],
            axis=1,
        )
    )
    local_all = by_adapter(onehots, lax.all_gather(local, "dp", axis=0, tiled=False))
    out_expand_query, out_expand_key, out_expand_value = (
        local_all[:, :, starts[i] : starts[i] + widths[i]] for i in range(3)
    )
    out_shrink_output = local_all[:, :, sum(widths) :]

    shared = low(jnp.concatenate([grad_shrink_qkv, grad_expand_output]))
    shared = lax.psum_scatter(shared, "tensor", scatter_dimension=0, tiled=True)
    shared_all = lax.all_gather(shared, ("dp", "tensor"), axis=0, tiled=True)
    shared_all = by_adapter(onehots, shared_all.reshape(trees, 4 * rank, -1))
    out_shrink_query, out_shrink_key, out_shrink_value, out_expand_output = (
        shared_all[:, i * rank : (i + 1) * rank] for i in range(4)
    )
    return (
        layer_output,
        input_grad,
        out_shrink_query,
        out_shrink_key,
        out_shrink_value,
        out_shrink_output,
        out_shrink_gate,
        out_shrink_up,
        out_shrink_down,
        out_expand_query,
        out_expand_key,
        out_expand_value,
        out_expand_output,
        out_expand_gate,
        out_expand_up,
        out_expand_down,
    )


def solution(mesh):
    placed = (
        P(("dp", "tensor"), None),
        P(("dp", "tensor"), None),
        P(),
        P("dp", "tensor"),
        P("dp", "tensor"),
        P("dp", "tensor"),
        P("tensor", "dp"),
        P("dp", "tensor"),
        P("dp", "tensor"),
        P("tensor", "dp"),
        P(),
        P(),
        P(),
        P(None, None, "tensor"),
        P(),
        P(),
        P(None, None, "tensor"),
        P(None, None, "tensor"),
        P(None, None, "tensor"),
        P(None, None, "tensor"),
        P(),
        P(None, None, "tensor"),
        P(None, None, "tensor"),
        P(),
        P("dp"),
        P("dp", None),
        P("dp"),
    )
    return jax.shard_map(
        on_device,
        mesh=mesh,
        in_specs=placed,
        out_specs=(
            P(("dp", "tensor"), None),
            P(("dp", "tensor"), None),
            P(),
            P(),
            P(),
            P(None, None, "tensor"),
            P(),
            P(),
            P(None, None, "tensor"),
            P(None, None, "tensor"),
            P(None, None, "tensor"),
            P(None, None, "tensor"),
            P(),
            P(None, None, "tensor"),
            P(None, None, "tensor"),
            P(),
        ),
        check_vma=False,
    )
```

```python
import functools
import math

import jax
import jax.numpy as jnp
from jax import lax
from jax.experimental import pallas as pl
from jax.experimental.pallas import tpu as pltpu
from jax.sharding import PartitionSpec as P

HEAD_WIDTH = 256
ADAPTERS = 8
TINY = pl.CostEstimate(flops=1, transcendentals=0, bytes_accessed=1)


def rms_scale(value_rows, gain_row):
    inverse = lax.rsqrt(jnp.mean(value_rows * value_rows, axis=-1, keepdims=True) + 1e-06)
    return value_rows * inverse * gain_row


def rms_back(value_rows, gain_row, upstream):
    inverse = lax.rsqrt(jnp.mean(value_rows * value_rows, axis=-1, keepdims=True) + 1e-06)
    scaled = gain_row * upstream
    return inverse * scaled - value_rows * (inverse * inverse * inverse) * jnp.mean(
        value_rows * scaled, axis=-1, keepdims=True
    )


def pick_from(lookup, indices, labels):
    return jnp.sum(jnp.where(indices[:, None] == labels[None, :], lookup[None, :], 0), axis=1)


def tree_tables(segments, parents, order):
    count_seg = parents.shape[0]
    sequence_length = segments.shape[0]
    blocks = order.shape[0]
    labels = jnp.arange(count_seg, dtype=jnp.int32)
    ordered_places = jnp.arange(sequence_length, dtype=jnp.int32)
    member = segments[None, :] == labels[:, None]
    starts = jnp.min(jnp.where(member, ordered_places[None, :], sequence_length), axis=1)
    counts = jnp.sum(member.astype(jnp.int32), axis=1)
    grands = pick_from(parents, parents, labels)
    offsets = jnp.where(parents != labels, pick_from(counts, parents, labels), 0) + jnp.where(
        grands != parents, pick_from(counts, grands, labels), 0
    )
    block_rows = sequence_length // blocks
    chosen = order[:, None] == jnp.arange(blocks, dtype=jnp.int32)[None, :]
    segments = jnp.sum(
        jnp.where(chosen[:, :, None], segments.reshape(1, blocks, block_rows), 0), axis=1
    ).reshape(sequence_length)
    places = (
        order[:, None] * block_rows + jnp.arange(block_rows, dtype=jnp.int32)[None, :]
    ).reshape(sequence_length)
    tok_start = pick_from(starts, segments, labels)
    tok_offset = pick_from(offsets, segments, labels)
    tok_parent = pick_from(parents, segments, labels)
    tok_grand = pick_from(grands, segments, labels)
    positions = (places - tok_start + tok_offset).astype(jnp.float32)
    same_seg = (segments[None, :] == segments[:, None]) & (places[None, :] <= places[:, None])
    from_parent = (segments[None, :] == tok_parent[:, None]) & (tok_parent != segments)[:, None]
    from_grand = (segments[None, :] == tok_grand[:, None]) & (tok_grand != tok_parent)[:, None]
    visible = same_seg | from_parent | from_grand
    inv_freq = jnp.exp(
        jnp.arange(HEAD_WIDTH // 2, dtype=jnp.float32) * (-2.0 * math.log(10000.0) / HEAD_WIDTH)
    )
    angles = positions[:, None] * inv_freq[None, :]
    return (visible, jnp.cos(angles), jnp.sin(angles))


def product(former, latter):
    return jnp.dot(former, latter, preferred_element_type=jnp.float32)


def times_rows(former, latter):
    return lax.dot_general(
        former, latter, (((1,), (1,)), ((), ())), preferred_element_type=jnp.float32
    )


def over_rows(former, latter):
    return lax.dot_general(
        former, latter, (((0,), (0,)), ((), ())), preferred_element_type=jnp.float32
    )


def low(values):
    return values.astype(jnp.bfloat16)


def flip(values, axis_name, bit):
    size = lax.axis_size(axis_name)
    return lax.ppermute(values, axis_name, [(i, i ^ bit) for i in range(size)])


def settle(*groups):
    flat, tree = jax.tree.flatten(groups)
    return jax.tree.unflatten(tree, lax.optimization_barrier(flat))


def along_z(blocks, columns_z):
    kinds = blocks.shape[0]
    lines = [[2 * z + x for z in range(columns_z)] for x in range(2)]
    sent = jnp.concatenate([blocks] * (columns_z // kinds))
    return lax.all_to_all(sent, "dp", 0, 0, axis_index_groups=lines)


def assemble(parts, place):
    columns_z, rows, columns = parts[0].shape

    def kernel(place_ref, mine_ref, cross_ref, core_ref, core_cross_ref, out_ref):
        my_x = place_ref[0]
        out_ref[my_x, :, :columns] = mine_ref[0]
        out_ref[my_x, :, columns:] = core_ref[0]
        out_ref[1 - my_x, :, :columns] = cross_ref[0]
        out_ref[1 - my_x, :, columns:] = core_cross_ref[0]

    out = pl.pallas_call(
        kernel,
        out_shape=jax.ShapeDtypeStruct((2 * columns_z, rows, 2 * columns), parts[0].dtype),
        grid_spec=pltpu.PrefetchScalarGridSpec(
            num_scalar_prefetch=1,
            grid=(columns_z,),
            in_specs=[pl.BlockSpec((1, rows, columns), lambda k, place_ref: (k, 0, 0))] * 4,
            out_specs=pl.BlockSpec((2, rows, 2 * columns), lambda k, place_ref: (k, 0, 0)),
        ),
        compiler_params=pltpu.CompilerParams(vmem_limit_bytes=32 << 20),
        cost_estimate=TINY,
    )(place, *parts)
    return out.reshape(2 * columns_z * rows, 2 * columns)


def beside(first, second):
    return jnp.concatenate([first, second], axis=1)


def pick_adapters(ids, whole, halved):
    rank = whole[0][0].shape[1]

    def kernel(ids_ref, *refs):
        count = len(refs) // 2
        for i in range(count):
            refs[count + i][...] = refs[i][0]

    in_specs, out_specs, shapes, stacks = [], [], [], []
    for entries, parity in ((whole, False), (halved, True)):
        for stack, near in entries:
            columns = stack.shape[2] // (2 if parity else 1)
            in_specs.append(
                pl.BlockSpec(
                    (1, rank, columns),
                    functools.partial(
                        lambda near, parity, i, ids_ref: (
                            ids_ref[1 if near else 0],
                            0,
                            ids_ref[2] if parity else 0,
                        ),
                        near,
                        parity,
                    ),
                )
            )
            out_specs.append(pl.BlockSpec((rank, columns), lambda i, ids_ref: (0, 0)))
            shapes.append(jax.ShapeDtypeStruct((rank, columns), stack.dtype))
            stacks.append(stack)
    return pl.pallas_call(
        kernel,
        out_shape=shapes,
        grid_spec=pltpu.PrefetchScalarGridSpec(
            num_scalar_prefetch=1, grid=(1,), in_specs=in_specs, out_specs=out_specs
        ),
        cost_estimate=TINY,
    )(ids, *stacks)


def fdot(former, latter, dims=((1,), (0,))):
    return lax.dot_general(former, latter, (dims, ((), ())), preferred_element_type=jnp.float32)


def turn(values, cosine, sine):
    half = values.shape[1] // 2
    front, back = values[:, :half], values[:, half:]
    return jnp.concatenate(
        [front * cosine - back * sine, back * cosine + front * sine], axis=1
    )


def project_heads(rows, weight, inner, expand, cosine, sine, queries):
    count, depth = rows.shape
    kinds = queries + 2

    def kernel(rows_ref, weight_ref, inner_ref, expand_ref, cosine_ref, sine_ref, out_ref):
        kind = pl.program_id(0) % kinds
        values = fdot(rows_ref[...], weight_ref[...]) + fdot(inner_ref[...], expand_ref[...])

        @pl.when(kind == kinds - 1)
        def _():
            out_ref[...] = low(values)

        @pl.when(kind < kinds - 1)
        def _():
            scale = jnp.where(kind < queries, HEAD_WIDTH ** (-0.5), 1.0)
            out_ref[...] = low(turn(values, cosine_ref[...], sine_ref[...]) * scale)

    whole = lambda array: pl.BlockSpec(array.shape, lambda j: (0, 0))
    return pl.pallas_call(
        kernel,
        out_shape=jax.ShapeDtypeStruct((count, weight.shape[1]), jnp.bfloat16),
        grid=(weight.shape[1] // HEAD_WIDTH,),
        in_specs=[
            whole(rows),
            pl.BlockSpec((depth, HEAD_WIDTH), lambda j: (0, j)),
            whole(inner),
            pl.BlockSpec((expand.shape[0], HEAD_WIDTH), lambda j: (0, j)),
            whole(cosine),
            whole(sine),
        ],
        out_specs=pl.BlockSpec((count, HEAD_WIDTH), lambda j: (0, j)),
        compiler_params=pltpu.CompilerParams(vmem_limit_bytes=40 << 20),
        cost_estimate=TINY,
    )(rows, weight, inner, expand, cosine, sine)


def soft_scores(query, keys, keep):
    bounded = jnp.tanh(fdot(query, keys, ((1,), (1,))) * (1.0 / 50.0))
    masked = jnp.where(keep, 50.0 * bounded, -1e30)
    exponent = jnp.exp(masked - jnp.max(masked, axis=1, keepdims=True))
    return bounded, exponent / jnp.sum(exponent, axis=1, keepdims=True)


def attend(projected, received, visible, queries):
    count = projected.shape[0]
    wide, pair = (queries + 2) * HEAD_WIDTH, 2 * HEAD_WIDTH

    def kernel(mine_ref, got_ref, visible_ref, out_ref):
        first = queries * HEAD_WIDTH
        mine = mine_ref[:, first:]
        got = got_ref[...]
        keys = jnp.concatenate([mine[:, :HEAD_WIDTH], got[:, :HEAD_WIDTH]])
        values = jnp.concatenate([mine[:, HEAD_WIDTH:], got[:, HEAD_WIDTH:]])
        keep = visible_ref[...] > 0
        for h in range(queries):
            columns = slice(h * HEAD_WIDTH, (h + 1) * HEAD_WIDTH)
            _, probs = soft_scores(mine_ref[:, columns], keys, keep)
            out_ref[:, columns] = low(fdot(low(probs), values))

    return pl.pallas_call(
        kernel,
        out_shape=jax.ShapeDtypeStruct((count, 2 * queries * HEAD_WIDTH), jnp.bfloat16),
        grid=(2,),
        in_specs=[
            pl.BlockSpec((count, wide), lambda j: (0, j)),
            pl.BlockSpec((count, pair), lambda j: (0, j)),
            pl.BlockSpec(visible.shape, lambda j: (0, 0)),
        ],
        out_specs=pl.BlockSpec((count, queries * HEAD_WIDTH), lambda j: (0, j)),
        compiler_params=pltpu.CompilerParams(vmem_limit_bytes=40 << 20),
        cost_estimate=TINY,
    )(projected, received, visible)


def attend_back(projected, received, visible, grad_mixed, cosine, sine, queries):
    count = projected.shape[0]
    wide, pair = (queries + 2) * HEAD_WIDTH, 2 * HEAD_WIDTH

    def kernel(mine_ref, got_ref, visible_ref, grad_ref, cos_ref, sin_ref, query_ref, pair_ref):
        first = queries * HEAD_WIDTH
        mine = mine_ref[:, first:]
        got = got_ref[...]
        keys = jnp.concatenate([mine[:, :HEAD_WIDTH], got[:, :HEAD_WIDTH]])
        values = jnp.concatenate([mine[:, HEAD_WIDTH:], got[:, HEAD_WIDTH:]])
        keep = visible_ref[...] > 0
        grad_keys, grad_values = 0.0, 0.0
        for h in range(queries):
            columns = slice(h * HEAD_WIDTH, (h + 1) * HEAD_WIDTH)
            query, grad = mine_ref[:, columns], grad_ref[:, columns]
            bounded, probs = soft_scores(query, keys, keep)
            grad_values = grad_values + fdot(low(probs), grad, ((0,), (0,)))
            grad_probs = fdot(grad, values, ((1,), (1,)))
            inner = jnp.sum(probs * grad_probs, axis=1, keepdims=True)
            grad_scores = low(probs * (grad_probs - inner) * (1.0 - bounded * bounded))
            grad_query = fdot(grad_scores, keys) * HEAD_WIDTH ** (-0.5)
            query_ref[:, columns] = low(turn(grad_query, cos_ref[...], -sin_ref[...]))
            grad_keys = grad_keys + fdot(grad_scores, query, ((0,), (0,)))
        pair_ref[:, :HEAD_WIDTH] = grad_keys
        pair_ref[:, HEAD_WIDTH:] = grad_values

    whole = lambda array: pl.BlockSpec(array.shape, lambda j: (0, 0))
    return pl.pallas_call(
        kernel,
        out_shape=[
            jax.ShapeDtypeStruct((count, 2 * queries * HEAD_WIDTH), jnp.bfloat16),
            jax.ShapeDtypeStruct((2 * count, 2 * pair), jnp.float32),
        ],
        grid=(2,),
        in_specs=[
            pl.BlockSpec((count, wide), lambda j: (0, j)),
            pl.BlockSpec((count, pair), lambda j: (0, j)),
            whole(visible),
            pl.BlockSpec((count, queries * HEAD_WIDTH), lambda j: (0, j)),
            whole(cosine),
            whole(sine),
        ],
        out_specs=[
            pl.BlockSpec((count, queries * HEAD_WIDTH), lambda j: (0, j)),
            pl.BlockSpec((2 * count, pair), lambda j: (0, j)),
        ],
        compiler_params=pltpu.CompilerParams(vmem_limit_bytes=48 << 20),
        cost_estimate=TINY,
    )(projected, received, visible, grad_mixed, cosine, sine)


GELU_A = math.sqrt(2.0 / math.pi)
GELU_B = 0.044715


def gate_and_up(rows, w_gate, w_up, inner, e_gate, e_up):
    count, depth = rows.shape
    units, tile = w_gate.shape[1], 256
    half = inner.shape[1] // 2

    def kernel(rows_ref, gate_w, up_w, inner_ref, gate_e, up_e, gate_ref, up_ref, hidden_ref):
        inner_rows = inner_ref[...]
        gate = fdot(rows_ref[...], gate_w[...]) + fdot(inner_rows[:, :half], gate_e[...])
        up = fdot(rows_ref[...], up_w[...]) + fdot(inner_rows[:, half:], up_e[...])
        bend = jnp.tanh(GELU_A * (gate + GELU_B * (gate * gate * gate)))
        gate_ref[...] = gate
        up_ref[...] = up
        hidden_ref[...] = low(0.5 * gate * (1.0 + bend) * up)

    whole = lambda array: pl.BlockSpec(array.shape, lambda j: (0, 0))
    column = lambda array: pl.BlockSpec((array.shape[0], tile), lambda j: (0, j))
    result = lambda dtype: jax.ShapeDtypeStruct((count, units), dtype)
    return pl.pallas_call(
        kernel,
        out_shape=[result(jnp.float32), result(jnp.float32), result(jnp.bfloat16)],
        grid=(units // tile,),
        in_specs=[whole(rows), column(w_gate), column(w_up), whole(inner), column(e_gate),
                  column(e_up)],
        out_specs=[pl.BlockSpec((count, tile), lambda j: (0, j))] * 3,
        compiler_params=pltpu.CompilerParams(vmem_limit_bytes=48 << 20),
        cost_estimate=TINY,
    )(rows, w_gate, w_up, inner, e_gate, e_up)


def feed_forward_back(grad_rows, grad_inner, inner_t, grad_inner_t, s_gate_up, keep, chunks):
    count, depth = grad_rows.shape
    tile = 256
    tiles = [chunk[0].shape[1] // tile for chunk in chunks]
    firsts = [sum(tiles[:i]) for i in range(len(tiles))]
    total = sum(tiles)
    twice = grad_inner.shape[1]
    each = len(chunks[0])

    def kernel(grad_ref, inner_grad_ref, inner_t_ref, inner_grad_t_ref, s_ref, keep_ref, *refs):
        ins, (rows_ref, inner_ref, units_ref, total_ref, sums_ref) = refs[:-5], refs[-5:]
        step = pl.program_id(0)

        @pl.when(step == 0)
        def _():
            total_ref[...] = jnp.zeros_like(total_ref)
            sums_ref[...] = jnp.zeros_like(sums_ref)

        def one(down, gate_w, up_w, gate_in, up_in, hidden, s_down, e_gate, e_up):
            grad = fdot(grad_ref[...], down[...]) + fdot(inner_grad_ref[...], s_down[...])
            gate, up = gate_in[...], up_in[...]
            square = gate * gate
            bend = jnp.tanh(GELU_A * gate * (1.0 + GELU_B * square))
            half_up = 0.5 * (1.0 + bend)
            slope = half_up + 0.5 * gate * (1.0 - bend * bend) * (
                GELU_A * (1.0 + 3.0 * GELU_B * square)
            )
            grad_gate = low(grad * up * slope)
            grad_up = low(grad * (gate * half_up))
            total_ref[...] += fdot(grad_gate, gate_w[...], ((1,), (1,))) + fdot(
                grad_up, up_w[...], ((1,), (1,))
            )
            sums_ref[:, :twice] += fdot(grad_gate, e_gate[...], ((1,), (1,)))
            sums_ref[:, twice:] += fdot(grad_up, e_up[...], ((1,), (1,)))
            units_ref[:twice] = fdot(inner_t_ref[:twice], grad_gate)
            units_ref[twice : 2 * twice] = fdot(inner_t_ref[twice:], grad_up)
            units_ref[2 * twice :] = fdot(inner_grad_t_ref[...], hidden[...])

        for i in range(len(chunks)):
            within = (step >= firsts[i]) & (step < firsts[i] + tiles[i])
            pl.when(within)(functools.partial(one, *ins[i * each : (i + 1) * each]))

        @pl.when(step == total - 1)
        def _():
            kept = low(sums_ref[...] * keep_ref[...])
            inner_ref[...] = kept
            rows_ref[...] = low(total_ref[...] + fdot(kept, s_ref[...]))

    whole = lambda array: pl.BlockSpec(array.shape, lambda j: (0, 0))

    def column(i, array):
        return pl.BlockSpec(
            (array.shape[0], tile),
            lambda j: (0, jnp.clip(j - firsts[i], 0, tiles[i] - 1)),
        )

    fixed = [grad_rows, grad_inner, inner_t, grad_inner_t, s_gate_up, keep]
    return pl.pallas_call(
        kernel,
        out_shape=[
            jax.ShapeDtypeStruct((count, depth), jnp.bfloat16),
            jax.ShapeDtypeStruct((count, 2 * twice), jnp.bfloat16),
            jax.ShapeDtypeStruct((3 * twice, total * tile), jnp.float32),
        ],
        grid=(total,),
        in_specs=[whole(array) for array in fixed]
        + [column(i, array) for i, chunk in enumerate(chunks) for array in chunk],
        out_specs=[
            pl.BlockSpec((count, depth), lambda j: (0, 0)),
            pl.BlockSpec((count, 2 * twice), lambda j: (0, 0)),
            pl.BlockSpec((3 * twice, tile), lambda j: (0, j)),
        ],
        scratch_shapes=[
            pltpu.VMEM((count, depth), jnp.float32),
            pltpu.VMEM((count, 2 * twice), jnp.float32),
        ],
        compiler_params=pltpu.CompilerParams(vmem_limit_bytes=60 << 20),
        cost_estimate=TINY,
    )(*fixed, *[array for chunk in chunks for array in chunk])


def scatter_pair(part):
    rows = part.shape[0] // 2
    got = flip(low(part[rows:]), "tensor", 2)
    return part[:rows] + got.astype(jnp.float32)


def gather_pair(own):
    return jnp.concatenate([own, flip(own, "tensor", 2)])


def gather_square(own):
    half = own.shape[0] // 2
    from_y = flip(own, "tensor", 2)
    from_z = flip(own, "dp", 2)
    diagonal = [flip(from_y[:half], "dp", 2), flip(from_z[half:], "tensor", 2)]
    return jnp.concatenate([own, from_y, from_z] + diagonal)


def scatter_square(part):
    rows = part.shape[0] // 4
    half = rows // 2
    mine, to_y, to_z, to_zy = (part[i * rows : (i + 1) * rows] for i in range(4))
    got_y = flip(low(jnp.concatenate([to_y[:half], to_zy[:half]])), "tensor", 2)
    got_z = flip(low(jnp.concatenate([to_z[half:], to_zy[half:]])), "dp", 2)
    got_y, got_z = got_y.astype(jnp.float32), got_z.astype(jnp.float32)
    last_y = flip(low(to_y[half:] + got_z[half:]), "tensor", 2).astype(jnp.float32)
    last_z = flip(low(to_z[:half] + got_y[half:]), "dp", 2).astype(jnp.float32)
    return jnp.concatenate(
        [mine[:half] + got_y[:half] + last_z, mine[half:] + got_z[:half] + last_y]
    )


def gather_trees(values, trees):
    values = values[None]
    bits = [1 << b for b in range(1, trees.bit_length() - 1)][::-1] + [1]
    for bit in bits:
        values = jnp.concatenate([values, flip(values, "dp", bit)])
    index = [0]
    for bit in bits:
        index += [i ^ bit for i in index]
    return values, index


def on_device(
    layer_input,
    cotangent,
    norm_gains,
    w_query,
    w_key,
    w_value,
    w_output,
    w_gate,
    w_up,
    w_down,
    query_shrink,
    key_shrink,
    value_shrink,
    output_shrink,
    gate_shrink,
    up_shrink,
    down_shrink,
    query_expand,
    key_expand,
    value_expand,
    output_expand,
    gate_expand,
    up_expand,
    down_expand,
    adapter_ids,
    parent_segments,
    segment_ids,
):
    trees = lax.axis_size("dp")
    columns_z = trees // 2
    my_tree = lax.axis_index("dp")
    my_z, my_x = my_tree // 2, my_tree % 2
    my_part = lax.axis_index("tensor")
    odd = my_z % 2 == 1
    norm_gain = norm_gains.astype(jnp.float32)
    place = my_x.astype(jnp.int32)[None]

    def halves(values):
        half = values.shape[-1] // 2
        return jnp.stack([values[:, :half], values[:, half:]])

    def on_core(values):
        return flip(values, "tensor", 1)

    w_qkv = jnp.concatenate([w_query, w_key, w_value], axis=1)
    cut = w_qkv.shape[0] // 2 // 16 * 16
    gate_halves, up_halves, down_halves = halves(w_gate), halves(w_up), halves(w_down.T)
    units = gate_halves.shape[2]
    first_units = (units // 128 + 1) // 2 * 128
    waiting = [
        w_qkv[None, :cut],
        w_qkv[None, cut:],
        w_output.T[None],
        gate_halves[:, :, first_units:],
        up_halves[:, :, first_units:],
        gate_halves[:, :, :first_units],
        up_halves[:, :, :first_units],
        down_halves[:, :, :first_units],
        down_halves[:, :, first_units:],
    ]
    count = len(waiting)
    near, cross = {}, {}

    near_core, cross_core = {}, {}

    def transfers(step):
        if step < count:
            near[step] = along_z(waiting[step], columns_z)
        if 0 <= step - 1 < count:
            cross[step - 1] = flip(near[step - 1], "dp", 1)
            near_core[step - 1] = on_core(near[step - 1])
        if 0 <= step - 2 < count:
            cross_core[step - 2] = on_core(cross[step - 2])

    def close(step, *values):
        moved = [
            (store, key)
            for store, key in (
                (near, step),
                (cross, step - 1),
                (near_core, step - 1),
                (cross_core, step - 2),
            )
            if key in store
        ]
        following = [waiting[step + 1]] if step + 1 < count else []
        moved_values, following, values = settle(
            [store[key] for store, key in moved], following, values
        )
        for (store, key), value in zip(moved, moved_values):
            store[key] = value
        if following:
            waiting[step + 1] = following[0]
        return values

    def matrix(*keys):
        parts = [
            jnp.concatenate([store[key] for key in keys], axis=1) if len(keys) > 1 else store[keys[0]]
            for store in (near, cross, near_core, cross_core)
        ]
        return assemble(parts, place)

    transfers(0)
    own_rows = layer_input.astype(jnp.float32)
    normed = low(rms_scale(own_rows, norm_gain[0]))
    normed_all = gather_pair(normed)
    near_ids = flip(adapter_ids, "dp", 2)
    labels = jnp.arange(ADAPTERS, dtype=jnp.int32)
    order = jnp.stack([my_part, my_part ^ 2, my_part ^ 1, my_part ^ 3]).astype(jnp.int32)
    visible, cos_rows, sin_rows = tree_tables(segment_ids, parent_segments[0], order)
    row_count = normed_all.shape[0]
    visible = low(visible[:row_count])
    cos_rows, sin_rows = cos_rows[:row_count], sin_rows[:row_count]
    normed_all, near_ids, visible, cos_rows, sin_rows = close(
        0, normed_all, near_ids, visible, cos_rows, sin_rows
    )

    transfers(1)
    picked = pick_adapters(
        jnp.concatenate([adapter_ids, near_ids, (my_z % 2).astype(jnp.int32)[None]]),
        [
            (stack, False)
            for stack in (
                query_shrink,
                key_shrink,
                value_shrink,
                query_expand,
                key_expand,
                value_expand,
                output_shrink,
                output_expand,
            )
        ]
        + [
            (stack, near_tree)
            for stack in (gate_shrink, up_shrink, down_expand)
            for near_tree in (False, True)
        ],
        [
            (stack, near_tree)
            for stack in (gate_expand, up_expand, down_shrink)
            for near_tree in (False, True)
        ],
    )
    s_qkv = jnp.concatenate(picked[0:3])
    e_parts = picked[3:6]
    rank = e_parts[0].shape[0]
    widths = [part.shape[1] for part in e_parts]
    attn_mine = jnp.concatenate(picked[3:7], axis=1)
    e_output = picked[7]
    s_gate_up = jnp.concatenate(picked[8:12])
    e_down = jnp.concatenate(picked[12:14])
    ffn_mine = jnp.concatenate(picked[14:20])
    inner_qkv = low(times_rows(normed_all, s_qkv))
    attn_mine, e_output, s_gate_up, e_down, ffn_mine, s_qkv, inner_qkv = close(
        1, attn_mine, e_output, s_gate_up, e_down, ffn_mine, s_qkv, inner_qkv
    )

    transfers(2)
    attn_other = on_core(attn_mine)
    ffn_other = on_core(ffn_mine)
    attn_other, ffn_other = close(2, attn_other, ffn_other)

    transfers(3)
    heads_here = sum(widths)
    queries = widths[0] // HEAD_WIDTH
    e_mine = attn_mine[:, :heads_here]
    e_other = attn_other[:, :heads_here]
    s_output = beside(attn_mine[:, heads_here:], attn_other[:, heads_here:])
    starts = [sum(widths[:i]) for i in range(4)]
    column_kind = sum(
        (jnp.arange(heads_here, dtype=jnp.int32) >= start).astype(jnp.int32)
        for start in starts[1:3]
    )
    kind_mask = (
        jnp.arange(3 * rank, dtype=jnp.int32)[:, None] // rank
        == jnp.concatenate([column_kind, column_kind])[None, :]
    )
    e_qkv = low(jnp.where(kind_mask, jnp.tile(beside(e_mine, e_other), (3, 1)), 0.0))
    tree_ids, tree_index = gather_trees(adapter_ids, trees)
    units_a = beside(ffn_mine[:, :first_units], ffn_other[:, :first_units])
    units_b = beside(ffn_mine[:, first_units:], ffn_other[:, first_units:])
    adapters_ab = [
        [block[i * 2 * rank : (i + 1) * 2 * rank] for i in range(3)] for block in (units_a, units_b)
    ]
    tree_ids, e_qkv, s_output, adapters_ab = close(3, tree_ids, e_qkv, s_output, adapters_ab)

    transfers(4)
    full_qkv = matrix(0, 1)
    projected = project_heads(
        normed_all, full_qkv, inner_qkv, e_qkv, cos_rows, sin_rows, queries
    )
    received = on_core(
        beside(projected[:, heads_here + starts[1] :], projected[:, starts[1] : heads_here])
    )
    full_qkv, projected, received = close(4, full_qkv, projected, received)

    transfers(5)
    full_out_t = matrix(2)
    mixed_heads = attend(projected, received, visible, queries)
    inner_output = low(times_rows(mixed_heads, s_output))
    attn_part = times_rows(mixed_heads, full_out_t) + product(inner_output, e_output)
    mixed_heads, full_out_t, inner_output, attn_part = close(
        5, mixed_heads, full_out_t, inner_output, attn_part
    )

    transfers(6)
    attended = scatter_pair(attn_part)
    full_gate_b = matrix(3)
    residual = own_rows + rms_scale(attended, norm_gain[1])
    normed_ffn = low(rms_scale(residual, norm_gain[2]))
    residual, attended, normed_ffn, full_gate_b = close(
        6, residual, attended, normed_ffn, full_gate_b
    )

    transfers(7)
    normed_y = flip(normed_ffn, "tensor", 2)
    full_up_b = matrix(4)
    normed_y, full_up_b = close(7, normed_y, full_up_b)

    transfers(8)
    normed_z = flip(normed_ffn, "dp", 2)
    full_gate_a = matrix(5)
    normed_z, full_gate_a = close(8, normed_z, full_gate_a)

    transfers(9)
    normed_zy = flip(normed_z, "tensor", 2)
    full_up_a = matrix(6)
    ffn_rows = jnp.concatenate([normed_ffn, normed_y, normed_z, normed_zy])
    block_rows = residual.shape[0]
    row_block = jnp.arange(4 * block_rows, dtype=jnp.int32) // block_rows
    row_near = (row_block // 2)[:, None]
    rank_near = (jnp.arange(4 * rank, dtype=jnp.int32) // rank % 2)[None, :]
    keep_four = (row_near == rank_near).astype(jnp.float32)
    keep_two = keep_four[:, : 2 * rank]
    inner_gate_up = low(keep_four * times_rows(ffn_rows, s_gate_up))
    chunk_out = [
        gate_and_up(ffn_rows, full_gate, full_up, inner_gate_up, e_gate, e_up)
        for full_gate, full_up, (e_gate, e_up, _) in (
            (full_gate_a, full_up_a, adapters_ab[0]),
            (full_gate_b, full_up_b, adapters_ab[1]),
        )
    ]
    chunk_out, full_gate_a, full_up_a, full_gate_b, full_up_b = close(
        9, chunk_out, full_gate_a, full_up_a, full_gate_b, full_up_b
    )

    cross_core[8] = on_core(cross[8])
    full_down_a = matrix(7)
    hidden = [parts[2] for parts in chunk_out]
    inner_down = low(
        keep_two
        * (times_rows(hidden[0], adapters_ab[0][2]) + times_rows(hidden[1], adapters_ab[1][2]))
    )
    ffn_first = times_rows(hidden[0], full_down_a) + product(inner_down, e_down)
    full_down_b = matrix(8)
    ffn_part = ffn_first + times_rows(hidden[1], full_down_b)
    ffn_out = scatter_square(ffn_part)
    layer_output = low(residual + rms_scale(ffn_out, norm_gain[3]))

    grad_out = cotangent.astype(jnp.float32)
    grad_ffn = gather_square(low(rms_back(ffn_out, norm_gain[3], grad_out)))
    grad_inner_down = low(keep_two * times_rows(grad_ffn, e_down))
    grad_normed_part, grad_inner_gate_up, grad_units = feed_forward_back(
        grad_ffn,
        grad_inner_down,
        inner_gate_up.T,
        grad_inner_down.T,
        s_gate_up,
        keep_four,
        [
            (full_down, full_gate, full_up, *parts, adapters[2], adapters[0], adapters[1])
            for full_down, full_gate, full_up, parts, adapters in (
                (full_down_a, full_gate_a, full_up_a, chunk_out[0], adapters_ab[0]),
                (full_down_b, full_gate_b, full_up_b, chunk_out[1], adapters_ab[1]),
            )
        ],
    )
    grad_normed_ffn = scatter_square(grad_normed_part)
    grad_expand_down = over_rows(inner_down, grad_ffn)
    grad_shrink_gate_up = over_rows(grad_inner_gate_up, ffn_rows)

    grad_resid = grad_out + rms_back(residual, norm_gain[2], grad_normed_ffn)
    grad_attn = gather_pair(low(rms_back(attended, norm_gain[1], grad_resid)))

    grad_inner_output = low(times_rows(grad_attn, e_output))
    grad_mixed = low(
        product(grad_attn, full_out_t) + product(grad_inner_output, s_output)
    )
    grad_expand_output = over_rows(inner_output, grad_attn)
    grad_shrink_output = over_rows(grad_inner_output, mixed_heads)
    grad_queries, grad_pairs = attend_back(
        projected, received, visible, grad_mixed, cos_rows, sin_rows, queries
    )
    pair = 2 * HEAD_WIDTH
    to_core = low(beside(grad_pairs[row_count:, pair:], grad_pairs[row_count:, :pair]))
    grad_pairs = grad_pairs[:row_count] + on_core(to_core).astype(jnp.float32)
    grad_sides = []
    for side in range(2):
        keys_values = grad_pairs[:, side * pair : (side + 1) * pair]
        grad_sides += [
            grad_queries[:, side * widths[0] : (side + 1) * widths[0]],
            low(turn(keys_values[:, :HEAD_WIDTH], cos_rows, -sin_rows)),
            low(keys_values[:, HEAD_WIDTH:]),
        ]
    grad_qkv = jnp.concatenate(grad_sides, axis=1)
    grad_inner_qkv = low(times_rows(grad_qkv, e_qkv))
    grad_expand_qkv = over_rows(inner_qkv, grad_qkv)
    grad_shrink_qkv = over_rows(grad_inner_qkv, normed_all)
    grad_normed = scatter_pair(
        times_rows(grad_qkv, full_qkv) + product(grad_inner_qkv, s_qkv)
    )
    input_grad = grad_resid + rms_back(own_rows, norm_gain[0], grad_normed)

    tree_ids = tree_ids.reshape(trees)
    hot_near = low(tree_ids[:, None] == labels[None, :])

    def by_adapter(hot, gathered):
        return lax.dot_general(
            hot, gathered, (((0,), (0,)), ((), ())), preferred_element_type=jnp.float32
        )

    def from_other_core(mine, other):
        return low(mine + on_core(low(other)).astype(jnp.float32))

    rest = units - first_units
    cuts = [0, first_units, 2 * first_units, 2 * first_units + rest, 2 * units]
    quarters = [grad_units[:, cuts[i] : cuts[i + 1]] for i in range(4)]
    mine, other = beside(quarters[0], quarters[2]), beside(quarters[1], quarters[3])
    local = from_other_core(mine, other)
    local_all, _ = gather_trees(local, trees)
    local_all = local_all.reshape(trees, 3, 2, rank, units)
    same, crossed, same_hot, crossed_hot = [], [], [], []
    where_is = {tree: i for i, tree in enumerate(tree_index)}
    for j in range(trees):
        for near in range(2):
            target = (crossed if (j // 2) % 2 else same)
            hots = (crossed_hot if (j // 2) % 2 else same_hot)
            target.append(local_all[where_is[j], :, near])
            hots.append(hot_near[where_is[j ^ (2 * near)]])
    mine_sum = by_adapter(jnp.stack(same_hot), jnp.stack(same))
    other_sum = by_adapter(jnp.stack(crossed_hot), jnp.stack(crossed))
    low_half = jnp.where(odd, other_sum, mine_sum)
    high_half = jnp.where(odd, mine_sum, other_sum)
    both_halves = jnp.concatenate([low_half, high_half], axis=-1)
    out_expand_gate, out_expand_up, out_shrink_down = (both_halves[:, i] for i in range(3))

    def share(blocks):
        blocks = low(blocks)
        swapped = jnp.where(my_part % 2 == 1, blocks.reshape(2, 2, rank, -1)[:, ::-1], blocks.reshape(2, 2, rank, -1))
        swapped = jnp.where(my_part // 2 == 1, swapped[::-1], swapped)
        kept = swapped[:, 0].astype(jnp.float32) + on_core(swapped[:, 1]).astype(jnp.float32)
        kept = kept[0] + flip(low(kept[1]), "tensor", 2).astype(jnp.float32)
        gathered, _ = gather_trees(low(kept), trees)
        total = low(by_adapter(hot_near, gathered))[None]
        total = jnp.concatenate([total, flip(total, "tensor", 2)])
        total = jnp.stack([total, on_core(total)], axis=1)
        total = jnp.where(my_part // 2 == 1, total[::-1], total)
        total = jnp.where(my_part % 2 == 1, total[:, ::-1], total)
        return total.reshape((4,) + total.shape[2:]).astype(jnp.float32)

    shared = jnp.concatenate([grad_shrink_gate_up, grad_expand_down]).reshape(3, 2, rank, -1)
    shared = shared[:, 0] + flip(low(shared[:, 1]), "dp", 2).astype(jnp.float32)
    shared = share(jnp.concatenate([shared, grad_expand_output[None]]))
    out_shrink_gate, out_shrink_up, out_expand_down, out_expand_output = (
        shared[i] for i in range(4)
    )

    pieces = []
    for side in range(2):
        for i in range(3):
            first = side * heads_here + starts[i]
            pieces.append(grad_expand_qkv[i * rank : (i + 1) * rank, first : first + widths[i]])
        pieces.append(grad_shrink_output[:, side * widths[0] : (side + 1) * widths[0]])
    local = from_other_core(
        jnp.concatenate(pieces[:4], axis=1), jnp.concatenate(pieces[4:], axis=1)
    )
    local_all, _ = gather_trees(local, trees)
    local_all = by_adapter(hot_near, local_all)
    out_expand_query, out_expand_key, out_expand_value = (
        local_all[:, :, starts[i] : starts[i] + widths[i]] for i in range(3)
    )
    out_shrink_output = local_all[:, :, heads_here:]

    shared = grad_shrink_qkv.reshape(3, rank, -1)
    shared = share(jnp.concatenate([shared, jnp.zeros_like(shared[:1])]))
    out_shrink_query, out_shrink_key, out_shrink_value = (shared[i] for i in range(3))
    return (
        layer_output,
        input_grad,
        out_shrink_query,
        out_shrink_key,
        out_shrink_value,
        out_shrink_output,
        out_shrink_gate,
        out_shrink_up,
        out_shrink_down,
        out_expand_query,
        out_expand_key,
        out_expand_value,
        out_expand_output,
        out_expand_gate,
        out_expand_up,
        out_expand_down,
    )


def solution(mesh):
    placed = (
        P(("dp", "tensor"), None),
        P(("dp", "tensor"), None),
        P(),
        P("dp", "tensor"),
        P("dp", "tensor"),
        P("dp", "tensor"),
        P("tensor", "dp"),
        P("dp", "tensor"),
        P("dp", "tensor"),
        P("tensor", "dp"),
        P(),
        P(),
        P(),
        P(None, None, "tensor"),
        P(),
        P(),
        P(None, None, "tensor"),
        P(None, None, "tensor"),
        P(None, None, "tensor"),
        P(None, None, "tensor"),
        P(),
        P(None, None, "tensor"),
        P(None, None, "tensor"),
        P(),
        P("dp"),
        P("dp", None),
        P("dp"),
    )
    return jax.shard_map(
        on_device,
        mesh=mesh,
        in_specs=placed,
        out_specs=(
            P(("dp", "tensor"), None),
            P(("dp", "tensor"), None),
            P(),
            P(),
            P(),
            P(None, None, "tensor"),
            P(),
            P(),
            P(None, None, "tensor"),
            P(None, None, "tensor"),
            P(None, None, "tensor"),
            P(None, None, "tensor"),
            P(),
            P(None, None, "tensor"),
            P(None, None, "tensor"),
            P(),
        ),
        check_vma=False,
    )
```

```python
import functools
import math

import jax
import jax.numpy as jnp
from jax import lax
from jax.experimental import pallas as pl
from jax.experimental.pallas import tpu as pltpu
from jax.sharding import PartitionSpec as P

HEAD_WIDTH = 256
ADAPTERS = 8
TINY = pl.CostEstimate(flops=1, transcendentals=0, bytes_accessed=1)


def rms_scale(value_rows, gain_row):
    inverse = lax.rsqrt(jnp.mean(value_rows * value_rows, axis=-1, keepdims=True) + 1e-06)
    return value_rows * inverse * gain_row


def rms_back(value_rows, gain_row, upstream):
    inverse = lax.rsqrt(jnp.mean(value_rows * value_rows, axis=-1, keepdims=True) + 1e-06)
    scaled = gain_row * upstream
    return inverse * scaled - value_rows * (inverse * inverse * inverse) * jnp.mean(
        value_rows * scaled, axis=-1, keepdims=True
    )


def pick_from(lookup, indices, labels):
    return jnp.sum(jnp.where(indices[:, None] == labels[None, :], lookup[None, :], 0), axis=1)


def tree_tables(segments, parents, order):
    count_seg = parents.shape[0]
    sequence_length = segments.shape[0]
    blocks = order.shape[0]
    labels = jnp.arange(count_seg, dtype=jnp.int32)
    ordered_places = jnp.arange(sequence_length, dtype=jnp.int32)
    member = segments[None, :] == labels[:, None]
    starts = jnp.min(jnp.where(member, ordered_places[None, :], sequence_length), axis=1)
    counts = jnp.sum(member.astype(jnp.int32), axis=1)
    grands = pick_from(parents, parents, labels)
    offsets = jnp.where(parents != labels, pick_from(counts, parents, labels), 0) + jnp.where(
        grands != parents, pick_from(counts, grands, labels), 0
    )
    block_rows = sequence_length // blocks
    chosen = order[:, None] == jnp.arange(blocks, dtype=jnp.int32)[None, :]
    segments = jnp.sum(
        jnp.where(chosen[:, :, None], segments.reshape(1, blocks, block_rows), 0), axis=1
    ).reshape(sequence_length)
    places = (
        order[:, None] * block_rows + jnp.arange(block_rows, dtype=jnp.int32)[None, :]
    ).reshape(sequence_length)
    tok_start = pick_from(starts, segments, labels)
    tok_offset = pick_from(offsets, segments, labels)
    tok_parent = pick_from(parents, segments, labels)
    tok_grand = pick_from(grands, segments, labels)
    positions = (places - tok_start + tok_offset).astype(jnp.float32)
    same_seg = (segments[None, :] == segments[:, None]) & (places[None, :] <= places[:, None])
    from_parent = (segments[None, :] == tok_parent[:, None]) & (tok_parent != segments)[:, None]
    from_grand = (segments[None, :] == tok_grand[:, None]) & (tok_grand != tok_parent)[:, None]
    visible = same_seg | from_parent | from_grand
    inv_freq = jnp.exp(
        jnp.arange(HEAD_WIDTH // 2, dtype=jnp.float32) * (-2.0 * math.log(10000.0) / HEAD_WIDTH)
    )
    angles = positions[:, None] * inv_freq[None, :]
    return (visible, jnp.cos(angles), jnp.sin(angles))


def product(former, latter):
    return jnp.dot(former, latter, preferred_element_type=jnp.float32)


def times_rows(former, latter):
    return lax.dot_general(
        former, latter, (((1,), (1,)), ((), ())), preferred_element_type=jnp.float32
    )


def over_rows(former, latter):
    return lax.dot_general(
        former, latter, (((0,), (0,)), ((), ())), preferred_element_type=jnp.float32
    )


def low(values):
    return values.astype(jnp.bfloat16)


def flip(values, axis_name, bit):
    size = lax.axis_size(axis_name)
    return lax.ppermute(values, axis_name, [(i, i ^ bit) for i in range(size)])


def settle(*groups):
    flat, tree = jax.tree.flatten(groups)
    return jax.tree.unflatten(tree, lax.optimization_barrier(flat))


def along_z(sent, columns_z):
    lines = [[2 * z + x for z in range(columns_z)] for x in range(2)]
    return lax.all_to_all(sent, "dp", 0, 0, axis_index_groups=lines)


def assemble(pieces, place):
    columns_z, _, columns = pieces[0][0].shape
    heights = [parts[0].shape[1] for parts in pieces]
    rows = sum(heights)

    def kernel(place_ref, *refs):
        out_ref = refs[-1]
        my_x = place_ref[0]
        for i, height in enumerate(heights):
            mine_ref, cross_ref, core_ref, core_cross_ref = refs[4 * i : 4 * i + 4]
            here = pl.ds(sum(heights[:i]), height)
            out_ref[my_x, here, :columns] = mine_ref[0]
            out_ref[my_x, here, columns:] = core_ref[0]
            out_ref[1 - my_x, here, :columns] = cross_ref[0]
            out_ref[1 - my_x, here, columns:] = core_cross_ref[0]

    out = pl.pallas_call(
        kernel,
        out_shape=jax.ShapeDtypeStruct((2 * columns_z, rows, 2 * columns), jnp.bfloat16),
        grid_spec=pltpu.PrefetchScalarGridSpec(
            num_scalar_prefetch=1,
            grid=(columns_z,),
            in_specs=[
                pl.BlockSpec((1, height, columns), lambda k, place_ref: (k, 0, 0))
                for height in heights
                for _ in range(4)
            ],
            out_specs=pl.BlockSpec((2, rows, 2 * columns), lambda k, place_ref: (k, 0, 0)),
        ),
        compiler_params=pltpu.CompilerParams(vmem_limit_bytes=32 << 20),
        cost_estimate=pl.CostEstimate(
            flops=0, transcendentals=0, bytes_accessed=16 * columns_z * rows * columns
        ),
    )(place, *[part for parts in pieces for part in parts])
    return out.reshape(2 * columns_z * rows, 2 * columns)


def beside(first, second):
    return jnp.concatenate([first, second], axis=1)


def pick_adapters(ids, whole, halved):
    rank = whole[0][0].shape[1]

    def kernel(ids_ref, *refs):
        count = len(refs) // 2
        for i in range(count):
            refs[count + i][...] = refs[i][0]

    in_specs, out_specs, shapes, stacks = [], [], [], []
    for entries, parity in ((whole, False), (halved, True)):
        for stack, near in entries:
            columns = stack.shape[2] // (2 if parity else 1)
            in_specs.append(
                pl.BlockSpec(
                    (1, rank, columns),
                    functools.partial(
                        lambda near, parity, i, ids_ref: (
                            ids_ref[1 if near else 0],
                            0,
                            ids_ref[2] if parity else 0,
                        ),
                        near,
                        parity,
                    ),
                )
            )
            out_specs.append(pl.BlockSpec((rank, columns), lambda i, ids_ref: (0, 0)))
            shapes.append(jax.ShapeDtypeStruct((rank, columns), stack.dtype))
            stacks.append(stack)
    return pl.pallas_call(
        kernel,
        out_shape=shapes,
        grid_spec=pltpu.PrefetchScalarGridSpec(
            num_scalar_prefetch=1, grid=(1,), in_specs=in_specs, out_specs=out_specs
        ),
        cost_estimate=TINY,
    )(ids, *stacks)


def fdot(former, latter, dims=((1,), (0,))):
    return lax.dot_general(former, latter, (dims, ((), ())), preferred_element_type=jnp.float32)


def turn(values, cosine, sine):
    half = values.shape[1] // 2
    front, back = values[:, :half], values[:, half:]
    return jnp.concatenate(
        [front * cosine - back * sine, back * cosine + front * sine], axis=1
    )


def project_heads(rows, weight, inner, expand, cosine, sine, queries):
    count, depth = rows.shape
    kinds = queries + 2

    def kernel(rows_ref, weight_ref, inner_ref, expand_ref, cosine_ref, sine_ref, out_ref):
        kind = pl.program_id(0) % kinds
        values = fdot(rows_ref[...], weight_ref[...]) + fdot(inner_ref[...], expand_ref[...])

        @pl.when(kind == kinds - 1)
        def _():
            out_ref[...] = low(values)

        @pl.when(kind < kinds - 1)
        def _():
            scale = jnp.where(kind < queries, HEAD_WIDTH ** (-0.5), 1.0)
            out_ref[...] = low(turn(values, cosine_ref[...], sine_ref[...]) * scale)

    whole = lambda array: pl.BlockSpec(array.shape, lambda j: (0, 0))
    return pl.pallas_call(
        kernel,
        out_shape=jax.ShapeDtypeStruct((count, weight.shape[1]), jnp.bfloat16),
        grid=(weight.shape[1] // HEAD_WIDTH,),
        in_specs=[
            whole(rows),
            pl.BlockSpec((depth, HEAD_WIDTH), lambda j: (0, j)),
            whole(inner),
            pl.BlockSpec((expand.shape[0], HEAD_WIDTH), lambda j: (0, j)),
            whole(cosine),
            whole(sine),
        ],
        out_specs=pl.BlockSpec((count, HEAD_WIDTH), lambda j: (0, j)),
        compiler_params=pltpu.CompilerParams(vmem_limit_bytes=40 << 20),
        cost_estimate=TINY,
    )(rows, weight, inner, expand, cosine, sine)


def soft_scores(query, keys, keep):
    bounded = jnp.tanh(fdot(query, keys, ((1,), (1,))) * (1.0 / 50.0))
    masked = jnp.where(keep, 50.0 * bounded, -1e30)
    exponent = jnp.exp(masked - jnp.max(masked, axis=1, keepdims=True))
    return bounded, exponent / jnp.sum(exponent, axis=1, keepdims=True)


def attend(projected, received, visible, queries):
    count = projected.shape[0]
    wide, pair = (queries + 2) * HEAD_WIDTH, 2 * HEAD_WIDTH

    def kernel(mine_ref, got_ref, visible_ref, out_ref):
        first = queries * HEAD_WIDTH
        mine = mine_ref[:, first:]
        got = got_ref[...]
        keys = jnp.concatenate([mine[:, :HEAD_WIDTH], got[:, :HEAD_WIDTH]])
        values = jnp.concatenate([mine[:, HEAD_WIDTH:], got[:, HEAD_WIDTH:]])
        keep = visible_ref[...] > 0
        for h in range(queries):
            columns = slice(h * HEAD_WIDTH, (h + 1) * HEAD_WIDTH)
            _, probs = soft_scores(mine_ref[:, columns], keys, keep)
            out_ref[:, columns] = low(fdot(low(probs), values))

    return pl.pallas_call(
        kernel,
        out_shape=jax.ShapeDtypeStruct((count, 2 * queries * HEAD_WIDTH), jnp.bfloat16),
        grid=(2,),
        in_specs=[
            pl.BlockSpec((count, wide), lambda j: (0, j)),
            pl.BlockSpec((count, pair), lambda j: (0, j)),
            pl.BlockSpec(visible.shape, lambda j: (0, 0)),
        ],
        out_specs=pl.BlockSpec((count, queries * HEAD_WIDTH), lambda j: (0, j)),
        compiler_params=pltpu.CompilerParams(vmem_limit_bytes=40 << 20),
        cost_estimate=TINY,
    )(projected, received, visible)


def attend_back(projected, received, visible, grad_mixed, cosine, sine, queries):
    count = projected.shape[0]
    wide, pair = (queries + 2) * HEAD_WIDTH, 2 * HEAD_WIDTH

    def kernel(mine_ref, got_ref, visible_ref, grad_ref, cos_ref, sin_ref, query_ref, pair_ref):
        first = queries * HEAD_WIDTH
        mine = mine_ref[:, first:]
        got = got_ref[...]
        keys = jnp.concatenate([mine[:, :HEAD_WIDTH], got[:, :HEAD_WIDTH]])
        values = jnp.concatenate([mine[:, HEAD_WIDTH:], got[:, HEAD_WIDTH:]])
        keep = visible_ref[...] > 0
        grad_keys, grad_values = 0.0, 0.0
        for h in range(queries):
            columns = slice(h * HEAD_WIDTH, (h + 1) * HEAD_WIDTH)
            query, grad = mine_ref[:, columns], grad_ref[:, columns]
            bounded, probs = soft_scores(query, keys, keep)
            grad_values = grad_values + fdot(low(probs), grad, ((0,), (0,)))
            grad_probs = fdot(grad, values, ((1,), (1,)))
            inner = jnp.sum(probs * grad_probs, axis=1, keepdims=True)
            grad_scores = low(probs * (grad_probs - inner) * (1.0 - bounded * bounded))
            grad_query = fdot(grad_scores, keys) * HEAD_WIDTH ** (-0.5)
            query_ref[:, columns] = low(turn(grad_query, cos_ref[...], -sin_ref[...]))
            grad_keys = grad_keys + fdot(grad_scores, query, ((0,), (0,)))
        pair_ref[:, :HEAD_WIDTH] = grad_keys
        pair_ref[:, HEAD_WIDTH:] = grad_values

    whole = lambda array: pl.BlockSpec(array.shape, lambda j: (0, 0))
    return pl.pallas_call(
        kernel,
        out_shape=[
            jax.ShapeDtypeStruct((count, 2 * queries * HEAD_WIDTH), jnp.bfloat16),
            jax.ShapeDtypeStruct((2 * count, 2 * pair), jnp.float32),
        ],
        grid=(2,),
        in_specs=[
            pl.BlockSpec((count, wide), lambda j: (0, j)),
            pl.BlockSpec((count, pair), lambda j: (0, j)),
            whole(visible),
            pl.BlockSpec((count, queries * HEAD_WIDTH), lambda j: (0, j)),
            whole(cosine),
            whole(sine),
        ],
        out_specs=[
            pl.BlockSpec((count, queries * HEAD_WIDTH), lambda j: (0, j)),
            pl.BlockSpec((2 * count, pair), lambda j: (0, j)),
        ],
        compiler_params=pltpu.CompilerParams(vmem_limit_bytes=48 << 20),
        cost_estimate=TINY,
    )(projected, received, visible, grad_mixed, cosine, sine)


GELU_A = math.sqrt(2.0 / math.pi)
GELU_B = 0.044715


def gate_and_up(rows, w_gate, w_up, inner, e_gate, e_up):
    count, depth = rows.shape
    units, tile = w_gate.shape[1], 256
    half = inner.shape[1] // 2
    step = count // 4

    def kernel(rows_ref, gate_w, up_w, inner_ref, gate_e, up_e, hidden_ref, gate_ref, up_ref):
        for i in range(4):
            here = slice(i * step, (i + 1) * step)
            inner_rows = inner_ref[here]
            gate = fdot(rows_ref[here], gate_w[...]) + fdot(inner_rows[:, :half], gate_e[...])
            up = fdot(rows_ref[here], up_w[...]) + fdot(inner_rows[:, half:], up_e[...])
            square = gate * gate
            bend = jnp.tanh(GELU_A * gate * (1.0 + GELU_B * square))
            half_up = 0.5 * (1.0 + bend)
            slope = half_up + 0.5 * gate * (1.0 - bend * bend) * (
                GELU_A * (1.0 + 3.0 * GELU_B * square)
            )
            bent = gate * half_up
            hidden_ref[here] = low(bent * up)
            gate_ref[here] = low(up * slope)
            up_ref[here] = low(bent)

    whole = lambda array: pl.BlockSpec(array.shape, lambda j: (0, 0))
    column = lambda array: pl.BlockSpec((array.shape[0], tile), lambda j: (0, j))
    return pl.pallas_call(
        kernel,
        out_shape=[jax.ShapeDtypeStruct((count, units), jnp.bfloat16)] * 3,
        grid=(units // tile,),
        in_specs=[whole(rows), column(w_gate), column(w_up), whole(inner), column(e_gate),
                  column(e_up)],
        out_specs=[pl.BlockSpec((count, tile), lambda j: (0, j))] * 3,
        compiler_params=pltpu.CompilerParams(vmem_limit_bytes=63 << 20),
        cost_estimate=TINY,
    )(rows, w_gate, w_up, inner, e_gate, e_up)


def square_shapes(count, depth):
    rows = count // 4
    half = rows // 2
    return [
        jax.ShapeDtypeStruct((rows, depth), jnp.float32),
        jax.ShapeDtypeStruct((half, depth), jnp.float32),
        jax.ShapeDtypeStruct((half, depth), jnp.float32),
        jax.ShapeDtypeStruct((rows, depth), jnp.bfloat16),
        jax.ShapeDtypeStruct((rows, depth), jnp.bfloat16),
    ]


def store_square(values, refs):
    rows = values.shape[0] // 4
    half = rows // 2
    mine_ref, y_ref, z_ref, send_y_ref, send_z_ref = refs
    mine_ref[...] = values[:rows]
    y_ref[...] = values[rows + half : 2 * rows]
    z_ref[...] = values[2 * rows : 2 * rows + half]
    send_y_ref[:half] = low(values[rows : rows + half])
    send_y_ref[half:] = low(values[3 * rows : 3 * rows + half])
    send_z_ref[:half] = low(values[2 * rows + half : 3 * rows])
    send_z_ref[half:] = low(values[3 * rows + half :])


def down_last(first, hidden, w_down_t):
    count, depth = first.shape
    tile = depth // 3

    def kernel(first_ref, hidden_ref, weight_ref, *out_refs):
        store_square(
            first_ref[...] + fdot(hidden_ref[...], weight_ref[...], ((1,), (1,))), out_refs
        )

    shapes = square_shapes(count, depth)
    return pl.pallas_call(
        kernel,
        out_shape=shapes,
        grid=(depth // tile,),
        in_specs=[
            pl.BlockSpec((count, tile), lambda j: (0, j)),
            pl.BlockSpec(hidden.shape, lambda j: (0, 0)),
            pl.BlockSpec((tile, w_down_t.shape[1]), lambda j: (j, 0)),
        ],
        out_specs=[pl.BlockSpec((shape.shape[0], tile), lambda j: (0, j)) for shape in shapes],
        compiler_params=pltpu.CompilerParams(vmem_limit_bytes=48 << 20),
        cost_estimate=TINY,
    )(first, hidden, w_down_t)


def feed_forward_back(grad_rows, e_down, s_gate_up, keep, chunks):
    count, depth = grad_rows.shape
    tiles = [chunk[0].shape[1] // 2 for chunk in chunks]
    columns = depth // 3
    steps = []
    for i, chunk in enumerate(chunks):
        steps += [(i, j) for j in range(chunk[0].shape[1] // tiles[i])]
    total = len(steps)
    firsts = [steps.index((i, 0)) for i in range(len(chunks))]
    counts = [chunk[0].shape[1] // tiles[i] for i, chunk in enumerate(chunks)]
    starts = [sum(chunk[0].shape[1] for chunk in chunks[:i]) for i in range(len(chunks))]
    width = sum(chunk[0].shape[1] for chunk in chunks)
    twice = e_down.shape[0]
    each = len(chunks[0])
    parts = square_shapes(count, depth)

    def kernel(grad_ref, e_down_ref, s_ref, keep_ref, *refs):
        ins = refs[: each * len(chunks)]
        out_refs = refs[each * len(chunks) :]
        rows_refs = out_refs[: len(parts)]
        inner_grad_ref, inner_ref, gates_ref, ups_ref, sums_ref = out_refs[len(parts) :]
        step = pl.program_id(0)

        @pl.when(step == 0)
        def _():
            inner_grad = fdot(grad_ref[...], e_down_ref[...], ((1,), (1,)))
            inner_grad_ref[...] = low(inner_grad * keep_ref[:, :twice])

        def one(place, begin, down, gate_in, up_in, s_down, e_gate, e_up, gate_w, up_w):
            grad = fdot(grad_ref[...], down[...]) + fdot(inner_grad_ref[...], s_down[...])
            grad_gate = low(grad * gate_in[...].astype(jnp.float32))
            grad_up = low(grad * up_in[...].astype(jnp.float32))
            gates_ref[:, place] = grad_gate
            ups_ref[:, place] = grad_up
            first = fdot(grad_gate, e_gate[...], ((1,), (1,)))
            second = fdot(grad_up, e_up[...], ((1,), (1,)))
            if begin:
                sums_ref[:, :twice] = first
                sums_ref[:, twice:] = second
            else:
                sums_ref[:, :twice] += first
                sums_ref[:, twice:] += second

        for k, (i, j) in enumerate(steps):
            place = slice(starts[i] + j * tiles[i], starts[i] + (j + 1) * tiles[i])
            pl.when(step == k)(
                functools.partial(one, place, k == 0, *ins[i * each : (i + 1) * each])
            )

        @pl.when(step == total - 1)
        def _():
            inner_ref[...] = low(sums_ref[...] * keep_ref[...])

        @pl.when(step >= total)
        def _():
            rows = fdot(inner_ref[...], s_ref[...])
            for i, chunk in enumerate(chunks):
                gate_w, up_w = ins[(i + 1) * each - 2 : (i + 1) * each]
                place = slice(starts[i], starts[i] + chunk[0].shape[1])
                rows += fdot(gates_ref[:, place], gate_w[...], ((1,), (1,)))
                rows += fdot(ups_ref[:, place], up_w[...], ((1,), (1,)))
            store_square(rows, rows_refs)

    once = pl.Buffered(1)
    whole = lambda array: pl.BlockSpec(array.shape, lambda j: (0, 0), pipeline_mode=once)
    second = lambda j: jnp.clip(j - total, 0, depth // columns - 1)

    def column(i, array):
        return pl.BlockSpec(
            (array.shape[0], tiles[i]),
            lambda j: (0, jnp.clip(j - firsts[i], 0, counts[i] - 1)),
        )

    def specs(i, chunk):
        return [column(i, array) for array in chunk[:-2]] + [
            pl.BlockSpec((columns, array.shape[1]), lambda j: (second(j), 0))
            for array in chunk[-2:]
        ]

    return pl.pallas_call(
        kernel,
        out_shape=parts
        + [
            jax.ShapeDtypeStruct((count, twice), jnp.bfloat16),
            jax.ShapeDtypeStruct((count, 2 * twice), jnp.bfloat16),
            jax.ShapeDtypeStruct((count, width), jnp.bfloat16),
            jax.ShapeDtypeStruct((count, width), jnp.bfloat16),
        ],
        grid=(total + depth // columns,),
        in_specs=[
            whole(grad_rows),
            whole(e_down),
            pl.BlockSpec((s_gate_up.shape[0], columns), lambda j: (0, second(j))),
            whole(keep),
        ]
        + [spec for i, chunk in enumerate(chunks) for spec in specs(i, chunk)],
        out_specs=[
            pl.BlockSpec((part.shape[0], columns), lambda j: (0, second(j))) for part in parts
        ]
        + [
            pl.BlockSpec((count, twice), lambda j: (0, 0)),
            pl.BlockSpec((count, 2 * twice), lambda j: (0, 0)),
            pl.BlockSpec((count, width), lambda j: (0, 0), pipeline_mode=once),
            pl.BlockSpec((count, width), lambda j: (0, 0), pipeline_mode=once),
        ],
        scratch_shapes=[pltpu.VMEM((count, 2 * twice), jnp.float32)],
        compiler_params=pltpu.CompilerParams(vmem_limit_bytes=63 << 20),
        cost_estimate=TINY,
    )(grad_rows, e_down, s_gate_up, keep, *[array for chunk in chunks for array in chunk])


def scatter_pair(part):
    rows = part.shape[0] // 2
    got = flip(low(part[rows:]), "tensor", 2)
    return part[:rows] + got.astype(jnp.float32)


def gather_pair(own):
    return jnp.concatenate([own, flip(own, "tensor", 2)])


def gather_square(own):
    half = own.shape[0] // 2
    from_y = flip(own, "tensor", 2)
    from_z = flip(own, "dp", 2)
    send_z, send_y = settle(from_y[:half], from_z[half:])
    diagonal = [flip(send_z, "dp", 2), flip(send_y, "tensor", 2)]
    return jnp.concatenate([own, from_y, from_z] + diagonal)


def sum_by_adapter(hots, gathered, shared, widths):
    count, rows, columns = gathered.shape
    adapters = hots.shape[1]
    cuts = [0, shared] + [shared + sum(widths[: i + 1]) for i in range(len(widths))]

    def kernel(hots_ref, gathered_ref, *out_refs):
        for i, out_ref in enumerate(out_refs):
            here = slice(cuts[i], cuts[i + 1])
            for adapter in range(adapters):
                total = 0.0
                for entry in range(count):
                    total += hots_ref[entry, adapter] * gathered_ref[entry, :, here].astype(
                        jnp.float32
                    )
                out_ref[adapter] = total.astype(out_ref.dtype)

    shapes = [jax.ShapeDtypeStruct((adapters, rows, shared), jnp.bfloat16)] + [
        jax.ShapeDtypeStruct((adapters, rows, width), jnp.float32) for width in widths
    ]
    return pl.pallas_call(
        kernel,
        out_shape=shapes,
        in_specs=[
            pl.BlockSpec(memory_space=pltpu.SMEM),
            pl.BlockSpec(gathered.shape, lambda: (0, 0, 0)),
        ],
        out_specs=[pl.BlockSpec(shape.shape, lambda: (0, 0, 0)) for shape in shapes],
        compiler_params=pltpu.CompilerParams(vmem_limit_bytes=40 << 20),
        cost_estimate=TINY,
    )(hots, gathered)


def sum_unit_grads(hots, gathered, kinds):
    count, rows, columns = gathered.shape
    rank = rows // kinds
    adapters = hots.shape[2]

    def kernel(hots_ref, gathered_ref, *out_refs):
        for side in range(2):
            for kind in range(kinds):
                here = slice(kind * rank, (kind + 1) * rank)
                for adapter in range(adapters):
                    total = 0.0
                    for entry in range(count):
                        total += hots_ref[side, entry, adapter] * gathered_ref[
                            entry, here
                        ].astype(jnp.float32)
                    out_refs[kind][adapter, :, side * columns : (side + 1) * columns] = total

    return pl.pallas_call(
        kernel,
        out_shape=[jax.ShapeDtypeStruct((adapters, rank, 2 * columns), jnp.float32)] * kinds,
        in_specs=[
            pl.BlockSpec(memory_space=pltpu.SMEM),
            pl.BlockSpec(gathered.shape, lambda: (0, 0, 0)),
        ],
        out_specs=[pl.BlockSpec((adapters, rank, 2 * columns), lambda: (0, 0, 0))] * kinds,
        compiler_params=pltpu.CompilerParams(vmem_limit_bytes=48 << 20),
        cost_estimate=TINY,
    )(hots, gathered)


def join_halves(core, mine, other, kinds):
    adapters, rank, columns = mine.shape
    half = columns // kinds

    def kernel(core_ref, mine_ref, other_ref, *out_refs):
        swap = core_ref[0] == 1
        for kind in range(kinds):
            here = slice(kind * half, (kind + 1) * half)
            first = mine_ref[:, :, here].astype(jnp.float32)
            second = other_ref[:, :, here].astype(jnp.float32)
            out_refs[kind][:, :, :half] = jnp.where(swap, second, first)
            out_refs[kind][:, :, half:] = jnp.where(swap, first, second)

    return pl.pallas_call(
        kernel,
        out_shape=[jax.ShapeDtypeStruct((adapters, rank, 2 * half), jnp.float32)] * kinds,
        in_specs=[pl.BlockSpec(memory_space=pltpu.SMEM)]
        + [pl.BlockSpec(mine.shape, lambda: (0, 0, 0))] * 2,
        out_specs=[pl.BlockSpec((adapters, rank, 2 * half), lambda: (0, 0, 0))] * kinds,
        compiler_params=pltpu.CompilerParams(vmem_limit_bytes=48 << 20),
        cost_estimate=TINY,
    )(core, mine, other)


def square_first(parts):
    mine, to_y, to_z, send_y, send_z = parts
    return (flip(send_y, "tensor", 2), flip(send_z, "dp", 2)), (mine, to_y, to_z)


def square_last(first, rest):
    got_y, got_z = (got.astype(jnp.float32) for got in first)
    mine, to_y, to_z = rest
    half = to_y.shape[0]
    send_y, send_z = settle(low(to_y + got_z[half:]), low(to_z + got_y[half:]))
    last_y = flip(send_y, "tensor", 2).astype(jnp.float32)
    last_z = flip(send_z, "dp", 2).astype(jnp.float32)
    return jnp.concatenate(
        [mine[:half] + got_y[:half] + last_z, mine[half:] + got_z[:half] + last_y]
    )


def tree_bits(trees):
    return [1 << b for b in range(1, trees.bit_length() - 1)][::-1] + [1]


def tree_order(trees):
    order = [0]
    for bit in tree_bits(trees):
        order += [i ^ bit for i in order]
    return order


def on_device(
    layer_input,
    cotangent,
    norm_gains,
    w_query,
    w_key,
    w_value,
    w_output,
    w_gate,
    w_up,
    w_down,
    query_shrink,
    key_shrink,
    value_shrink,
    output_shrink,
    gate_shrink,
    up_shrink,
    down_shrink,
    query_expand,
    key_expand,
    value_expand,
    output_expand,
    gate_expand,
    up_expand,
    down_expand,
    adapter_ids,
    parent_segments,
    segment_ids,
):
    trees = lax.axis_size("dp")
    columns_z = trees // 2
    my_tree = lax.axis_index("dp")
    my_z, my_x = my_tree // 2, my_tree % 2
    my_part = lax.axis_index("tensor")
    odd = my_z % 2 == 1
    norm_gain = norm_gains.astype(jnp.float32)
    place = my_x.astype(jnp.int32)[None]

    def halves(values):
        half = values.shape[-1] // 2
        return jnp.stack([values[:, :half], values[:, half:]])

    def on_core(values):
        return flip(values, "tensor", 1)

    w_qkv = jnp.concatenate([w_query, w_key, w_value], axis=1)
    cut = w_qkv.shape[0] // 2 // 16 * 16
    gate_halves, up_halves, down_halves = halves(w_gate), halves(w_up), halves(w_down.T)
    units = gate_halves.shape[2]
    first_units = (units // 128 + 1) // 2 * 128
    waiting = [
        w_qkv[None, :cut],
        w_qkv[None, cut:],
        w_output.T[None],
        gate_halves[:, :, first_units:],
        up_halves[:, :, first_units:],
        gate_halves[:, :, :first_units],
        up_halves[:, :, :first_units],
        down_halves[:, :, :first_units],
        down_halves[:, :, first_units:],
    ]
    waiting = [
        jnp.concatenate([blocks] * (columns_z // blocks.shape[0])) for blocks in waiting
    ]
    count = len(waiting)
    near, cross = {}, {}

    near_core, cross_core = {}, {}

    def transfers(step):
        if step < count:
            near[step] = along_z(waiting[step], columns_z)
        if 0 <= step - 1 < count:
            cross[step - 1] = flip(near[step - 1], "dp", 1)
            near_core[step - 1] = on_core(near[step - 1])
        if 0 <= step - 2 < count:
            cross_core[step - 2] = on_core(cross[step - 2])

    def close(step, *values):
        moved = [
            (store, key)
            for store, key in (
                (near, step),
                (cross, step - 1),
                (near_core, step - 1),
                (cross_core, step - 2),
            )
            if key in store
        ]
        following = [waiting[step + 1]] if step + 1 < count else []
        moved_values, following, values = settle(
            [store[key] for store, key in moved], following, values
        )
        for (store, key), value in zip(moved, moved_values):
            store[key] = value
        if following:
            waiting[step + 1] = following[0]
        return values

    def matrix(*keys):
        stores = (near, cross, near_core, cross_core)
        return assemble([[store[key] for store in stores] for key in keys], place)

    transfers(0)
    own_rows = layer_input.astype(jnp.float32)
    normed = low(rms_scale(own_rows, norm_gain[0]))
    near_ids = flip(adapter_ids, "dp", 2)
    labels = jnp.arange(ADAPTERS, dtype=jnp.int32)
    order = jnp.stack([my_part, my_part ^ 2, my_part ^ 1, my_part ^ 3]).astype(jnp.int32)
    visible, cos_rows, sin_rows = tree_tables(segment_ids, parent_segments[0], order)
    row_count = 2 * normed.shape[0]
    visible = low(visible[:row_count])
    cos_rows, sin_rows = cos_rows[:row_count], sin_rows[:row_count]
    normed, near_ids, visible, cos_rows, sin_rows = close(
        0, normed, near_ids, visible, cos_rows, sin_rows
    )

    transfers(1)
    normed_all = gather_pair(normed)
    picked = pick_adapters(
        jnp.concatenate([adapter_ids, near_ids, (my_z % 2).astype(jnp.int32)[None]]),
        [
            (stack, False)
            for stack in (
                query_shrink,
                key_shrink,
                value_shrink,
                query_expand,
                key_expand,
                value_expand,
                output_shrink,
                output_expand,
            )
        ]
        + [
            (stack, near_tree)
            for stack in (gate_shrink, up_shrink, down_expand)
            for near_tree in (False, True)
        ],
        [
            (stack, near_tree)
            for stack in (gate_expand, up_expand, down_shrink)
            for near_tree in (False, True)
        ],
    )
    s_qkv = jnp.concatenate(picked[0:3])
    e_parts = picked[3:6]
    rank = e_parts[0].shape[0]
    widths = [part.shape[1] for part in e_parts]
    attn_mine = jnp.concatenate(picked[3:7], axis=1)
    e_output = picked[7]
    s_gate_up = jnp.concatenate(picked[8:12])
    e_down = jnp.concatenate(picked[12:14])
    ffn_mine = jnp.concatenate(picked[14:20])
    normed_all, attn_mine, e_output, s_gate_up, e_down, ffn_mine, s_qkv = close(
        1, normed_all, attn_mine, e_output, s_gate_up, e_down, ffn_mine, s_qkv
    )

    transfers(2)
    attn_other = on_core(attn_mine)
    ffn_other = on_core(ffn_mine)
    inner_qkv = low(times_rows(normed_all, s_qkv))
    attn_other, ffn_other, inner_qkv = close(2, attn_other, ffn_other, inner_qkv)

    transfers(3)
    heads_here = sum(widths)
    queries = widths[0] // HEAD_WIDTH
    e_mine = attn_mine[:, :heads_here]
    e_other = attn_other[:, :heads_here]
    s_output = beside(attn_mine[:, heads_here:], attn_other[:, heads_here:])
    starts = [sum(widths[:i]) for i in range(4)]
    column_kind = sum(
        (jnp.arange(heads_here, dtype=jnp.int32) >= start).astype(jnp.int32)
        for start in starts[1:3]
    )
    kind_mask = (
        jnp.arange(3 * rank, dtype=jnp.int32)[:, None] // rank
        == jnp.concatenate([column_kind, column_kind])[None, :]
    )
    e_qkv = low(jnp.where(kind_mask, jnp.tile(beside(e_mine, e_other), (3, 1)), 0.0))
    units_a = beside(ffn_mine[:, :first_units], ffn_other[:, :first_units])
    units_b = beside(ffn_mine[:, first_units:], ffn_other[:, first_units:])
    adapters_ab = [
        [block[i * 2 * rank : (i + 1) * 2 * rank] for i in range(3)] for block in (units_a, units_b)
    ]
    e_qkv, s_output, adapters_ab = close(3, e_qkv, s_output, adapters_ab)

    bits = tree_bits(trees)
    tree_ids = adapter_ids
    transfers(4)
    for bit in bits[:-2]:
        tree_ids = jnp.concatenate([tree_ids, flip(tree_ids, "dp", bit)])
    full_qkv = matrix(0, 1)
    projected = project_heads(
        normed_all, full_qkv, inner_qkv, e_qkv, cos_rows, sin_rows, queries
    )
    received = on_core(
        beside(projected[:, heads_here + starts[1] :], projected[:, starts[1] : heads_here])
    )
    full_qkv, projected, received, tree_ids = close(
        4, full_qkv, projected, received, tree_ids
    )

    transfers(5)
    full_out_t = matrix(2)
    tree_ids = jnp.concatenate([tree_ids, flip(tree_ids, "dp", bits[-2])])
    mixed_heads = attend(projected, received, visible, queries)
    inner_output = low(times_rows(mixed_heads, s_output))
    attn_part = times_rows(mixed_heads, full_out_t) + product(inner_output, e_output)
    attended = scatter_pair(attn_part)
    mixed_heads, full_out_t, inner_output, attended, tree_ids = close(
        5, mixed_heads, full_out_t, inner_output, attended, tree_ids
    )

    transfers(6)
    full_gate_b = matrix(3)
    residual = own_rows + rms_scale(attended, norm_gain[1])
    normed_ffn = low(rms_scale(residual, norm_gain[2]))
    normed_y = flip(normed_ffn, "tensor", 2)
    half_rows = normed_ffn.shape[0] // 2
    normed_z_first = flip(normed_ffn[:half_rows], "dp", 2)
    residual, normed_ffn, normed_y, normed_z_first, full_gate_b = close(
        6, residual, normed_ffn, normed_y, normed_z_first, full_gate_b
    )

    transfers(7)
    normed_z_last = flip(normed_ffn[half_rows:], "dp", 2)
    full_up_b = matrix(4)
    tree_ids = jnp.concatenate([tree_ids, flip(tree_ids, "dp", bits[-1])])
    normed_z_last, full_up_b, tree_ids = close(7, normed_z_last, full_up_b, tree_ids)

    transfers(8)
    normed_z = jnp.concatenate([normed_z_first, normed_z_last])
    normed_zy = flip(normed_z, "tensor", 2)
    full_gate_a = matrix(5)
    ffn_rows = jnp.concatenate([normed_ffn, normed_y, normed_z, normed_zy])
    block_rows = residual.shape[0]
    row_block = jnp.arange(4 * block_rows, dtype=jnp.int32) // block_rows
    row_near = (row_block // 2)[:, None]
    rank_near = (jnp.arange(4 * rank, dtype=jnp.int32) // rank % 2)[None, :]
    keep_four = (row_near == rank_near).astype(jnp.float32)
    keep_two = keep_four[:, : 2 * rank]
    inner_gate_up = low(keep_four * times_rows(ffn_rows, s_gate_up))
    chunk_b = gate_and_up(
        ffn_rows, full_gate_b, full_up_b, inner_gate_up, adapters_ab[1][0], adapters_ab[1][1]
    )
    ffn_rows, inner_gate_up, chunk_b, full_gate_a = close(
        8, ffn_rows, inner_gate_up, chunk_b, full_gate_a
    )

    transfers(9)
    full_up_a = matrix(6)
    chunk_a = gate_and_up(
        ffn_rows, full_gate_a, full_up_a, inner_gate_up, adapters_ab[0][0], adapters_ab[0][1]
    )
    chunk_out = [chunk_a, chunk_b]
    hidden = [parts[0] for parts in chunk_out]
    inner_down = low(
        keep_two
        * (times_rows(hidden[0], adapters_ab[0][2]) + times_rows(hidden[1], adapters_ab[1][2]))
    )
    full_down_a = matrix(7)
    ffn_first = times_rows(hidden[0], full_down_a) + product(inner_down, e_down)
    chunk_out, inner_down, ffn_first = close(9, chunk_out, inner_down, ffn_first)
    hidden = [parts[0] for parts in chunk_out]

    cross_core[8] = on_core(cross[8])
    full_down_b = matrix(8)
    ffn_out = square_last(*square_first(down_last(ffn_first, hidden[1], full_down_b)))
    layer_output = low(residual + rms_scale(ffn_out, norm_gain[3]))

    grad_out = cotangent.astype(jnp.float32)
    grad_ffn = gather_square(low(rms_back(ffn_out, norm_gain[3], grad_out)))
    *grad_normed_parts, grad_inner_down, grad_inner_gate_up, grad_gate, grad_up = feed_forward_back(
        grad_ffn,
        e_down,
        s_gate_up,
        keep_four,
        [
            (full_down, *parts[1:], adapters[2], adapters[0], adapters[1], full_gate, full_up)
            for full_down, full_gate, full_up, parts, adapters in (
                (full_down_a, full_gate_a, full_up_a, chunk_out[0], adapters_ab[0]),
                (full_down_b, full_gate_b, full_up_b, chunk_out[1], adapters_ab[1]),
            )
        ],
    )
    def from_other_core(mine, other):
        return low(mine + on_core(low(other)).astype(jnp.float32))

    parts_first, parts_rest = square_first(grad_normed_parts)
    grad_shrink_down = jnp.concatenate(
        [over_rows(grad_inner_down, units_of) for units_of in hidden], axis=1
    )
    inner_gate, inner_up = inner_gate_up[:, : 2 * rank], inner_gate_up[:, 2 * rank :]
    grad_units = jnp.stack(
        [
            grads.reshape(2, rank, 2 * units)
            for grads in (
                over_rows(inner_gate, grad_gate),
                over_rows(inner_up, grad_up),
                grad_shrink_down,
            )
        ],
        axis=1,
    ).reshape(6 * rank, 2 * units)
    rest = units - first_units
    cuts = [0, first_units, 2 * first_units, 2 * first_units + rest, 2 * units]
    quarters = [grad_units[:, cuts[i] : cuts[i + 1]] for i in range(4)]
    mine, other = beside(quarters[0], quarters[2]), beside(quarters[1], quarters[3])
    local = from_other_core(mine, other)
    parts_first, local, grad_inner_gate_up, grad_ffn = settle(
        parts_first, local, grad_inner_gate_up, grad_ffn
    )
    local_all = jnp.stack([local, flip(local, "dp", 1)])
    grad_expand_down = over_rows(inner_down, grad_ffn)
    grad_shrink_gate_up = over_rows(grad_inner_gate_up, ffn_rows)
    grad_normed_ffn = square_last(parts_first, parts_rest)
    grad_resid = grad_out + rms_back(residual, norm_gain[2], grad_normed_ffn)
    grad_attn_mine = low(rms_back(attended, norm_gain[1], grad_resid))
    shared = jnp.concatenate([grad_shrink_gate_up, grad_expand_down]).reshape(3, 2, rank, -1)
    grad_attn_mine, grad_resid, local_all, shared = settle(
        grad_attn_mine, grad_resid, local_all, shared
    )

    def core_half(blocks):
        half = blocks.shape[-1] // 2
        kept = jnp.where(my_part % 2 == 1, blocks[..., half:], blocks[..., :half])
        return jnp.concatenate([low(block) for block in kept], axis=1)

    def with_bit(values, bit):
        return jnp.concatenate([values, flip(values, "dp", bit)])

    grad_attn = gather_pair(grad_attn_mine)
    shared_near = flip(low(shared[:, 1]), "dp", 2)
    bits = tree_bits(trees)
    for bit in bits[:-2]:
        local_all = with_bit(local_all, bit)
    grad_attn, local_all, shared, shared_near = settle(grad_attn, local_all, shared, shared_near)

    local_near = flip(local_all, "dp", bits[-2])
    grad_inner_output = low(times_rows(grad_attn, e_output))
    grad_mixed = low(product(grad_attn, full_out_t) + product(grad_inner_output, s_output))
    grad_queries, grad_pairs = attend_back(
        projected, received, visible, grad_mixed, cos_rows, sin_rows, queries
    )
    pair = 2 * HEAD_WIDTH
    to_core = low(beside(grad_pairs[row_count:, pair:], grad_pairs[row_count:, :pair]))
    from_core = on_core(to_core)
    shared = shared[:, 0] + shared_near.astype(jnp.float32)
    shared = shared + on_core(low(shared)).astype(jnp.float32)
    shared = shared + flip(low(shared), "tensor", 2).astype(jnp.float32)
    shared_mine = core_half(shared)
    from_core, grad_queries, grad_pairs, shared_mine = settle(
        from_core, grad_queries, grad_pairs, shared_mine
    )

    shared_all = with_bit(shared_mine[None], 1)
    grad_expand_output = over_rows(inner_output, grad_attn)
    grad_shrink_output = over_rows(grad_inner_output, mixed_heads)
    grad_pairs = grad_pairs[:row_count] + from_core.astype(jnp.float32)
    grad_sides = []
    for side in range(2):
        keys_values = grad_pairs[:, side * pair : (side + 1) * pair]
        grad_sides += [
            grad_queries[:, side * widths[0] : (side + 1) * widths[0]],
            low(turn(keys_values[:, :HEAD_WIDTH], cos_rows, -sin_rows)),
            low(keys_values[:, HEAD_WIDTH:]),
        ]
    grad_qkv = jnp.concatenate(grad_sides, axis=1)
    grad_inner_qkv = low(times_rows(grad_qkv, e_qkv))
    grad_expand_qkv = over_rows(inner_qkv, grad_qkv)
    last = jnp.concatenate(
        [over_rows(grad_inner_qkv, normed_all), grad_expand_output]
    ).reshape(4, rank, -1)
    pieces = []
    for side in range(2):
        for i in range(3):
            first = side * heads_here + starts[i]
            pieces.append(grad_expand_qkv[i * rank : (i + 1) * rank, first : first + widths[i]])
        pieces.append(grad_shrink_output[:, side * widths[0] : (side + 1) * widths[0]])
    local_attn = from_other_core(
        jnp.concatenate(pieces[:4], axis=1), jnp.concatenate(pieces[4:], axis=1)
    )
    last = last + on_core(low(last)).astype(jnp.float32)
    last, local_attn, grad_qkv, grad_inner_qkv, shared_all = settle(
        last, local_attn, grad_qkv, grad_inner_qkv, shared_all
    )

    last_y = flip(low(last), "tensor", 2)
    for bit in bits[:-2]:
        shared_all = with_bit(shared_all, bit)
    part = times_rows(grad_qkv, full_qkv) + product(grad_inner_qkv, s_qkv)
    last_y, part, shared_all, local_near = settle(last_y, part, shared_all, local_near)

    last_mine = beside(core_half(last + last_y.astype(jnp.float32)), local_attn)
    last_all = lax.all_to_all(
        jnp.broadcast_to(last_mine[None], (trees,) + last_mine.shape), "dp", 0, 0
    )
    from_y = flip(low(part[block_rows:]), "tensor", 2)
    shared_all = with_bit(shared_all, bits[-2])
    from_y, shared_all = settle(from_y, shared_all)
    grad_normed = part[:block_rows] + from_y.astype(jnp.float32)
    input_grad = grad_resid + rms_back(own_rows, norm_gain[0], grad_normed)
    local_all = jnp.concatenate([local_all, local_near])

    tree_ids = tree_ids.reshape(trees)
    hot_near = (tree_ids[:, None] == labels[None, :]).astype(jnp.float32)
    distances = my_tree ^ jnp.arange(trees, dtype=jnp.int32)
    place_of = jnp.stack(
        [jnp.asarray(tree_order(trees).index(j), jnp.int32) for j in range(trees)]
    )
    at = jnp.sum(
        jnp.where(
            distances[:, None] == jnp.arange(trees, dtype=jnp.int32)[None, :], place_of[None, :], 0
        ),
        axis=1,
    )
    hot_trees = jnp.sum(
        jnp.where(
            at[:, None, None] == jnp.arange(trees, dtype=jnp.int32)[None, :, None],
            hot_near[None],
            0.0,
        ),
        axis=1,
    )

    order_local = [0, 1]
    for bit in bits[:-1]:
        order_local += [i ^ bit for i in order_local]
    ids_at = {tree: i for i, tree in enumerate(tree_order(trees))}
    hots, crossing = [], []
    for j in order_local:
        for near_tree in range(2):
            hots.append(hot_near[ids_at[j ^ (2 * near_tree)]])
            crossing.append((j // 2) % 2)
    hots = jnp.stack(hots)
    parity = jnp.asarray(crossing, jnp.int32) ^ (my_z % 2).astype(jnp.int32)
    local_all = local_all.reshape(2 * trees, 3 * rank, units)
    hots = jnp.stack([jnp.where(parity[:, None] == side, hots, 0.0) for side in range(2)])
    hots_local = jnp.stack([hot_near[ids_at[j]] for j in order_local])
    out_expand_gate, out_expand_up, out_shrink_down = sum_unit_grads(hots, local_all, 3)
    core = (my_part % 2).astype(jnp.int32)[None]
    depth_half = s_qkv.shape[1] // 2
    (sums,) = sum_by_adapter(hots_local, shared_all, 3 * depth_half, [])
    out_shrink_gate, out_shrink_up, out_expand_down = join_halves(core, sums, on_core(sums), 3)
    (last_all, input_grad, out_expand_gate, out_expand_up, out_shrink_down, out_shrink_gate,
     out_shrink_up, out_expand_down) = settle(
        last_all, input_grad, out_expand_gate, out_expand_up, out_shrink_down, out_shrink_gate,
        out_shrink_up, out_expand_down,
    )
    sums, out_expand_query, out_expand_key, out_expand_value, out_shrink_output = sum_by_adapter(
        hot_trees, last_all, 4 * depth_half, widths + widths[:1]
    )
    out_shrink_query, out_shrink_key, out_shrink_value, out_expand_output = join_halves(
        core, sums, on_core(sums), 4
    )
    return (
        layer_output,
        input_grad,
        out_shrink_query,
        out_shrink_key,
        out_shrink_value,
        out_shrink_output,
        out_shrink_gate,
        out_shrink_up,
        out_shrink_down,
        out_expand_query,
        out_expand_key,
        out_expand_value,
        out_expand_output,
        out_expand_gate,
        out_expand_up,
        out_expand_down,
    )


def solution(mesh):
    placed = (
        P(("dp", "tensor"), None),
        P(("dp", "tensor"), None),
        P(),
        P("dp", "tensor"),
        P("dp", "tensor"),
        P("dp", "tensor"),
        P("tensor", "dp"),
        P("dp", "tensor"),
        P("dp", "tensor"),
        P("tensor", "dp"),
        P(),
        P(),
        P(),
        P(None, None, "tensor"),
        P(),
        P(),
        P(None, None, "tensor"),
        P(None, None, "tensor"),
        P(None, None, "tensor"),
        P(None, None, "tensor"),
        P(),
        P(None, None, "tensor"),
        P(None, None, "tensor"),
        P(),
        P("dp"),
        P("dp", None),
        P("dp"),
    )
    return jax.shard_map(
        on_device,
        mesh=mesh,
        in_specs=placed,
        out_specs=(
            P(("dp", "tensor"), None),
            P(("dp", "tensor"), None),
            P(),
            P(),
            P(),
            P(None, None, "tensor"),
            P(),
            P(),
            P(None, None, "tensor"),
            P(None, None, "tensor"),
            P(None, None, "tensor"),
            P(None, None, "tensor"),
            P(),
            P(None, None, "tensor"),
            P(None, None, "tensor"),
            P(),
        ),
        check_vma=False,
    )
```

```python
import functools
import math

import jax
import jax.numpy as jnp
from jax import lax
from jax.experimental import pallas as pl
from jax.experimental.pallas import tpu as pltpu
from jax.sharding import PartitionSpec as P

HEAD_WIDTH = 256
ADAPTERS = 8
TINY = pl.CostEstimate(flops=1, transcendentals=0, bytes_accessed=1)


def rms_scale(value_rows, gain_row):
    inverse = lax.rsqrt(jnp.mean(value_rows * value_rows, axis=-1, keepdims=True) + 1e-06)
    return value_rows * inverse * gain_row


def rms_back(value_rows, gain_row, upstream):
    inverse = lax.rsqrt(jnp.mean(value_rows * value_rows, axis=-1, keepdims=True) + 1e-06)
    scaled = gain_row * upstream
    return inverse * scaled - value_rows * (inverse * inverse * inverse) * jnp.mean(
        value_rows * scaled, axis=-1, keepdims=True
    )


def pick_from(lookup, indices, labels):
    return jnp.sum(jnp.where(indices[:, None] == labels[None, :], lookup[None, :], 0), axis=1)


def tree_tables(segments, parents, order):
    count_seg = parents.shape[0]
    sequence_length = segments.shape[0]
    blocks = order.shape[0]
    labels = jnp.arange(count_seg, dtype=jnp.int32)
    ordered_places = jnp.arange(sequence_length, dtype=jnp.int32)
    member = segments[None, :] == labels[:, None]
    starts = jnp.min(jnp.where(member, ordered_places[None, :], sequence_length), axis=1)
    counts = jnp.sum(member.astype(jnp.int32), axis=1)
    grands = pick_from(parents, parents, labels)
    offsets = jnp.where(parents != labels, pick_from(counts, parents, labels), 0) + jnp.where(
        grands != parents, pick_from(counts, grands, labels), 0
    )
    block_rows = sequence_length // blocks
    chosen = order[:, None] == jnp.arange(blocks, dtype=jnp.int32)[None, :]
    segments = jnp.sum(
        jnp.where(chosen[:, :, None], segments.reshape(1, blocks, block_rows), 0), axis=1
    ).reshape(sequence_length)
    places = (
        order[:, None] * block_rows + jnp.arange(block_rows, dtype=jnp.int32)[None, :]
    ).reshape(sequence_length)
    tok_start = pick_from(starts, segments, labels)
    tok_offset = pick_from(offsets, segments, labels)
    tok_parent = pick_from(parents, segments, labels)
    tok_grand = pick_from(grands, segments, labels)
    positions = (places - tok_start + tok_offset).astype(jnp.float32)
    same_seg = (segments[None, :] == segments[:, None]) & (places[None, :] <= places[:, None])
    from_parent = (segments[None, :] == tok_parent[:, None]) & (tok_parent != segments)[:, None]
    from_grand = (segments[None, :] == tok_grand[:, None]) & (tok_grand != tok_parent)[:, None]
    visible = same_seg | from_parent | from_grand
    inv_freq = jnp.exp(
        jnp.arange(HEAD_WIDTH // 2, dtype=jnp.float32) * (-2.0 * math.log(10000.0) / HEAD_WIDTH)
    )
    angles = positions[:, None] * inv_freq[None, :]
    return (visible, jnp.cos(angles), jnp.sin(angles))


def product(former, latter):
    return jnp.dot(former, latter, preferred_element_type=jnp.float32)


def times_rows(former, latter):
    return lax.dot_general(
        former, latter, (((1,), (1,)), ((), ())), preferred_element_type=jnp.float32
    )


def over_rows(former, latter):
    return lax.dot_general(
        former, latter, (((0,), (0,)), ((), ())), preferred_element_type=jnp.float32
    )


def low(values):
    return values.astype(jnp.bfloat16)


def flip(values, axis_name, bit):
    size = lax.axis_size(axis_name)
    return lax.ppermute(values, axis_name, [(i, i ^ bit) for i in range(size)])


def settle(*groups):
    flat, tree = jax.tree.flatten(groups)
    return jax.tree.unflatten(tree, lax.optimization_barrier(flat))


def along_z(sent, columns_z):
    lines = [[2 * z + x for z in range(columns_z)] for x in range(2)]
    return lax.all_to_all(sent, "dp", 0, 0, axis_index_groups=lines)


def assemble(pieces, place):
    columns_z, _, columns = pieces[0][0].shape
    heights = [parts[0].shape[1] for parts in pieces]
    rows = sum(heights)

    def kernel(place_ref, *refs):
        out_ref = refs[-1]
        my_x = place_ref[0]
        for i, height in enumerate(heights):
            mine_ref, cross_ref, core_ref, core_cross_ref = refs[4 * i : 4 * i + 4]
            here = pl.ds(sum(heights[:i]), height)
            out_ref[my_x, here, :columns] = mine_ref[0]
            out_ref[my_x, here, columns:] = core_ref[0]
            out_ref[1 - my_x, here, :columns] = cross_ref[0]
            out_ref[1 - my_x, here, columns:] = core_cross_ref[0]

    out = pl.pallas_call(
        kernel,
        out_shape=jax.ShapeDtypeStruct((2 * columns_z, rows, 2 * columns), jnp.bfloat16),
        grid_spec=pltpu.PrefetchScalarGridSpec(
            num_scalar_prefetch=1,
            grid=(columns_z,),
            in_specs=[
                pl.BlockSpec((1, height, columns), lambda k, place_ref: (k, 0, 0))
                for height in heights
                for _ in range(4)
            ],
            out_specs=pl.BlockSpec((2, rows, 2 * columns), lambda k, place_ref: (k, 0, 0)),
        ),
        compiler_params=pltpu.CompilerParams(vmem_limit_bytes=32 << 20),
        cost_estimate=pl.CostEstimate(
            flops=0, transcendentals=0, bytes_accessed=16 * columns_z * rows * columns
        ),
    )(place, *[part for parts in pieces for part in parts])
    return out.reshape(2 * columns_z * rows, 2 * columns)


def beside(first, second):
    return jnp.concatenate([first, second], axis=1)


def pick_adapters(ids, whole, halved):
    rank = whole[0][0].shape[1]

    def kernel(ids_ref, *refs):
        count = len(refs) // 2
        for i in range(count):
            refs[count + i][...] = refs[i][0]

    in_specs, out_specs, shapes, stacks = [], [], [], []
    for entries, parity in ((whole, False), (halved, True)):
        for stack, near in entries:
            columns = stack.shape[2] // (2 if parity else 1)
            in_specs.append(
                pl.BlockSpec(
                    (1, rank, columns),
                    functools.partial(
                        lambda near, parity, i, ids_ref: (
                            ids_ref[1 if near else 0],
                            0,
                            ids_ref[2] if parity else 0,
                        ),
                        near,
                        parity,
                    ),
                )
            )
            out_specs.append(pl.BlockSpec((rank, columns), lambda i, ids_ref: (0, 0)))
            shapes.append(jax.ShapeDtypeStruct((rank, columns), stack.dtype))
            stacks.append(stack)
    return pl.pallas_call(
        kernel,
        out_shape=shapes,
        grid_spec=pltpu.PrefetchScalarGridSpec(
            num_scalar_prefetch=1, grid=(1,), in_specs=in_specs, out_specs=out_specs
        ),
        cost_estimate=TINY,
    )(ids, *stacks)


def fdot(former, latter, dims=((1,), (0,))):
    return lax.dot_general(former, latter, (dims, ((), ())), preferred_element_type=jnp.float32)


def turn(values, cosine, sine):
    half = values.shape[1] // 2
    front, back = values[:, :half], values[:, half:]
    return jnp.concatenate(
        [front * cosine - back * sine, back * cosine + front * sine], axis=1
    )


def project_heads(rows, weight, inner, expand, cosine, sine, queries):
    count, depth = rows.shape
    kinds = queries + 2

    def kernel(rows_ref, weight_ref, inner_ref, expand_ref, cosine_ref, sine_ref, out_ref):
        kind = pl.program_id(0) % kinds
        values = fdot(rows_ref[...], weight_ref[...]) + fdot(inner_ref[...], expand_ref[...])

        @pl.when(kind == kinds - 1)
        def _():
            out_ref[...] = low(values)

        @pl.when(kind < kinds - 1)
        def _():
            scale = jnp.where(kind < queries, HEAD_WIDTH ** (-0.5), 1.0)
            out_ref[...] = low(turn(values, cosine_ref[...], sine_ref[...]) * scale)

    whole = lambda array: pl.BlockSpec(array.shape, lambda j: (0, 0))
    return pl.pallas_call(
        kernel,
        out_shape=jax.ShapeDtypeStruct((count, weight.shape[1]), jnp.bfloat16),
        grid=(weight.shape[1] // HEAD_WIDTH,),
        in_specs=[
            whole(rows),
            pl.BlockSpec((depth, HEAD_WIDTH), lambda j: (0, j)),
            whole(inner),
            pl.BlockSpec((expand.shape[0], HEAD_WIDTH), lambda j: (0, j)),
            whole(cosine),
            whole(sine),
        ],
        out_specs=pl.BlockSpec((count, HEAD_WIDTH), lambda j: (0, j)),
        compiler_params=pltpu.CompilerParams(vmem_limit_bytes=40 << 20),
        cost_estimate=TINY,
    )(rows, weight, inner, expand, cosine, sine)


def soft_scores(query, keys, keep):
    bounded = jnp.tanh(fdot(query, keys, ((1,), (1,))) * (1.0 / 50.0))
    masked = jnp.where(keep, 50.0 * bounded, -1e30)
    exponent = jnp.exp(masked - jnp.max(masked, axis=1, keepdims=True))
    return bounded, exponent / jnp.sum(exponent, axis=1, keepdims=True)


def attend(projected, received, visible, queries):
    count = projected.shape[0]
    wide, pair = (queries + 2) * HEAD_WIDTH, 2 * HEAD_WIDTH

    def kernel(mine_ref, got_ref, visible_ref, out_ref):
        first = queries * HEAD_WIDTH
        mine = mine_ref[:, first:]
        got = got_ref[...]
        keys = jnp.concatenate([mine[:, :HEAD_WIDTH], got[:, :HEAD_WIDTH]])
        values = jnp.concatenate([mine[:, HEAD_WIDTH:], got[:, HEAD_WIDTH:]])
        keep = visible_ref[...] > 0
        for h in range(queries):
            columns = slice(h * HEAD_WIDTH, (h + 1) * HEAD_WIDTH)
            _, probs = soft_scores(mine_ref[:, columns], keys, keep)
            out_ref[:, columns] = low(fdot(low(probs), values))

    return pl.pallas_call(
        kernel,
        out_shape=jax.ShapeDtypeStruct((count, 2 * queries * HEAD_WIDTH), jnp.bfloat16),
        grid=(2,),
        in_specs=[
            pl.BlockSpec((count, wide), lambda j: (0, j)),
            pl.BlockSpec((count, pair), lambda j: (0, j)),
            pl.BlockSpec(visible.shape, lambda j: (0, 0)),
        ],
        out_specs=pl.BlockSpec((count, queries * HEAD_WIDTH), lambda j: (0, j)),
        compiler_params=pltpu.CompilerParams(vmem_limit_bytes=40 << 20),
        cost_estimate=TINY,
    )(projected, received, visible)


def attend_back(projected, received, visible, grad_mixed, cosine, sine, queries):
    count = projected.shape[0]
    wide, pair = (queries + 2) * HEAD_WIDTH, 2 * HEAD_WIDTH

    def kernel(mine_ref, got_ref, visible_ref, grad_ref, cos_ref, sin_ref, query_ref, pair_ref):
        first = queries * HEAD_WIDTH
        mine = mine_ref[:, first:]
        got = got_ref[...]
        keys = jnp.concatenate([mine[:, :HEAD_WIDTH], got[:, :HEAD_WIDTH]])
        values = jnp.concatenate([mine[:, HEAD_WIDTH:], got[:, HEAD_WIDTH:]])
        keep = visible_ref[...] > 0
        grad_keys, grad_values = 0.0, 0.0
        for h in range(queries):
            columns = slice(h * HEAD_WIDTH, (h + 1) * HEAD_WIDTH)
            query, grad = mine_ref[:, columns], grad_ref[:, columns]
            bounded, probs = soft_scores(query, keys, keep)
            grad_values = grad_values + fdot(low(probs), grad, ((0,), (0,)))
            grad_probs = fdot(grad, values, ((1,), (1,)))
            inner = jnp.sum(probs * grad_probs, axis=1, keepdims=True)
            grad_scores = low(probs * (grad_probs - inner) * (1.0 - bounded * bounded))
            grad_query = fdot(grad_scores, keys) * HEAD_WIDTH ** (-0.5)
            query_ref[:, columns] = low(turn(grad_query, cos_ref[...], -sin_ref[...]))
            grad_keys = grad_keys + fdot(grad_scores, query, ((0,), (0,)))
        pair_ref[:, :HEAD_WIDTH] = grad_keys
        pair_ref[:, HEAD_WIDTH:] = grad_values

    whole = lambda array: pl.BlockSpec(array.shape, lambda j: (0, 0))
    return pl.pallas_call(
        kernel,
        out_shape=[
            jax.ShapeDtypeStruct((count, 2 * queries * HEAD_WIDTH), jnp.bfloat16),
            jax.ShapeDtypeStruct((2 * count, 2 * pair), jnp.float32),
        ],
        grid=(2,),
        in_specs=[
            pl.BlockSpec((count, wide), lambda j: (0, j)),
            pl.BlockSpec((count, pair), lambda j: (0, j)),
            whole(visible),
            pl.BlockSpec((count, queries * HEAD_WIDTH), lambda j: (0, j)),
            whole(cosine),
            whole(sine),
        ],
        out_specs=[
            pl.BlockSpec((count, queries * HEAD_WIDTH), lambda j: (0, j)),
            pl.BlockSpec((2 * count, pair), lambda j: (0, j)),
        ],
        compiler_params=pltpu.CompilerParams(vmem_limit_bytes=48 << 20),
        cost_estimate=TINY,
    )(projected, received, visible, grad_mixed, cosine, sine)


GELU_A = math.sqrt(2.0 / math.pi)
GELU_B = 0.044715


def gate_and_up(rows, w_gate, w_up, inner, e_gate, e_up):
    count, depth = rows.shape
    units, tile = w_gate.shape[1], 256
    half = inner.shape[1] // 2
    step = count // 4

    def kernel(rows_ref, gate_w, up_w, inner_ref, gate_e, up_e, hidden_ref, gate_ref, up_ref):
        for i in range(4):
            here = slice(i * step, (i + 1) * step)
            inner_rows = inner_ref[here]
            gate = fdot(rows_ref[here], gate_w[...]) + fdot(inner_rows[:, :half], gate_e[...])
            up = fdot(rows_ref[here], up_w[...]) + fdot(inner_rows[:, half:], up_e[...])
            square = gate * gate
            bend = jnp.tanh(GELU_A * gate * (1.0 + GELU_B * square))
            half_up = 0.5 * (1.0 + bend)
            slope = half_up + 0.5 * gate * (1.0 - bend * bend) * (
                GELU_A * (1.0 + 3.0 * GELU_B * square)
            )
            bent = gate * half_up
            hidden_ref[here] = low(bent * up)
            gate_ref[here] = low(up * slope)
            up_ref[here] = low(bent)

    whole = lambda array: pl.BlockSpec(array.shape, lambda j: (0, 0))
    column = lambda array: pl.BlockSpec((array.shape[0], tile), lambda j: (0, j))
    return pl.pallas_call(
        kernel,
        out_shape=[jax.ShapeDtypeStruct((count, units), jnp.bfloat16)] * 3,
        grid=(units // tile,),
        in_specs=[whole(rows), column(w_gate), column(w_up), whole(inner), column(e_gate),
                  column(e_up)],
        out_specs=[pl.BlockSpec((count, tile), lambda j: (0, j))] * 3,
        compiler_params=pltpu.CompilerParams(vmem_limit_bytes=63 << 20),
        cost_estimate=TINY,
    )(rows, w_gate, w_up, inner, e_gate, e_up)


def square_shapes(count, depth):
    rows = count // 4
    half = rows // 2
    return [
        jax.ShapeDtypeStruct((rows, depth), jnp.float32),
        jax.ShapeDtypeStruct((half, depth), jnp.float32),
        jax.ShapeDtypeStruct((half, depth), jnp.float32),
        jax.ShapeDtypeStruct((rows, depth), jnp.bfloat16),
        jax.ShapeDtypeStruct((rows, depth), jnp.bfloat16),
    ]


def store_square(values, refs):
    rows = values.shape[0] // 4
    half = rows // 2
    mine_ref, y_ref, z_ref, send_y_ref, send_z_ref = refs
    mine_ref[...] = values[:rows]
    y_ref[...] = values[rows + half : 2 * rows]
    z_ref[...] = values[2 * rows : 2 * rows + half]
    send_y_ref[:half] = low(values[rows : rows + half])
    send_y_ref[half:] = low(values[3 * rows : 3 * rows + half])
    send_z_ref[:half] = low(values[2 * rows + half : 3 * rows])
    send_z_ref[half:] = low(values[3 * rows + half :])


def down_last(first, hidden, w_down_t):
    count, depth = first.shape
    tile = depth // 3

    def kernel(first_ref, hidden_ref, weight_ref, *out_refs):
        store_square(
            first_ref[...] + fdot(hidden_ref[...], weight_ref[...], ((1,), (1,))), out_refs
        )

    shapes = square_shapes(count, depth)
    return pl.pallas_call(
        kernel,
        out_shape=shapes,
        grid=(depth // tile,),
        in_specs=[
            pl.BlockSpec((count, tile), lambda j: (0, j)),
            pl.BlockSpec(hidden.shape, lambda j: (0, 0)),
            pl.BlockSpec((tile, w_down_t.shape[1]), lambda j: (j, 0)),
        ],
        out_specs=[pl.BlockSpec((shape.shape[0], tile), lambda j: (0, j)) for shape in shapes],
        compiler_params=pltpu.CompilerParams(vmem_limit_bytes=48 << 20),
        cost_estimate=TINY,
    )(first, hidden, w_down_t)


def feed_forward_back(grad_rows, e_down, s_gate_up, keep, chunks):
    count, depth = grad_rows.shape
    tiles = [chunk[0].shape[1] // 2 for chunk in chunks]
    columns = depth // 3
    steps = []
    for i, chunk in enumerate(chunks):
        steps += [(i, j) for j in range(chunk[0].shape[1] // tiles[i])]
    total = len(steps)
    firsts = [steps.index((i, 0)) for i in range(len(chunks))]
    counts = [chunk[0].shape[1] // tiles[i] for i, chunk in enumerate(chunks)]
    starts = [sum(chunk[0].shape[1] for chunk in chunks[:i]) for i in range(len(chunks))]
    width = sum(chunk[0].shape[1] for chunk in chunks)
    twice = e_down.shape[0]
    each = len(chunks[0])
    parts = square_shapes(count, depth)

    def kernel(grad_ref, e_down_ref, s_ref, keep_ref, *refs):
        ins = refs[: each * len(chunks)]
        out_refs = refs[each * len(chunks) :]
        rows_refs = out_refs[: len(parts)]
        inner_grad_ref, inner_ref, gates_ref, ups_ref, sums_ref = out_refs[len(parts) :]
        step = pl.program_id(0)

        @pl.when(step == 0)
        def _():
            inner_grad = fdot(grad_ref[...], e_down_ref[...], ((1,), (1,)))
            inner_grad_ref[...] = low(inner_grad * keep_ref[:, :twice])
            sums_ref[...] = jnp.zeros_like(sums_ref)

        def one(i, down, gate_in, up_in, s_down, e_gate, e_up, gate_w, up_w):
            place = pl.ds(pl.multiple_of(starts[i] + (step - firsts[i]) * tiles[i], 128), tiles[i])
            grad = fdot(grad_ref[...], down[...]) + fdot(inner_grad_ref[...], s_down[...])
            grad_gate = low(grad * gate_in[...].astype(jnp.float32))
            grad_up = low(grad * up_in[...].astype(jnp.float32))
            gates_ref[:, place] = grad_gate
            ups_ref[:, place] = grad_up
            first = fdot(grad_gate, e_gate[...], ((1,), (1,)))
            second = fdot(grad_up, e_up[...], ((1,), (1,)))
            sums_ref[:, :twice] += first
            sums_ref[:, twice:] += second

        for i in range(len(chunks)):
            within = (step >= firsts[i]) & (step < firsts[i] + counts[i])
            pl.when(within)(functools.partial(one, i, *ins[i * each : (i + 1) * each]))

        @pl.when(step == total - 1)
        def _():
            inner_ref[...] = low(sums_ref[...] * keep_ref[...])

        @pl.when(step >= total)
        def _():
            rows = fdot(inner_ref[...], s_ref[...])
            for i, chunk in enumerate(chunks):
                gate_w, up_w = ins[(i + 1) * each - 2 : (i + 1) * each]
                place = slice(starts[i], starts[i] + chunk[0].shape[1])
                rows += fdot(gates_ref[:, place], gate_w[...], ((1,), (1,)))
                rows += fdot(ups_ref[:, place], up_w[...], ((1,), (1,)))
            store_square(rows, rows_refs)

    once = pl.Buffered(1)
    whole = lambda array: pl.BlockSpec(array.shape, lambda j: (0, 0), pipeline_mode=once)
    second = lambda j: jnp.clip(j - total, 0, depth // columns - 1)

    def column(i, array):
        return pl.BlockSpec(
            (array.shape[0], tiles[i]),
            lambda j: (0, jnp.clip(j - firsts[i], 0, counts[i] - 1)),
        )

    def specs(i, chunk):
        return [column(i, array) for array in chunk[:-2]] + [
            pl.BlockSpec((columns, array.shape[1]), lambda j: (second(j), 0))
            for array in chunk[-2:]
        ]

    return pl.pallas_call(
        kernel,
        out_shape=parts
        + [
            jax.ShapeDtypeStruct((count, twice), jnp.bfloat16),
            jax.ShapeDtypeStruct((count, 2 * twice), jnp.bfloat16),
            jax.ShapeDtypeStruct((count, width), jnp.bfloat16),
            jax.ShapeDtypeStruct((count, width), jnp.bfloat16),
        ],
        grid=(total + depth // columns,),
        in_specs=[
            whole(grad_rows),
            whole(e_down),
            pl.BlockSpec((s_gate_up.shape[0], columns), lambda j: (0, second(j))),
            whole(keep),
        ]
        + [spec for i, chunk in enumerate(chunks) for spec in specs(i, chunk)],
        out_specs=[
            pl.BlockSpec((part.shape[0], columns), lambda j: (0, second(j))) for part in parts
        ]
        + [
            pl.BlockSpec((count, twice), lambda j: (0, 0)),
            pl.BlockSpec((count, 2 * twice), lambda j: (0, 0)),
            pl.BlockSpec((count, width), lambda j: (0, 0), pipeline_mode=once),
            pl.BlockSpec((count, width), lambda j: (0, 0), pipeline_mode=once),
        ],
        scratch_shapes=[pltpu.VMEM((count, 2 * twice), jnp.float32)],
        compiler_params=pltpu.CompilerParams(vmem_limit_bytes=63 << 20),
        cost_estimate=TINY,
    )(grad_rows, e_down, s_gate_up, keep, *[array for chunk in chunks for array in chunk])


def scatter_pair(part):
    rows = part.shape[0] // 2
    got = flip(low(part[rows:]), "tensor", 2)
    return part[:rows] + got.astype(jnp.float32)


def gather_pair(own):
    return jnp.concatenate([own, flip(own, "tensor", 2)])


def gather_square(own):
    half = own.shape[0] // 2
    from_y = flip(own, "tensor", 2)
    from_z = flip(own, "dp", 2)
    send_z, send_y = settle(from_y[:half], from_z[half:])
    diagonal = [flip(send_z, "dp", 2), flip(send_y, "tensor", 2)]
    return jnp.concatenate([own, from_y, from_z] + diagonal)


def sum_by_adapter(ids, gathered, shared, widths):
    count, rows, columns = gathered.shape
    cuts = [0, shared] + [shared + sum(widths[: i + 1]) for i in range(len(widths))]

    def kernel(ids_ref, gathered_ref, *refs):
        out_refs, total_ref = refs[:-1], refs[-1]
        total_refs = [total_ref] + list(out_refs[1:])
        for ref in total_refs:
            ref[...] = jnp.zeros_like(ref)
        for entry in range(count):
            adapter = ids_ref[entry]
            for i, ref in enumerate(total_refs):
                ref[adapter] += gathered_ref[entry, :, cuts[i] : cuts[i + 1]].astype(jnp.float32)
        out_refs[0][...] = low(total_ref[...])

    shapes = [jax.ShapeDtypeStruct((ADAPTERS, rows, shared), jnp.bfloat16)] + [
        jax.ShapeDtypeStruct((ADAPTERS, rows, width), jnp.float32) for width in widths
    ]
    return pl.pallas_call(
        kernel,
        out_shape=shapes,
        in_specs=[
            pl.BlockSpec(memory_space=pltpu.SMEM),
            pl.BlockSpec(gathered.shape, lambda: (0, 0, 0)),
        ],
        out_specs=[pl.BlockSpec(shape.shape, lambda: (0, 0, 0)) for shape in shapes],
        scratch_shapes=[pltpu.VMEM((ADAPTERS, rows, shared), jnp.float32)],
        compiler_params=pltpu.CompilerParams(vmem_limit_bytes=40 << 20),
        cost_estimate=TINY,
    )(ids, gathered)


def sum_unit_grads(hots, gathered, kinds):
    count, rows, columns = gathered.shape
    rank = rows // kinds
    adapters = hots.shape[2]

    def kernel(hots_ref, gathered_ref, *out_refs):
        for side in range(2):
            for kind in range(kinds):
                here = slice(kind * rank, (kind + 1) * rank)

                @pl.loop(0, adapters)
                def _(adapter):
                    total = 0.0
                    for entry in range(count):
                        total += hots_ref[side, entry, adapter] * gathered_ref[
                            entry, here
                        ].astype(jnp.float32)
                    out_refs[kind][adapter, :, side * columns : (side + 1) * columns] = total

    return pl.pallas_call(
        kernel,
        out_shape=[jax.ShapeDtypeStruct((adapters, rank, 2 * columns), jnp.float32)] * kinds,
        in_specs=[
            pl.BlockSpec(memory_space=pltpu.SMEM),
            pl.BlockSpec(gathered.shape, lambda: (0, 0, 0)),
        ],
        out_specs=[pl.BlockSpec((adapters, rank, 2 * columns), lambda: (0, 0, 0))] * kinds,
        compiler_params=pltpu.CompilerParams(vmem_limit_bytes=48 << 20),
        cost_estimate=TINY,
    )(hots, gathered)


def join_halves(core, mine, other, kinds):
    adapters, rank, columns = mine.shape
    half = columns // kinds

    def kernel(core_ref, mine_ref, other_ref, *out_refs):
        swap = core_ref[0] == 1
        for kind in range(kinds):
            here = slice(kind * half, (kind + 1) * half)
            first = mine_ref[:, :, here].astype(jnp.float32)
            second = other_ref[:, :, here].astype(jnp.float32)
            out_refs[kind][:, :, :half] = jnp.where(swap, second, first)
            out_refs[kind][:, :, half:] = jnp.where(swap, first, second)

    return pl.pallas_call(
        kernel,
        out_shape=[jax.ShapeDtypeStruct((adapters, rank, 2 * half), jnp.float32)] * kinds,
        in_specs=[pl.BlockSpec(memory_space=pltpu.SMEM)]
        + [pl.BlockSpec(mine.shape, lambda: (0, 0, 0))] * 2,
        out_specs=[pl.BlockSpec((adapters, rank, 2 * half), lambda: (0, 0, 0))] * kinds,
        compiler_params=pltpu.CompilerParams(vmem_limit_bytes=48 << 20),
        cost_estimate=TINY,
    )(core, mine, other)


def square_first(parts):
    mine, to_y, to_z, send_y, send_z = parts
    return (flip(send_y, "tensor", 2), flip(send_z, "dp", 2)), (mine, to_y, to_z)


def square_last(first, rest):
    got_y, got_z = (got.astype(jnp.float32) for got in first)
    mine, to_y, to_z = rest
    half = to_y.shape[0]
    send_y, send_z = settle(low(to_y + got_z[half:]), low(to_z + got_y[half:]))
    last_y = flip(send_y, "tensor", 2).astype(jnp.float32)
    last_z = flip(send_z, "dp", 2).astype(jnp.float32)
    return jnp.concatenate(
        [mine[:half] + got_y[:half] + last_z, mine[half:] + got_z[:half] + last_y]
    )


def tree_bits(trees):
    return [1 << b for b in range(1, trees.bit_length() - 1)][::-1] + [1]


def tree_order(trees):
    bits = tree_bits(trees)
    order = [0]
    for bit in bits[-1:] + bits[:-1]:
        order += [i ^ bit for i in order]
    return order


def on_device(
    layer_input,
    cotangent,
    norm_gains,
    w_query,
    w_key,
    w_value,
    w_output,
    w_gate,
    w_up,
    w_down,
    query_shrink,
    key_shrink,
    value_shrink,
    output_shrink,
    gate_shrink,
    up_shrink,
    down_shrink,
    query_expand,
    key_expand,
    value_expand,
    output_expand,
    gate_expand,
    up_expand,
    down_expand,
    adapter_ids,
    parent_segments,
    segment_ids,
):
    trees = lax.axis_size("dp")
    columns_z = trees // 2
    my_tree = lax.axis_index("dp")
    my_z, my_x = my_tree // 2, my_tree % 2
    my_part = lax.axis_index("tensor")
    odd = my_z % 2 == 1
    norm_gain = norm_gains.astype(jnp.float32)
    place = my_x.astype(jnp.int32)[None]

    def halves(values):
        half = values.shape[-1] // 2
        return jnp.stack([values[:, :half], values[:, half:]])

    def on_core(values):
        return flip(values, "tensor", 1)

    w_qkv = jnp.concatenate([w_query, w_key, w_value], axis=1)
    cut = w_qkv.shape[0] // 2 // 16 * 16
    gate_halves, up_halves, down_halves = halves(w_gate), halves(w_up), halves(w_down.T)
    units = gate_halves.shape[2]
    first_units = (units // 128 + 1) // 2 * 128
    waiting = [
        w_qkv[None, :cut],
        w_qkv[None, cut:],
        w_output.T[None],
        gate_halves[:, :, first_units:],
        up_halves[:, :, first_units:],
        gate_halves[:, :, :first_units],
        up_halves[:, :, :first_units],
        down_halves[:, :, :first_units],
        down_halves[:, :, first_units:],
    ]
    waiting = [
        jnp.concatenate([blocks] * (columns_z // blocks.shape[0])) for blocks in waiting
    ]
    count = len(waiting)
    near, cross = {}, {}

    near_core, cross_core = {}, {}

    def transfers(step):
        if step < count:
            near[step] = along_z(waiting[step], columns_z)
        if 0 <= step - 1 < count:
            cross[step - 1] = flip(near[step - 1], "dp", 1)
            near_core[step - 1] = on_core(near[step - 1])
        if 0 <= step - 2 < count:
            cross_core[step - 2] = on_core(cross[step - 2])

    def close(step, *values):
        moved = [
            (store, key)
            for store, key in (
                (near, step),
                (cross, step - 1),
                (near_core, step - 1),
                (cross_core, step - 2),
            )
            if key in store
        ]
        following = [waiting[step + 1]] if step + 1 < count else []
        moved_values, following, values = settle(
            [store[key] for store, key in moved], following, values
        )
        for (store, key), value in zip(moved, moved_values):
            store[key] = value
        if following:
            waiting[step + 1] = following[0]
        return values

    def matrix(*keys):
        stores = (near, cross, near_core, cross_core)
        return assemble([[store[key] for store in stores] for key in keys], place)

    transfers(0)
    own_rows = layer_input.astype(jnp.float32)
    normed = low(rms_scale(own_rows, norm_gain[0]))
    near_ids = flip(adapter_ids, "dp", 2)
    labels = jnp.arange(ADAPTERS, dtype=jnp.int32)
    order = jnp.stack([my_part, my_part ^ 2, my_part ^ 1, my_part ^ 3]).astype(jnp.int32)
    visible, cos_rows, sin_rows = tree_tables(segment_ids, parent_segments[0], order)
    row_count = 2 * normed.shape[0]
    visible = low(visible[:row_count])
    cos_rows, sin_rows = cos_rows[:row_count], sin_rows[:row_count]
    ids_parts = [adapter_ids, flip(adapter_ids, "dp", 1)]
    normed, near_ids, visible, cos_rows, sin_rows, ids_parts = close(
        0, normed, near_ids, visible, cos_rows, sin_rows, ids_parts
    )

    transfers(1)
    normed_all = gather_pair(normed)
    picks = jnp.concatenate([adapter_ids, near_ids, (my_z % 2).astype(jnp.int32)[None]])
    normed_all, picks = settle(normed_all, picks)
    picked = pick_adapters(
        picks,
        [
            (stack, False)
            for stack in (
                query_shrink,
                key_shrink,
                value_shrink,
                query_expand,
                key_expand,
                value_expand,
                output_shrink,
                output_expand,
            )
        ]
        + [
            (stack, near_tree)
            for stack in (gate_shrink, up_shrink, down_expand)
            for near_tree in (False, True)
        ],
        [
            (stack, near_tree)
            for stack in (gate_expand, up_expand, down_shrink)
            for near_tree in (False, True)
        ],
    )
    s_qkv = jnp.concatenate(picked[0:3])
    e_parts = picked[3:6]
    rank = e_parts[0].shape[0]
    widths = [part.shape[1] for part in e_parts]
    attn_mine = jnp.concatenate(picked[3:7], axis=1)
    e_output = picked[7]
    s_gate_up = jnp.concatenate(picked[8:12])
    e_down = jnp.concatenate(picked[12:14])
    ffn_mine = jnp.concatenate(picked[14:20])
    for bit in tree_bits(trees)[:-2]:
        tree_ids = jnp.concatenate(ids_parts)
        ids_parts = [tree_ids, flip(tree_ids, "dp", bit)]
    normed_all, attn_mine, e_output, s_gate_up, e_down, ffn_mine, s_qkv, ids_parts = close(
        1, normed_all, attn_mine, e_output, s_gate_up, e_down, ffn_mine, s_qkv, ids_parts
    )

    transfers(2)
    attn_other = on_core(attn_mine)
    ffn_other = on_core(ffn_mine)
    inner_qkv = low(times_rows(normed_all, s_qkv))
    tree_ids = jnp.concatenate(ids_parts)
    ids_parts = [tree_ids, flip(tree_ids, "dp", 2)]
    attn_other, ffn_other, inner_qkv, ids_parts = close(
        2, attn_other, ffn_other, inner_qkv, ids_parts
    )
    tree_ids = jnp.concatenate(ids_parts)

    transfers(3)
    heads_here = sum(widths)
    queries = widths[0] // HEAD_WIDTH
    e_mine = attn_mine[:, :heads_here]
    e_other = attn_other[:, :heads_here]
    s_output = beside(attn_mine[:, heads_here:], attn_other[:, heads_here:])
    starts = [sum(widths[:i]) for i in range(4)]
    column_kind = sum(
        (jnp.arange(heads_here, dtype=jnp.int32) >= start).astype(jnp.int32)
        for start in starts[1:3]
    )
    kind_mask = (
        jnp.arange(3 * rank, dtype=jnp.int32)[:, None] // rank
        == jnp.concatenate([column_kind, column_kind])[None, :]
    )
    e_qkv = low(jnp.where(kind_mask, jnp.tile(beside(e_mine, e_other), (3, 1)), 0.0))
    units_a = beside(ffn_mine[:, :first_units], ffn_other[:, :first_units])
    units_b = beside(ffn_mine[:, first_units:], ffn_other[:, first_units:])
    adapters_ab = [
        [block[i * 2 * rank : (i + 1) * 2 * rank] for i in range(3)] for block in (units_a, units_b)
    ]
    e_qkv, s_output, adapters_ab = close(3, e_qkv, s_output, adapters_ab)

    transfers(4)
    full_qkv = matrix(0, 1)
    projected = project_heads(
        normed_all, full_qkv, inner_qkv, e_qkv, cos_rows, sin_rows, queries
    )
    received = on_core(
        beside(projected[:, heads_here + starts[1] :], projected[:, starts[1] : heads_here])
    )
    full_qkv, projected, received = close(4, full_qkv, projected, received)

    transfers(5)
    full_out_t = matrix(2)
    mixed_heads = attend(projected, received, visible, queries)
    inner_output = low(times_rows(mixed_heads, s_output))
    attn_part = times_rows(mixed_heads, full_out_t) + product(inner_output, e_output)
    attended = scatter_pair(attn_part)
    mixed_heads, full_out_t, inner_output, attended = close(
        5, mixed_heads, full_out_t, inner_output, attended
    )

    transfers(6)
    full_gate_b = matrix(3)
    residual = own_rows + rms_scale(attended, norm_gain[1])
    normed_ffn = low(rms_scale(residual, norm_gain[2]))
    normed_y = flip(normed_ffn, "tensor", 2)
    half_rows = normed_ffn.shape[0] // 2
    normed_z_first = flip(normed_ffn[:half_rows], "dp", 2)
    residual, normed_ffn, normed_y, normed_z_first, full_gate_b = close(
        6, residual, normed_ffn, normed_y, normed_z_first, full_gate_b
    )

    transfers(7)
    normed_z_last = flip(normed_ffn[half_rows:], "dp", 2)
    full_up_b = matrix(4)
    normed_zy_first = flip(normed_z_first, "tensor", 2)
    normed_z_last, normed_zy_first, full_up_b = close(
        7, normed_z_last, normed_zy_first, full_up_b
    )

    transfers(8)
    normed_zy_last = flip(normed_z_last, "tensor", 2)
    full_gate_a = matrix(5)
    ffn_rows = jnp.concatenate(
        [normed_ffn, normed_y, normed_z_first, normed_z_last, normed_zy_first, normed_zy_last]
    )
    block_rows = residual.shape[0]
    row_block = jnp.arange(4 * block_rows, dtype=jnp.int32) // block_rows
    row_near = (row_block // 2)[:, None]
    rank_near = (jnp.arange(4 * rank, dtype=jnp.int32) // rank % 2)[None, :]
    keep_four = (row_near == rank_near).astype(jnp.float32)
    keep_two = keep_four[:, : 2 * rank]
    inner_gate_up = low(keep_four * times_rows(ffn_rows, s_gate_up))
    chunk_b = gate_and_up(
        ffn_rows, full_gate_b, full_up_b, inner_gate_up, adapters_ab[1][0], adapters_ab[1][1]
    )
    ffn_rows, inner_gate_up, chunk_b, full_gate_a = close(
        8, ffn_rows, inner_gate_up, chunk_b, full_gate_a
    )

    transfers(9)
    full_up_a = matrix(6)
    chunk_a = gate_and_up(
        ffn_rows, full_gate_a, full_up_a, inner_gate_up, adapters_ab[0][0], adapters_ab[0][1]
    )
    chunk_out = [chunk_a, chunk_b]
    hidden = [parts[0] for parts in chunk_out]
    inner_down = low(
        keep_two
        * (times_rows(hidden[0], adapters_ab[0][2]) + times_rows(hidden[1], adapters_ab[1][2]))
    )
    full_down_a = matrix(7)
    ffn_first = times_rows(hidden[0], full_down_a) + product(inner_down, e_down)
    chunk_out, inner_down, ffn_first = close(9, chunk_out, inner_down, ffn_first)
    hidden = [parts[0] for parts in chunk_out]

    cross_core[8] = on_core(cross[8])
    full_down_b = matrix(8)
    ffn_out = square_last(*square_first(down_last(ffn_first, hidden[1], full_down_b)))
    layer_output = low(residual + rms_scale(ffn_out, norm_gain[3]))

    grad_out = cotangent.astype(jnp.float32)
    grad_ffn = gather_square(low(rms_back(ffn_out, norm_gain[3], grad_out)))
    *grad_normed_parts, grad_inner_down, grad_inner_gate_up, grad_gate, grad_up = feed_forward_back(
        grad_ffn,
        e_down,
        s_gate_up,
        keep_four,
        [
            (full_down, *parts[1:], adapters[2], adapters[0], adapters[1], full_gate, full_up)
            for full_down, full_gate, full_up, parts, adapters in (
                (full_down_a, full_gate_a, full_up_a, chunk_out[0], adapters_ab[0]),
                (full_down_b, full_gate_b, full_up_b, chunk_out[1], adapters_ab[1]),
            )
        ],
    )
    def from_other_core(mine, other):
        return low(mine + on_core(low(other)).astype(jnp.float32))

    parts_first, parts_rest = square_first(grad_normed_parts)
    grad_shrink_down = jnp.concatenate(
        [over_rows(grad_inner_down, units_of) for units_of in hidden], axis=1
    )
    inner_gate, inner_up = inner_gate_up[:, : 2 * rank], inner_gate_up[:, 2 * rank :]
    grad_units = jnp.stack(
        [
            grads.reshape(2, rank, 2 * units)
            for grads in (
                over_rows(inner_gate, grad_gate),
                over_rows(inner_up, grad_up),
                grad_shrink_down,
            )
        ],
        axis=1,
    ).reshape(6 * rank, 2 * units)
    rest = units - first_units
    cuts = [0, first_units, 2 * first_units, 2 * first_units + rest, 2 * units]
    quarters = [grad_units[:, cuts[i] : cuts[i + 1]] for i in range(4)]
    mine, other = beside(quarters[0], quarters[2]), beside(quarters[1], quarters[3])
    local = from_other_core(mine, other)
    parts_first, local, grad_inner_gate_up, grad_ffn = settle(
        parts_first, local, grad_inner_gate_up, grad_ffn
    )
    local_all = jnp.stack([local, flip(local, "dp", 1)])
    grad_expand_down = over_rows(inner_down, grad_ffn)
    grad_shrink_gate_up = over_rows(grad_inner_gate_up, ffn_rows)
    grad_normed_ffn = square_last(parts_first, parts_rest)
    grad_resid = grad_out + rms_back(residual, norm_gain[2], grad_normed_ffn)
    grad_attn_mine = low(rms_back(attended, norm_gain[1], grad_resid))
    shared = jnp.concatenate([grad_shrink_gate_up, grad_expand_down]).reshape(3, 2, rank, -1)
    grad_attn_mine, grad_resid, local_all, shared = settle(
        grad_attn_mine, grad_resid, local_all, shared
    )

    def core_half(blocks):
        half = blocks.shape[-1] // 2
        kept = jnp.where(my_part % 2 == 1, blocks[..., half:], blocks[..., :half])
        return jnp.concatenate([low(block) for block in kept], axis=1)

    def with_bit(values, bit):
        return jnp.concatenate([values, flip(values, "dp", bit)])

    grad_attn = gather_pair(grad_attn_mine)
    shared_near = flip(low(shared[:, 1]), "dp", 2)
    bits = tree_bits(trees)
    for bit in bits[:-2]:
        local_all = with_bit(local_all, bit)
    grad_attn, local_all, shared, shared_near = settle(grad_attn, local_all, shared, shared_near)

    local_near = flip(local_all, "dp", bits[-2])
    grad_inner_output = low(times_rows(grad_attn, e_output))
    grad_mixed = low(product(grad_attn, full_out_t) + product(grad_inner_output, s_output))
    grad_queries, grad_pairs = attend_back(
        projected, received, visible, grad_mixed, cos_rows, sin_rows, queries
    )
    pair = 2 * HEAD_WIDTH
    to_core = low(beside(grad_pairs[row_count:, pair:], grad_pairs[row_count:, :pair]))
    from_core = on_core(to_core)
    shared = shared[:, 0] + shared_near.astype(jnp.float32)
    shared = shared + on_core(low(shared)).astype(jnp.float32)
    shared = shared + flip(low(shared), "tensor", 2).astype(jnp.float32)
    shared_mine = core_half(shared)
    from_core, grad_queries, grad_pairs, shared_mine = settle(
        from_core, grad_queries, grad_pairs, shared_mine
    )

    shared_all = shared_mine[None]
    for bit in bits[:-2]:
        shared_all = with_bit(shared_all, bit)
    grad_expand_output = over_rows(inner_output, grad_attn)
    grad_shrink_output = over_rows(grad_inner_output, mixed_heads)
    grad_pairs = grad_pairs[:row_count] + from_core.astype(jnp.float32)
    grad_sides = []
    for side in range(2):
        keys_values = grad_pairs[:, side * pair : (side + 1) * pair]
        grad_sides += [
            grad_queries[:, side * widths[0] : (side + 1) * widths[0]],
            low(turn(keys_values[:, :HEAD_WIDTH], cos_rows, -sin_rows)),
            low(keys_values[:, HEAD_WIDTH:]),
        ]
    grad_qkv = jnp.concatenate(grad_sides, axis=1)
    grad_inner_qkv = low(times_rows(grad_qkv, e_qkv))
    grad_expand_qkv = over_rows(inner_qkv, grad_qkv)
    last = jnp.concatenate(
        [over_rows(grad_inner_qkv, normed_all), grad_expand_output]
    ).reshape(4, rank, -1)
    pieces = []
    for side in range(2):
        for i in range(3):
            first = side * heads_here + starts[i]
            pieces.append(grad_expand_qkv[i * rank : (i + 1) * rank, first : first + widths[i]])
        pieces.append(grad_shrink_output[:, side * widths[0] : (side + 1) * widths[0]])
    local_attn = from_other_core(
        jnp.concatenate(pieces[:4], axis=1), jnp.concatenate(pieces[4:], axis=1)
    )
    last = last + on_core(low(last)).astype(jnp.float32)
    last, local_attn, grad_qkv, grad_inner_qkv, shared_all = settle(
        last, local_attn, grad_qkv, grad_inner_qkv, shared_all
    )

    last_y = flip(low(last), "tensor", 2)
    shared_all = with_bit(shared_all, bits[-2])
    part = times_rows(grad_qkv, full_qkv) + product(grad_inner_qkv, s_qkv)
    last_y, part, shared_all, local_near = settle(last_y, part, shared_all, local_near)

    last_mine = beside(core_half(last + last_y.astype(jnp.float32)), local_attn)
    last_all = lax.all_to_all(
        jnp.broadcast_to(last_mine[None], (trees,) + last_mine.shape), "dp", 0, 0
    )
    from_y = flip(low(part[block_rows:]), "tensor", 2)
    shared_all = with_bit(shared_all, 1)
    from_y, shared_all = settle(from_y, shared_all)
    grad_normed = part[:block_rows] + from_y.astype(jnp.float32)
    input_grad = grad_resid + rms_back(own_rows, norm_gain[0], grad_normed)
    local_all = jnp.concatenate([local_all, local_near])

    tree_ids = tree_ids.reshape(trees)
    hot_near = (tree_ids[:, None] == labels[None, :]).astype(jnp.float32)
    distances = my_tree ^ jnp.arange(trees, dtype=jnp.int32)
    place_of = jnp.stack(
        [jnp.asarray(tree_order(trees).index(j), jnp.int32) for j in range(trees)]
    )
    at = jnp.sum(
        jnp.where(
            distances[:, None] == jnp.arange(trees, dtype=jnp.int32)[None, :], place_of[None, :], 0
        ),
        axis=1,
    )
    ids_trees = jnp.sum(
        jnp.where(
            at[:, None] == jnp.arange(trees, dtype=jnp.int32)[None, :], tree_ids[None, :], 0
        ),
        axis=1,
    )
    order_local = [0, 1]
    for bit in bits[:-1]:
        order_local += [i ^ bit for i in order_local]
    ids_at = {tree: i for i, tree in enumerate(tree_order(trees))}
    hots, crossing = [], []
    for j in order_local:
        for near_tree in range(2):
            hots.append(hot_near[ids_at[j ^ (2 * near_tree)]])
            crossing.append((j // 2) % 2)
    hots = jnp.stack(hots)
    parity = jnp.asarray(crossing, jnp.int32) ^ (my_z % 2).astype(jnp.int32)
    local_all = local_all.reshape(2 * trees, 3 * rank, units)
    hots = jnp.stack([jnp.where(parity[:, None] == side, hots, 0.0) for side in range(2)])
    ids_shared = tree_ids.reshape(2, trees // 4, 2).transpose(2, 0, 1).reshape(trees)
    out_expand_gate, out_expand_up, out_shrink_down = sum_unit_grads(hots, local_all, 3)
    core = (my_part % 2).astype(jnp.int32)[None]
    depth_half = s_qkv.shape[1] // 2
    (sums,) = sum_by_adapter(ids_shared, shared_all, 3 * depth_half, [])
    out_shrink_gate, out_shrink_up, out_expand_down = join_halves(core, sums, on_core(sums), 3)
    (last_all, input_grad, out_expand_gate, out_expand_up, out_shrink_down, out_shrink_gate,
     out_shrink_up, out_expand_down) = settle(
        last_all, input_grad, out_expand_gate, out_expand_up, out_shrink_down, out_shrink_gate,
        out_shrink_up, out_expand_down,
    )
    sums, out_expand_query, out_expand_key, out_expand_value, out_shrink_output = sum_by_adapter(
        ids_trees, last_all, 4 * depth_half, widths + widths[:1]
    )
    out_shrink_query, out_shrink_key, out_shrink_value, out_expand_output = join_halves(
        core, sums, on_core(sums), 4
    )
    return (
        layer_output,
        input_grad,
        out_shrink_query,
        out_shrink_key,
        out_shrink_value,
        out_shrink_output,
        out_shrink_gate,
        out_shrink_up,
        out_shrink_down,
        out_expand_query,
        out_expand_key,
        out_expand_value,
        out_expand_output,
        out_expand_gate,
        out_expand_up,
        out_expand_down,
    )


def solution(mesh):
    placed = (
        P(("dp", "tensor"), None),
        P(("dp", "tensor"), None),
        P(),
        P("dp", "tensor"),
        P("dp", "tensor"),
        P("dp", "tensor"),
        P("tensor", "dp"),
        P("dp", "tensor"),
        P("dp", "tensor"),
        P("tensor", "dp"),
        P(),
        P(),
        P(),
        P(None, None, "tensor"),
        P(),
        P(),
        P(None, None, "tensor"),
        P(None, None, "tensor"),
        P(None, None, "tensor"),
        P(None, None, "tensor"),
        P(),
        P(None, None, "tensor"),
        P(None, None, "tensor"),
        P(),
        P("dp"),
        P("dp", None),
        P("dp"),
    )
    return jax.shard_map(
        on_device,
        mesh=mesh,
        in_specs=placed,
        out_specs=(
            P(("dp", "tensor"), None),
            P(("dp", "tensor"), None),
            P(),
            P(),
            P(),
            P(None, None, "tensor"),
            P(),
            P(),
            P(None, None, "tensor"),
            P(None, None, "tensor"),
            P(None, None, "tensor"),
            P(None, None, "tensor"),
            P(),
            P(None, None, "tensor"),
            P(None, None, "tensor"),
            P(),
        ),
        check_vma=False,
    )
```

```python
import functools
import math

import jax
import jax.numpy as jnp
from jax import lax
from jax.experimental import pallas as pl
from jax.experimental.pallas import tpu as pltpu
from jax.sharding import PartitionSpec as P

HEAD_WIDTH = 256
ADAPTERS = 8
TINY = pl.CostEstimate(flops=1, transcendentals=0, bytes_accessed=1)


def rms_scale(value_rows, gain_row):
    inverse = lax.rsqrt(jnp.mean(value_rows * value_rows, axis=-1, keepdims=True) + 1e-06)
    return value_rows * inverse * gain_row


def rms_back(value_rows, gain_row, upstream):
    inverse = lax.rsqrt(jnp.mean(value_rows * value_rows, axis=-1, keepdims=True) + 1e-06)
    scaled = gain_row * upstream
    return inverse * scaled - value_rows * (inverse * inverse * inverse) * jnp.mean(
        value_rows * scaled, axis=-1, keepdims=True
    )


def pick_from(lookup, indices, labels):
    return jnp.sum(jnp.where(indices[:, None] == labels[None, :], lookup[None, :], 0), axis=1)


def tree_tables(segments, parents, order):
    count_seg = parents.shape[0]
    sequence_length = segments.shape[0]
    blocks = order.shape[0]
    labels = jnp.arange(count_seg, dtype=jnp.int32)
    ordered_places = jnp.arange(sequence_length, dtype=jnp.int32)
    member = segments[None, :] == labels[:, None]
    starts = jnp.min(jnp.where(member, ordered_places[None, :], sequence_length), axis=1)
    counts = jnp.sum(member.astype(jnp.int32), axis=1)
    grands = pick_from(parents, parents, labels)
    offsets = jnp.where(parents != labels, pick_from(counts, parents, labels), 0) + jnp.where(
        grands != parents, pick_from(counts, grands, labels), 0
    )
    block_rows = sequence_length // blocks
    chosen = order[:, None] == jnp.arange(blocks, dtype=jnp.int32)[None, :]
    segments = jnp.sum(
        jnp.where(chosen[:, :, None], segments.reshape(1, blocks, block_rows), 0), axis=1
    ).reshape(sequence_length)
    places = (
        order[:, None] * block_rows + jnp.arange(block_rows, dtype=jnp.int32)[None, :]
    ).reshape(sequence_length)
    tok_start = pick_from(starts, segments, labels)
    tok_offset = pick_from(offsets, segments, labels)
    tok_parent = pick_from(parents, segments, labels)
    tok_grand = pick_from(grands, segments, labels)
    positions = (places - tok_start + tok_offset).astype(jnp.float32)
    same_seg = (segments[None, :] == segments[:, None]) & (places[None, :] <= places[:, None])
    from_parent = (segments[None, :] == tok_parent[:, None]) & (tok_parent != segments)[:, None]
    from_grand = (segments[None, :] == tok_grand[:, None]) & (tok_grand != tok_parent)[:, None]
    visible = same_seg | from_parent | from_grand
    inv_freq = jnp.exp(
        jnp.arange(HEAD_WIDTH // 2, dtype=jnp.float32) * (-2.0 * math.log(10000.0) / HEAD_WIDTH)
    )
    angles = positions[:, None] * inv_freq[None, :]
    return (visible, jnp.cos(angles), jnp.sin(angles))


def product(former, latter):
    return jnp.dot(former, latter, preferred_element_type=jnp.float32)


def times_rows(former, latter):
    return lax.dot_general(
        former, latter, (((1,), (1,)), ((), ())), preferred_element_type=jnp.float32
    )


def over_rows(former, latter):
    return lax.dot_general(
        former, latter, (((0,), (0,)), ((), ())), preferred_element_type=jnp.float32
    )


def low(values):
    return values.astype(jnp.bfloat16)


def flip(values, axis_name, bit):
    size = lax.axis_size(axis_name)
    return lax.ppermute(values, axis_name, [(i, i ^ bit) for i in range(size)])


def settle(*groups):
    flat, tree = jax.tree.flatten(groups)
    return jax.tree.unflatten(tree, lax.optimization_barrier(flat))


def along_z(sent, columns_z):
    lines = [[2 * z + x for z in range(columns_z)] for x in range(2)]
    return lax.all_to_all(sent, "dp", 0, 0, axis_index_groups=lines)


def assemble(pieces, place):
    columns_z, _, columns = pieces[0][0].shape
    heights = [parts[0].shape[1] for parts in pieces]
    rows = sum(heights)

    def kernel(place_ref, *refs):
        out_ref = refs[-1]
        my_x = place_ref[0]
        for i, height in enumerate(heights):
            mine_ref, cross_ref, core_ref, core_cross_ref = refs[4 * i : 4 * i + 4]
            here = pl.ds(sum(heights[:i]), height)
            out_ref[my_x, here, :columns] = mine_ref[0]
            out_ref[my_x, here, columns:] = core_ref[0]
            out_ref[1 - my_x, here, :columns] = cross_ref[0]
            out_ref[1 - my_x, here, columns:] = core_cross_ref[0]

    out = pl.pallas_call(
        kernel,
        out_shape=jax.ShapeDtypeStruct((2 * columns_z, rows, 2 * columns), jnp.bfloat16),
        grid_spec=pltpu.PrefetchScalarGridSpec(
            num_scalar_prefetch=1,
            grid=(columns_z,),
            in_specs=[
                pl.BlockSpec((1, height, columns), lambda k, place_ref: (k, 0, 0))
                for height in heights
                for _ in range(4)
            ],
            out_specs=pl.BlockSpec((2, rows, 2 * columns), lambda k, place_ref: (k, 0, 0)),
        ),
        compiler_params=pltpu.CompilerParams(vmem_limit_bytes=32 << 20),
        cost_estimate=pl.CostEstimate(
            flops=0, transcendentals=0, bytes_accessed=16 * columns_z * rows * columns
        ),
    )(place, *[part for parts in pieces for part in parts])
    return out.reshape(2 * columns_z * rows, 2 * columns)


def beside(first, second):
    return jnp.concatenate([first, second], axis=1)


def pick_adapters(ids, whole, halved):
    rank = whole[0][0].shape[1]

    def kernel(ids_ref, *refs):
        count = len(refs) // 2
        for i in range(count):
            refs[count + i][...] = refs[i][0]

    in_specs, out_specs, shapes, stacks = [], [], [], []
    for entries, parity in ((whole, False), (halved, True)):
        for stack, near in entries:
            columns = stack.shape[2] // (2 if parity else 1)
            in_specs.append(
                pl.BlockSpec(
                    (1, rank, columns),
                    functools.partial(
                        lambda near, parity, i, ids_ref: (
                            ids_ref[1 if near else 0],
                            0,
                            ids_ref[2] if parity else 0,
                        ),
                        near,
                        parity,
                    ),
                )
            )
            out_specs.append(pl.BlockSpec((rank, columns), lambda i, ids_ref: (0, 0)))
            shapes.append(jax.ShapeDtypeStruct((rank, columns), stack.dtype))
            stacks.append(stack)
    return pl.pallas_call(
        kernel,
        out_shape=shapes,
        grid_spec=pltpu.PrefetchScalarGridSpec(
            num_scalar_prefetch=1, grid=(1,), in_specs=in_specs, out_specs=out_specs
        ),
        cost_estimate=TINY,
    )(ids, *stacks)


def fdot(former, latter, dims=((1,), (0,))):
    return lax.dot_general(former, latter, (dims, ((), ())), preferred_element_type=jnp.float32)


def turn(values, cosine, sine):
    half = values.shape[1] // 2
    front, back = values[:, :half], values[:, half:]
    return jnp.concatenate(
        [front * cosine - back * sine, back * cosine + front * sine], axis=1
    )


def project_heads(rows, weight, inner, expand, cosine, sine, queries):
    count, depth = rows.shape
    kinds = queries + 2

    def kernel(rows_ref, weight_ref, inner_ref, expand_ref, cosine_ref, sine_ref, out_ref):
        kind = pl.program_id(0) % kinds
        values = fdot(rows_ref[...], weight_ref[...]) + fdot(inner_ref[...], expand_ref[...])

        @pl.when(kind == kinds - 1)
        def _():
            out_ref[...] = low(values)

        @pl.when(kind < kinds - 1)
        def _():
            scale = jnp.where(kind < queries, HEAD_WIDTH ** (-0.5), 1.0)
            out_ref[...] = low(turn(values, cosine_ref[...], sine_ref[...]) * scale)

    whole = lambda array: pl.BlockSpec(array.shape, lambda j: (0, 0))
    return pl.pallas_call(
        kernel,
        out_shape=jax.ShapeDtypeStruct((count, weight.shape[1]), jnp.bfloat16),
        grid=(weight.shape[1] // HEAD_WIDTH,),
        in_specs=[
            whole(rows),
            pl.BlockSpec((depth, HEAD_WIDTH), lambda j: (0, j)),
            whole(inner),
            pl.BlockSpec((expand.shape[0], HEAD_WIDTH), lambda j: (0, j)),
            whole(cosine),
            whole(sine),
        ],
        out_specs=pl.BlockSpec((count, HEAD_WIDTH), lambda j: (0, j)),
        compiler_params=pltpu.CompilerParams(vmem_limit_bytes=40 << 20),
        cost_estimate=TINY,
    )(rows, weight, inner, expand, cosine, sine)


def soft_scores(query, keys, keep):
    bounded = jnp.tanh(fdot(query, keys, ((1,), (1,))) * (1.0 / 50.0))
    masked = jnp.where(keep, 50.0 * bounded, -1e30)
    exponent = jnp.exp(masked - jnp.max(masked, axis=1, keepdims=True))
    return bounded, exponent / jnp.sum(exponent, axis=1, keepdims=True)


def attend(projected, received, visible, queries):
    count = projected.shape[0]
    wide, pair = (queries + 2) * HEAD_WIDTH, 2 * HEAD_WIDTH

    def kernel(mine_ref, got_ref, visible_ref, out_ref):
        first = queries * HEAD_WIDTH
        mine = mine_ref[:, first:]
        got = got_ref[...]
        keys = jnp.concatenate([mine[:, :HEAD_WIDTH], got[:, :HEAD_WIDTH]])
        values = jnp.concatenate([mine[:, HEAD_WIDTH:], got[:, HEAD_WIDTH:]])
        keep = visible_ref[...] > 0
        for h in range(queries):
            columns = slice(h * HEAD_WIDTH, (h + 1) * HEAD_WIDTH)
            _, probs = soft_scores(mine_ref[:, columns], keys, keep)
            out_ref[:, columns] = low(fdot(low(probs), values))

    return pl.pallas_call(
        kernel,
        out_shape=jax.ShapeDtypeStruct((count, 2 * queries * HEAD_WIDTH), jnp.bfloat16),
        grid=(2,),
        in_specs=[
            pl.BlockSpec((count, wide), lambda j: (0, j)),
            pl.BlockSpec((count, pair), lambda j: (0, j)),
            pl.BlockSpec(visible.shape, lambda j: (0, 0)),
        ],
        out_specs=pl.BlockSpec((count, queries * HEAD_WIDTH), lambda j: (0, j)),
        compiler_params=pltpu.CompilerParams(vmem_limit_bytes=40 << 20),
        cost_estimate=TINY,
    )(projected, received, visible)


def attend_back(projected, received, visible, grad_mixed, cosine, sine, queries):
    count = projected.shape[0]
    wide, pair = (queries + 2) * HEAD_WIDTH, 2 * HEAD_WIDTH

    def kernel(mine_ref, got_ref, visible_ref, grad_ref, cos_ref, sin_ref, *out_refs):
        query_ref, pair_ref, send_ref = out_refs
        first = queries * HEAD_WIDTH
        mine = mine_ref[:, first:]
        got = got_ref[...]
        keys = jnp.concatenate([mine[:, :HEAD_WIDTH], got[:, :HEAD_WIDTH]])
        values = jnp.concatenate([mine[:, HEAD_WIDTH:], got[:, HEAD_WIDTH:]])
        keep = visible_ref[...] > 0
        grad_keys, grad_values = 0.0, 0.0
        for h in range(queries):
            columns = slice(h * HEAD_WIDTH, (h + 1) * HEAD_WIDTH)
            query, grad = mine_ref[:, columns], grad_ref[:, columns]
            bounded, probs = soft_scores(query, keys, keep)
            grad_values = grad_values + fdot(low(probs), grad, ((0,), (0,)))
            grad_probs = fdot(grad, values, ((1,), (1,)))
            inner = jnp.sum(probs * grad_probs, axis=1, keepdims=True)
            grad_scores = low(probs * (grad_probs - inner) * (1.0 - bounded * bounded))
            grad_query = fdot(grad_scores, keys) * HEAD_WIDTH ** (-0.5)
            query_ref[:, columns] = low(turn(grad_query, cos_ref[...], -sin_ref[...]))
            grad_keys = grad_keys + fdot(grad_scores, query, ((0,), (0,)))
        pair_ref[:, :HEAD_WIDTH] = grad_keys[:count]
        pair_ref[:, HEAD_WIDTH:] = grad_values[:count]
        send_ref[:, :HEAD_WIDTH] = low(grad_keys[count:])
        send_ref[:, HEAD_WIDTH:] = low(grad_values[count:])

    whole = lambda array: pl.BlockSpec(array.shape, lambda j: (0, 0))
    return pl.pallas_call(
        kernel,
        out_shape=[
            jax.ShapeDtypeStruct((count, 2 * queries * HEAD_WIDTH), jnp.bfloat16),
            jax.ShapeDtypeStruct((count, 2 * pair), jnp.float32),
            jax.ShapeDtypeStruct((count, 2 * pair), jnp.bfloat16),
        ],
        grid=(2,),
        in_specs=[
            pl.BlockSpec((count, wide), lambda j: (0, j)),
            pl.BlockSpec((count, pair), lambda j: (0, j)),
            whole(visible),
            pl.BlockSpec((count, queries * HEAD_WIDTH), lambda j: (0, j)),
            whole(cosine),
            whole(sine),
        ],
        out_specs=[
            pl.BlockSpec((count, queries * HEAD_WIDTH), lambda j: (0, j)),
            pl.BlockSpec((count, pair), lambda j: (0, j)),
            pl.BlockSpec((count, pair), lambda j: (0, 1 - j)),
        ],
        compiler_params=pltpu.CompilerParams(vmem_limit_bytes=48 << 20),
        cost_estimate=TINY,
    )(projected, received, visible, grad_mixed, cosine, sine)


GELU_A = math.sqrt(2.0 / math.pi)
GELU_B = 0.044715


def gate_and_up(rows, w_gate, w_up, inner, e_gate, e_up):
    count, depth = rows.shape
    units, tile = w_gate.shape[1], 256
    half = inner.shape[1] // 2
    step = count // 4

    def kernel(rows_ref, gate_w, up_w, inner_ref, gate_e, up_e, hidden_ref, gate_ref, up_ref):
        for i in range(4):
            here = slice(i * step, (i + 1) * step)
            inner_rows = inner_ref[here]
            gate = fdot(rows_ref[here], gate_w[...]) + fdot(inner_rows[:, :half], gate_e[...])
            up = fdot(rows_ref[here], up_w[...]) + fdot(inner_rows[:, half:], up_e[...])
            square = gate * gate
            bend = jnp.tanh(GELU_A * gate * (1.0 + GELU_B * square))
            half_up = 0.5 * (1.0 + bend)
            slope = half_up + 0.5 * gate * (1.0 - bend * bend) * (
                GELU_A * (1.0 + 3.0 * GELU_B * square)
            )
            bent = gate * half_up
            hidden_ref[here] = low(bent * up)
            gate_ref[here] = low(up * slope)
            up_ref[here] = low(bent)

    whole = lambda array: pl.BlockSpec(array.shape, lambda j: (0, 0))
    column = lambda array: pl.BlockSpec((array.shape[0], tile), lambda j: (0, j))
    return pl.pallas_call(
        kernel,
        out_shape=[jax.ShapeDtypeStruct((count, units), jnp.bfloat16)] * 3,
        grid=(units // tile,),
        in_specs=[whole(rows), column(w_gate), column(w_up), whole(inner), column(e_gate),
                  column(e_up)],
        out_specs=[pl.BlockSpec((count, tile), lambda j: (0, j))] * 3,
        compiler_params=pltpu.CompilerParams(vmem_limit_bytes=63 << 20),
        cost_estimate=TINY,
    )(rows, w_gate, w_up, inner, e_gate, e_up)


def square_shapes(count, depth):
    rows = count // 4
    half = rows // 2
    return [
        jax.ShapeDtypeStruct((rows, depth), jnp.float32),
        jax.ShapeDtypeStruct((half, depth), jnp.float32),
        jax.ShapeDtypeStruct((half, depth), jnp.float32),
        jax.ShapeDtypeStruct((rows, depth), jnp.bfloat16),
        jax.ShapeDtypeStruct((rows, depth), jnp.bfloat16),
    ]


def store_square(values, refs):
    rows = values.shape[0] // 4
    half = rows // 2
    mine_ref, y_ref, z_ref, send_y_ref, send_z_ref = refs
    mine_ref[...] = values[:rows]
    y_ref[...] = values[rows + half : 2 * rows]
    z_ref[...] = values[2 * rows : 2 * rows + half]
    send_y_ref[:half] = low(values[rows : rows + half])
    send_y_ref[half:] = low(values[3 * rows : 3 * rows + half])
    send_z_ref[:half] = low(values[2 * rows + half : 3 * rows])
    send_z_ref[half:] = low(values[3 * rows + half :])


def down_last(first, hidden, w_down_t):
    count, depth = first.shape
    tile = depth // 3

    def kernel(first_ref, hidden_ref, weight_ref, *out_refs):
        store_square(
            first_ref[...] + fdot(hidden_ref[...], weight_ref[...], ((1,), (1,))), out_refs
        )

    shapes = square_shapes(count, depth)
    return pl.pallas_call(
        kernel,
        out_shape=shapes,
        grid=(depth // tile,),
        in_specs=[
            pl.BlockSpec((count, tile), lambda j: (0, j)),
            pl.BlockSpec(hidden.shape, lambda j: (0, 0)),
            pl.BlockSpec((tile, w_down_t.shape[1]), lambda j: (j, 0)),
        ],
        out_specs=[pl.BlockSpec((shape.shape[0], tile), lambda j: (0, j)) for shape in shapes],
        compiler_params=pltpu.CompilerParams(vmem_limit_bytes=48 << 20),
        cost_estimate=TINY,
    )(first, hidden, w_down_t)


def feed_forward_back(grad_rows, e_down, s_gate_up, keep, chunks):
    count, depth = grad_rows.shape
    tiles = [chunk[0].shape[1] // 2 for chunk in chunks]
    columns = depth // 3
    steps = []
    for i, chunk in enumerate(chunks):
        steps += [(i, j) for j in range(chunk[0].shape[1] // tiles[i])]
    total = len(steps)
    firsts = [steps.index((i, 0)) for i in range(len(chunks))]
    counts = [chunk[0].shape[1] // tiles[i] for i, chunk in enumerate(chunks)]
    starts = [sum(chunk[0].shape[1] for chunk in chunks[:i]) for i in range(len(chunks))]
    width = sum(chunk[0].shape[1] for chunk in chunks)
    twice = e_down.shape[0]
    each = len(chunks[0])
    parts = square_shapes(count, depth)

    def kernel(grad_ref, e_down_ref, s_ref, keep_ref, *refs):
        ins = refs[: each * len(chunks)]
        out_refs = refs[each * len(chunks) :]
        rows_refs = out_refs[: len(parts)]
        inner_grad_ref, inner_ref, gates_ref, ups_ref, sums_ref = out_refs[len(parts) :]
        step = pl.program_id(0)

        @pl.when(step == 0)
        def _():
            inner_grad = fdot(grad_ref[...], e_down_ref[...], ((1,), (1,)))
            inner_grad_ref[...] = low(inner_grad * keep_ref[:, :twice])
            sums_ref[...] = jnp.zeros_like(sums_ref)

        def one(i, down, gate_in, up_in, s_down, e_gate, e_up, gate_w, up_w):
            place = pl.ds(pl.multiple_of(starts[i] + (step - firsts[i]) * tiles[i], 128), tiles[i])
            grad = fdot(grad_ref[...], down[...]) + fdot(inner_grad_ref[...], s_down[...])
            grad_gate = low(grad * gate_in[...].astype(jnp.float32))
            grad_up = low(grad * up_in[...].astype(jnp.float32))
            gates_ref[:, place] = grad_gate
            ups_ref[:, place] = grad_up
            first = fdot(grad_gate, e_gate[...], ((1,), (1,)))
            second = fdot(grad_up, e_up[...], ((1,), (1,)))
            sums_ref[:, :twice] += first
            sums_ref[:, twice:] += second

        for i in range(len(chunks)):
            within = (step >= firsts[i]) & (step < firsts[i] + counts[i])
            pl.when(within)(functools.partial(one, i, *ins[i * each : (i + 1) * each]))

        @pl.when(step == total - 1)
        def _():
            inner_ref[...] = low(sums_ref[...] * keep_ref[...])

        @pl.when(step >= total)
        def _():
            rows = fdot(inner_ref[...], s_ref[...])
            for i, chunk in enumerate(chunks):
                gate_w, up_w = ins[(i + 1) * each - 2 : (i + 1) * each]
                place = slice(starts[i], starts[i] + chunk[0].shape[1])
                rows += fdot(gates_ref[:, place], gate_w[...], ((1,), (1,)))
                rows += fdot(ups_ref[:, place], up_w[...], ((1,), (1,)))
            store_square(rows, rows_refs)

    once = pl.Buffered(1)
    whole = lambda array: pl.BlockSpec(array.shape, lambda j: (0, 0), pipeline_mode=once)
    second = lambda j: jnp.clip(j - total, 0, depth // columns - 1)

    def column(i, array):
        return pl.BlockSpec(
            (array.shape[0], tiles[i]),
            lambda j: (0, jnp.clip(j - firsts[i], 0, counts[i] - 1)),
        )

    def specs(i, chunk):
        return [column(i, array) for array in chunk[:-2]] + [
            pl.BlockSpec((columns, array.shape[1]), lambda j: (second(j), 0))
            for array in chunk[-2:]
        ]

    return pl.pallas_call(
        kernel,
        out_shape=parts
        + [
            jax.ShapeDtypeStruct((count, twice), jnp.bfloat16),
            jax.ShapeDtypeStruct((count, 2 * twice), jnp.bfloat16),
            jax.ShapeDtypeStruct((count, width), jnp.bfloat16),
            jax.ShapeDtypeStruct((count, width), jnp.bfloat16),
        ],
        grid=(total + depth // columns,),
        in_specs=[
            whole(grad_rows),
            whole(e_down),
            pl.BlockSpec((s_gate_up.shape[0], columns), lambda j: (0, second(j))),
            whole(keep),
        ]
        + [spec for i, chunk in enumerate(chunks) for spec in specs(i, chunk)],
        out_specs=[
            pl.BlockSpec((part.shape[0], columns), lambda j: (0, second(j))) for part in parts
        ]
        + [
            pl.BlockSpec((count, twice), lambda j: (0, 0)),
            pl.BlockSpec((count, 2 * twice), lambda j: (0, 0)),
            pl.BlockSpec((count, width), lambda j: (0, 0), pipeline_mode=once),
            pl.BlockSpec((count, width), lambda j: (0, 0), pipeline_mode=once),
        ],
        scratch_shapes=[pltpu.VMEM((count, 2 * twice), jnp.float32)],
        compiler_params=pltpu.CompilerParams(vmem_limit_bytes=63 << 20),
        cost_estimate=TINY,
    )(grad_rows, e_down, s_gate_up, keep, *[array for chunk in chunks for array in chunk])


def scatter_pair(part):
    rows = part.shape[0] // 2
    got = flip(low(part[rows:]), "tensor", 2)
    return part[:rows] + got.astype(jnp.float32)


def gather_pair(own):
    return jnp.concatenate([own, flip(own, "tensor", 2)])


def gather_square(own):
    half = own.shape[0] // 2
    from_y = flip(own, "tensor", 2)
    from_z = flip(own, "dp", 2)
    send_z, send_y = settle(from_y[:half], from_z[half:])
    diagonal = [flip(send_z, "dp", 2), flip(send_y, "tensor", 2)]
    return jnp.concatenate([own, from_y, from_z] + diagonal)


def sum_by_adapter(ids, gathered, shared, widths):
    count, rows, columns = gathered.shape
    cuts = [0, shared] + [shared + sum(widths[: i + 1]) for i in range(len(widths))]

    def kernel(ids_ref, gathered_ref, *refs):
        out_refs, total_ref = refs[:-1], refs[-1]
        total_refs = [total_ref] + list(out_refs[1:])
        for ref in total_refs:
            ref[...] = jnp.zeros_like(ref)
        for entry in range(count):
            adapter = ids_ref[entry]
            for i, ref in enumerate(total_refs):
                ref[adapter] += gathered_ref[entry, :, cuts[i] : cuts[i + 1]].astype(jnp.float32)
        out_refs[0][...] = low(total_ref[...])

    shapes = [jax.ShapeDtypeStruct((ADAPTERS, rows, shared), jnp.bfloat16)] + [
        jax.ShapeDtypeStruct((ADAPTERS, rows, width), jnp.float32) for width in widths
    ]
    return pl.pallas_call(
        kernel,
        out_shape=shapes,
        in_specs=[
            pl.BlockSpec(memory_space=pltpu.SMEM),
            pl.BlockSpec(gathered.shape, lambda: (0, 0, 0)),
        ],
        out_specs=[pl.BlockSpec(shape.shape, lambda: (0, 0, 0)) for shape in shapes],
        scratch_shapes=[pltpu.VMEM((ADAPTERS, rows, shared), jnp.float32)],
        compiler_params=pltpu.CompilerParams(vmem_limit_bytes=40 << 20),
        cost_estimate=TINY,
    )(ids, gathered)


def sum_unit_grads(hots, gathered, kinds):
    count, rows, columns = gathered.shape
    rank = rows // kinds
    adapters = hots.shape[2]

    def kernel(hots_ref, gathered_ref, *out_refs):
        for side in range(2):
            for kind in range(kinds):
                here = slice(kind * rank, (kind + 1) * rank)

                @pl.loop(0, adapters)
                def _(adapter):
                    total = 0.0
                    for entry in range(count):
                        total += hots_ref[side, entry, adapter] * gathered_ref[
                            entry, here
                        ].astype(jnp.float32)
                    out_refs[kind][adapter, :, side * columns : (side + 1) * columns] = total

    return pl.pallas_call(
        kernel,
        out_shape=[jax.ShapeDtypeStruct((adapters, rank, 2 * columns), jnp.float32)] * kinds,
        in_specs=[
            pl.BlockSpec(memory_space=pltpu.SMEM),
            pl.BlockSpec(gathered.shape, lambda: (0, 0, 0)),
        ],
        out_specs=[pl.BlockSpec((adapters, rank, 2 * columns), lambda: (0, 0, 0))] * kinds,
        compiler_params=pltpu.CompilerParams(vmem_limit_bytes=48 << 20),
        cost_estimate=TINY,
    )(hots, gathered)


def join_halves(core, mine, other, kinds):
    adapters, rank, columns = mine.shape
    half = columns // kinds

    def kernel(core_ref, mine_ref, other_ref, *out_refs):
        swap = core_ref[0] == 1
        for kind in range(kinds):
            here = slice(kind * half, (kind + 1) * half)
            first = mine_ref[:, :, here].astype(jnp.float32)
            second = other_ref[:, :, here].astype(jnp.float32)
            out_refs[kind][:, :, :half] = jnp.where(swap, second, first)
            out_refs[kind][:, :, half:] = jnp.where(swap, first, second)

    return pl.pallas_call(
        kernel,
        out_shape=[jax.ShapeDtypeStruct((adapters, rank, 2 * half), jnp.float32)] * kinds,
        in_specs=[pl.BlockSpec(memory_space=pltpu.SMEM)]
        + [pl.BlockSpec(mine.shape, lambda: (0, 0, 0))] * 2,
        out_specs=[pl.BlockSpec((adapters, rank, 2 * half), lambda: (0, 0, 0))] * kinds,
        compiler_params=pltpu.CompilerParams(vmem_limit_bytes=48 << 20),
        cost_estimate=TINY,
    )(core, mine, other)


def square_first(parts):
    mine, to_y, to_z, send_y, send_z = parts
    return (flip(send_y, "tensor", 2), flip(send_z, "dp", 2)), (mine, to_y, to_z)


def square_last(first, rest):
    got_y, got_z = (got.astype(jnp.float32) for got in first)
    mine, to_y, to_z = rest
    half = to_y.shape[0]
    send_y, send_z = settle(low(to_y + got_z[half:]), low(to_z + got_y[half:]))
    last_y = flip(send_y, "tensor", 2).astype(jnp.float32)
    last_z = flip(send_z, "dp", 2).astype(jnp.float32)
    return jnp.concatenate(
        [mine[:half] + got_y[:half] + last_z, mine[half:] + got_z[:half] + last_y]
    )


def tree_bits(trees):
    return [1 << b for b in range(1, trees.bit_length() - 1)][::-1] + [1]


def tree_order(trees):
    bits = tree_bits(trees)
    order = [0]
    for bit in bits[-1:] + bits[:-1]:
        order += [i ^ bit for i in order]
    return order


def on_device(
    layer_input,
    cotangent,
    norm_gains,
    w_query,
    w_key,
    w_value,
    w_output,
    w_gate,
    w_up,
    w_down,
    query_shrink,
    key_shrink,
    value_shrink,
    output_shrink,
    gate_shrink,
    up_shrink,
    down_shrink,
    query_expand,
    key_expand,
    value_expand,
    output_expand,
    gate_expand,
    up_expand,
    down_expand,
    adapter_ids,
    parent_segments,
    segment_ids,
):
    trees = lax.axis_size("dp")
    columns_z = trees // 2
    my_tree = lax.axis_index("dp")
    my_z, my_x = my_tree // 2, my_tree % 2
    my_part = lax.axis_index("tensor")
    odd = my_z % 2 == 1
    norm_gain = norm_gains.astype(jnp.float32)
    place = my_x.astype(jnp.int32)[None]

    def halves(values):
        half = values.shape[-1] // 2
        return jnp.stack([values[:, :half], values[:, half:]])

    def on_core(values):
        return flip(values, "tensor", 1)

    cut = w_query.shape[0] // 2 // 16 * 16
    qkv_parts = [
        jnp.concatenate([weight[rows] for weight in (w_query, w_key, w_value)], axis=1)
        for rows in (slice(0, cut), slice(cut, None))
    ]
    gate_halves, up_halves, down_halves = halves(w_gate), halves(w_up), halves(w_down.T)
    units = gate_halves.shape[2]
    first_units = (units // 128 + 1) // 2 * 128
    waiting = [
        qkv_parts[0][None],
        qkv_parts[1][None],
        w_output.T[None],
        gate_halves[:, :, first_units:],
        up_halves[:, :, first_units:],
        gate_halves[:, :, :first_units],
        up_halves[:, :, :first_units],
        down_halves[:, :, :first_units],
        down_halves[:, :, first_units:],
    ]
    waiting = [
        jnp.concatenate([blocks] * (columns_z // blocks.shape[0])) for blocks in waiting
    ]
    count = len(waiting)
    near, cross = {}, {}

    near_core, cross_core = {}, {}

    def transfers(step):
        if step < count:
            near[step] = along_z(waiting[step], columns_z)
        if 0 <= step - 1 < count:
            cross[step - 1] = flip(near[step - 1], "dp", 1)
            near_core[step - 1] = on_core(near[step - 1])
        if 0 <= step - 2 < count:
            cross_core[step - 2] = on_core(cross[step - 2])

    def close(step, *values):
        moved = [
            (store, key)
            for store, key in (
                (near, step),
                (cross, step - 1),
                (near_core, step - 1),
                (cross_core, step - 2),
            )
            if key in store
        ]
        following = [waiting[step + 1]] if step + 1 < count else []
        moved_values, following, values = settle(
            [store[key] for store, key in moved], following, values
        )
        for (store, key), value in zip(moved, moved_values):
            store[key] = value
        if following:
            waiting[step + 1] = following[0]
        return values

    def matrix(*keys):
        stores = (near, cross, near_core, cross_core)
        return assemble([[store[key] for store in stores] for key in keys], place)

    transfers(0)
    own_rows = layer_input.astype(jnp.float32)
    normed = low(rms_scale(own_rows, norm_gain[0]))
    near_ids = flip(adapter_ids, "dp", 2)
    labels = jnp.arange(ADAPTERS, dtype=jnp.int32)
    order = jnp.stack([my_part, my_part ^ 2, my_part ^ 1, my_part ^ 3]).astype(jnp.int32)
    visible, cos_rows, sin_rows = tree_tables(segment_ids, parent_segments[0], order)
    row_count = 2 * normed.shape[0]
    visible = low(visible[:row_count])
    cos_rows, sin_rows = cos_rows[:row_count], sin_rows[:row_count]
    ids_parts = [adapter_ids, flip(adapter_ids, "dp", 1)]
    normed, near_ids, visible, cos_rows, sin_rows, ids_parts = close(
        0, normed, near_ids, visible, cos_rows, sin_rows, ids_parts
    )

    transfers(1)
    normed_all = gather_pair(normed)
    picks = jnp.concatenate([adapter_ids, near_ids, (my_z % 2).astype(jnp.int32)[None]])
    normed_all, picks = settle(normed_all, picks)
    picked = pick_adapters(
        picks,
        [
            (stack, False)
            for stack in (
                query_shrink,
                key_shrink,
                value_shrink,
                query_expand,
                key_expand,
                value_expand,
                output_shrink,
                output_expand,
            )
        ]
        + [
            (stack, near_tree)
            for stack in (gate_shrink, up_shrink, down_expand)
            for near_tree in (False, True)
        ],
        [
            (stack, near_tree)
            for stack in (gate_expand, up_expand, down_shrink)
            for near_tree in (False, True)
        ],
    )
    s_qkv = jnp.concatenate(picked[0:3])
    e_parts = picked[3:6]
    rank = e_parts[0].shape[0]
    widths = [part.shape[1] for part in e_parts]
    attn_mine = jnp.concatenate(picked[3:7], axis=1)
    e_output = picked[7]
    s_gate_up = jnp.concatenate(picked[8:12])
    e_down = jnp.concatenate(picked[12:14])
    ffn_mine = jnp.concatenate(picked[14:20])
    for bit in tree_bits(trees)[:-2]:
        tree_ids = jnp.concatenate(ids_parts)
        ids_parts = [tree_ids, flip(tree_ids, "dp", bit)]
    normed_all, attn_mine, e_output, s_gate_up, e_down, ffn_mine, s_qkv, ids_parts = close(
        1, normed_all, attn_mine, e_output, s_gate_up, e_down, ffn_mine, s_qkv, ids_parts
    )

    transfers(2)
    attn_other = on_core(attn_mine)
    ffn_other = on_core(ffn_mine)
    inner_qkv = low(times_rows(normed_all, s_qkv))
    tree_ids = jnp.concatenate(ids_parts)
    ids_parts = [tree_ids, flip(tree_ids, "dp", 2)]
    attn_other, ffn_other, inner_qkv, ids_parts = close(
        2, attn_other, ffn_other, inner_qkv, ids_parts
    )
    tree_ids = jnp.concatenate(ids_parts)

    transfers(3)
    heads_here = sum(widths)
    queries = widths[0] // HEAD_WIDTH
    e_mine = attn_mine[:, :heads_here]
    e_other = attn_other[:, :heads_here]
    s_output = beside(attn_mine[:, heads_here:], attn_other[:, heads_here:])
    starts = [sum(widths[:i]) for i in range(4)]
    column_kind = sum(
        (jnp.arange(heads_here, dtype=jnp.int32) >= start).astype(jnp.int32)
        for start in starts[1:3]
    )
    kind_mask = (
        jnp.arange(3 * rank, dtype=jnp.int32)[:, None] // rank
        == jnp.concatenate([column_kind, column_kind])[None, :]
    )
    e_qkv = low(jnp.where(kind_mask, jnp.tile(beside(e_mine, e_other), (3, 1)), 0.0))
    units_a = beside(ffn_mine[:, :first_units], ffn_other[:, :first_units])
    units_b = beside(ffn_mine[:, first_units:], ffn_other[:, first_units:])
    adapters_ab = [
        [block[i * 2 * rank : (i + 1) * 2 * rank] for i in range(3)] for block in (units_a, units_b)
    ]
    e_qkv, s_output, adapters_ab = close(3, e_qkv, s_output, adapters_ab)

    transfers(4)
    full_qkv = matrix(0, 1)
    projected = project_heads(
        normed_all, full_qkv, inner_qkv, e_qkv, cos_rows, sin_rows, queries
    )
    received = on_core(
        beside(projected[:, heads_here + starts[1] :], projected[:, starts[1] : heads_here])
    )
    full_qkv, projected, received = close(4, full_qkv, projected, received)

    transfers(5)
    full_out_t = matrix(2)
    mixed_heads = attend(projected, received, visible, queries)
    inner_output = low(times_rows(mixed_heads, s_output))
    attn_part = times_rows(mixed_heads, full_out_t) + product(inner_output, e_output)
    attended = scatter_pair(attn_part)
    mixed_heads, full_out_t, inner_output, attended = close(
        5, mixed_heads, full_out_t, inner_output, attended
    )

    transfers(6)
    full_gate_b = matrix(3)
    residual = own_rows + rms_scale(attended, norm_gain[1])
    normed_ffn = low(rms_scale(residual, norm_gain[2]))
    normed_y = flip(normed_ffn, "tensor", 2)
    half_rows = normed_ffn.shape[0] // 2
    normed_z_first = flip(normed_ffn[:half_rows], "dp", 2)
    residual, normed_ffn, normed_y, normed_z_first, full_gate_b = close(
        6, residual, normed_ffn, normed_y, normed_z_first, full_gate_b
    )

    transfers(7)
    normed_z_last = flip(normed_ffn[half_rows:], "dp", 2)
    full_up_b = matrix(4)
    normed_zy_first = flip(normed_z_first, "tensor", 2)
    normed_z_last, normed_zy_first, full_up_b = close(
        7, normed_z_last, normed_zy_first, full_up_b
    )

    transfers(8)
    normed_zy_last = flip(normed_z_last, "tensor", 2)
    full_gate_a = matrix(5)
    ffn_rows = jnp.concatenate(
        [normed_ffn, normed_y, normed_z_first, normed_z_last, normed_zy_first, normed_zy_last]
    )
    block_rows = residual.shape[0]
    row_block = jnp.arange(4 * block_rows, dtype=jnp.int32) // block_rows
    row_near = (row_block // 2)[:, None]
    rank_near = (jnp.arange(4 * rank, dtype=jnp.int32) // rank % 2)[None, :]
    keep_four = (row_near == rank_near).astype(jnp.float32)
    keep_two = keep_four[:, : 2 * rank]
    inner_gate_up = low(keep_four * times_rows(ffn_rows, s_gate_up))
    chunk_b = gate_and_up(
        ffn_rows, full_gate_b, full_up_b, inner_gate_up, adapters_ab[1][0], adapters_ab[1][1]
    )
    ffn_rows, inner_gate_up, chunk_b, full_gate_a = close(
        8, ffn_rows, inner_gate_up, chunk_b, full_gate_a
    )

    transfers(9)
    full_up_a = matrix(6)
    chunk_a = gate_and_up(
        ffn_rows, full_gate_a, full_up_a, inner_gate_up, adapters_ab[0][0], adapters_ab[0][1]
    )
    chunk_out = [chunk_a, chunk_b]
    hidden = [parts[0] for parts in chunk_out]
    inner_down = low(
        keep_two
        * (times_rows(hidden[0], adapters_ab[0][2]) + times_rows(hidden[1], adapters_ab[1][2]))
    )
    full_down_a = matrix(7)
    ffn_first = times_rows(hidden[0], full_down_a) + product(inner_down, e_down)
    chunk_out, inner_down, ffn_first = close(9, chunk_out, inner_down, ffn_first)
    hidden = [parts[0] for parts in chunk_out]

    cross_core[8] = on_core(cross[8])
    full_down_b = matrix(8)
    ffn_out = square_last(*square_first(down_last(ffn_first, hidden[1], full_down_b)))
    layer_output = low(residual + rms_scale(ffn_out, norm_gain[3]))

    grad_out = cotangent.astype(jnp.float32)
    grad_ffn = gather_square(low(rms_back(ffn_out, norm_gain[3], grad_out)))
    *grad_normed_parts, grad_inner_down, grad_inner_gate_up, grad_gate, grad_up = feed_forward_back(
        grad_ffn,
        e_down,
        s_gate_up,
        keep_four,
        [
            (full_down, *parts[1:], adapters[2], adapters[0], adapters[1], full_gate, full_up)
            for full_down, full_gate, full_up, parts, adapters in (
                (full_down_a, full_gate_a, full_up_a, chunk_out[0], adapters_ab[0]),
                (full_down_b, full_gate_b, full_up_b, chunk_out[1], adapters_ab[1]),
            )
        ],
    )
    def from_other_core(mine, other):
        return low(mine + on_core(low(other)).astype(jnp.float32))

    parts_first, parts_rest = square_first(grad_normed_parts)
    grad_shrink_down = jnp.concatenate(
        [over_rows(grad_inner_down, units_of) for units_of in hidden], axis=1
    )
    inner_gate, inner_up = inner_gate_up[:, : 2 * rank], inner_gate_up[:, 2 * rank :]
    grad_units = jnp.stack(
        [
            grads.reshape(2, rank, 2 * units)
            for grads in (
                over_rows(inner_gate, grad_gate),
                over_rows(inner_up, grad_up),
                grad_shrink_down,
            )
        ],
        axis=1,
    ).reshape(6 * rank, 2 * units)
    rest = units - first_units
    cuts = [0, first_units, 2 * first_units, 2 * first_units + rest, 2 * units]
    quarters = [grad_units[:, cuts[i] : cuts[i + 1]] for i in range(4)]
    mine, other = beside(quarters[0], quarters[2]), beside(quarters[1], quarters[3])
    local = from_other_core(mine, other)
    parts_first, local, grad_inner_gate_up, grad_ffn = settle(
        parts_first, local, grad_inner_gate_up, grad_ffn
    )
    local_all = jnp.stack([local, flip(local, "dp", 1)])
    grad_expand_down = over_rows(inner_down, grad_ffn)
    grad_shrink_gate_up = over_rows(grad_inner_gate_up, ffn_rows)
    grad_normed_ffn = square_last(parts_first, parts_rest)
    grad_resid = grad_out + rms_back(residual, norm_gain[2], grad_normed_ffn)
    grad_attn_mine = low(rms_back(attended, norm_gain[1], grad_resid))
    shared = jnp.concatenate([grad_shrink_gate_up, grad_expand_down]).reshape(3, 2, rank, -1)
    grad_attn_mine, grad_resid, local_all, shared = settle(
        grad_attn_mine, grad_resid, local_all, shared
    )

    def core_half(blocks):
        half = blocks.shape[-1] // 2
        kept = jnp.where(my_part % 2 == 1, blocks[..., half:], blocks[..., :half])
        return jnp.concatenate([low(block) for block in kept], axis=1)

    def with_bit(values, bit):
        return jnp.concatenate([values, flip(values, "dp", bit)])

    grad_attn = gather_pair(grad_attn_mine)
    shared_near = flip(low(shared[:, 1]), "dp", 2)
    bits = tree_bits(trees)
    for bit in bits[:-2]:
        local_all = with_bit(local_all, bit)
    grad_attn, local_all, shared, shared_near = settle(grad_attn, local_all, shared, shared_near)

    local_near = flip(local_all, "dp", bits[-2])
    grad_inner_output = low(times_rows(grad_attn, e_output))
    grad_mixed = low(product(grad_attn, full_out_t) + product(grad_inner_output, s_output))
    grad_queries, grad_pairs, to_core = attend_back(
        projected, received, visible, grad_mixed, cos_rows, sin_rows, queries
    )
    pair = 2 * HEAD_WIDTH
    from_core = on_core(to_core)
    shared = shared[:, 0] + shared_near.astype(jnp.float32)
    shared = shared + on_core(low(shared)).astype(jnp.float32)
    shared = shared + flip(low(shared), "tensor", 2).astype(jnp.float32)
    shared_mine = core_half(shared)
    from_core, grad_queries, grad_pairs, shared_mine = settle(
        from_core, grad_queries, grad_pairs, shared_mine
    )

    shared_all = shared_mine[None]
    for bit in bits[:-2]:
        shared_all = with_bit(shared_all, bit)
    grad_expand_output = over_rows(inner_output, grad_attn)
    grad_shrink_output = over_rows(grad_inner_output, mixed_heads)
    grad_pairs = grad_pairs + from_core.astype(jnp.float32)
    grad_sides = []
    for side in range(2):
        keys_values = grad_pairs[:, side * pair : (side + 1) * pair]
        grad_sides += [
            grad_queries[:, side * widths[0] : (side + 1) * widths[0]],
            low(turn(keys_values[:, :HEAD_WIDTH], cos_rows, -sin_rows)),
            low(keys_values[:, HEAD_WIDTH:]),
        ]
    grad_qkv = jnp.concatenate(grad_sides, axis=1)
    grad_inner_qkv = low(times_rows(grad_qkv, e_qkv))
    grad_expand_qkv = over_rows(inner_qkv, grad_qkv)
    last = jnp.concatenate(
        [over_rows(grad_inner_qkv, normed_all), grad_expand_output]
    ).reshape(4, rank, -1)
    pieces = []
    for side in range(2):
        for i in range(3):
            first = side * heads_here + starts[i]
            pieces.append(grad_expand_qkv[i * rank : (i + 1) * rank, first : first + widths[i]])
        pieces.append(grad_shrink_output[:, side * widths[0] : (side + 1) * widths[0]])
    local_attn = from_other_core(
        jnp.concatenate(pieces[:4], axis=1), jnp.concatenate(pieces[4:], axis=1)
    )
    last = last + on_core(low(last)).astype(jnp.float32)
    last, local_attn, grad_qkv, grad_inner_qkv, shared_all = settle(
        last, local_attn, grad_qkv, grad_inner_qkv, shared_all
    )

    last_y = flip(low(last), "tensor", 2)
    shared_all = with_bit(shared_all, bits[-2])
    part = times_rows(grad_qkv, full_qkv) + product(grad_inner_qkv, s_qkv)
    last_y, part, shared_all, local_near = settle(last_y, part, shared_all, local_near)

    last_mine = beside(core_half(last + last_y.astype(jnp.float32)), local_attn)
    last_all = lax.all_to_all(
        jnp.broadcast_to(last_mine[None], (trees,) + last_mine.shape), "dp", 0, 0
    )
    from_y = flip(low(part[block_rows:]), "tensor", 2)
    shared_all = with_bit(shared_all, 1)
    from_y, shared_all = settle(from_y, shared_all)
    grad_normed = part[:block_rows] + from_y.astype(jnp.float32)
    input_grad = grad_resid + rms_back(own_rows, norm_gain[0], grad_normed)
    local_all = jnp.concatenate([local_all, local_near])

    tree_ids = tree_ids.reshape(trees)
    hot_near = (tree_ids[:, None] == labels[None, :]).astype(jnp.float32)
    distances = my_tree ^ jnp.arange(trees, dtype=jnp.int32)
    place_of = jnp.stack(
        [jnp.asarray(tree_order(trees).index(j), jnp.int32) for j in range(trees)]
    )
    at = jnp.sum(
        jnp.where(
            distances[:, None] == jnp.arange(trees, dtype=jnp.int32)[None, :], place_of[None, :], 0
        ),
        axis=1,
    )
    ids_trees = jnp.sum(
        jnp.where(
            at[:, None] == jnp.arange(trees, dtype=jnp.int32)[None, :], tree_ids[None, :], 0
        ),
        axis=1,
    )
    order_local = [0, 1]
    for bit in bits[:-1]:
        order_local += [i ^ bit for i in order_local]
    ids_at = {tree: i for i, tree in enumerate(tree_order(trees))}
    hots, crossing = [], []
    for j in order_local:
        for near_tree in range(2):
            hots.append(hot_near[ids_at[j ^ (2 * near_tree)]])
            crossing.append((j // 2) % 2)
    hots = jnp.stack(hots)
    parity = jnp.asarray(crossing, jnp.int32) ^ (my_z % 2).astype(jnp.int32)
    local_all = local_all.reshape(2 * trees, 3 * rank, units)
    hots = jnp.stack([jnp.where(parity[:, None] == side, hots, 0.0) for side in range(2)])
    ids_shared = tree_ids.reshape(2, trees // 4, 2).transpose(2, 0, 1).reshape(trees)
    out_expand_gate, out_expand_up, out_shrink_down = sum_unit_grads(hots, local_all, 3)
    core = (my_part % 2).astype(jnp.int32)[None]
    depth_half = s_qkv.shape[1] // 2
    (sums,) = sum_by_adapter(ids_shared, shared_all, 3 * depth_half, [])
    out_shrink_gate, out_shrink_up, out_expand_down = join_halves(core, sums, on_core(sums), 3)
    (last_all, input_grad, out_expand_gate, out_expand_up, out_shrink_down, out_shrink_gate,
     out_shrink_up, out_expand_down) = settle(
        last_all, input_grad, out_expand_gate, out_expand_up, out_shrink_down, out_shrink_gate,
        out_shrink_up, out_expand_down,
    )
    sums, out_expand_query, out_expand_key, out_expand_value, out_shrink_output = sum_by_adapter(
        ids_trees, last_all, 4 * depth_half, widths + widths[:1]
    )
    out_shrink_query, out_shrink_key, out_shrink_value, out_expand_output = join_halves(
        core, sums, on_core(sums), 4
    )
    return (
        layer_output,
        input_grad,
        out_shrink_query,
        out_shrink_key,
        out_shrink_value,
        out_shrink_output,
        out_shrink_gate,
        out_shrink_up,
        out_shrink_down,
        out_expand_query,
        out_expand_key,
        out_expand_value,
        out_expand_output,
        out_expand_gate,
        out_expand_up,
        out_expand_down,
    )


def solution(mesh):
    placed = (
        P(("dp", "tensor"), None),
        P(("dp", "tensor"), None),
        P(),
        P("dp", "tensor"),
        P("dp", "tensor"),
        P("dp", "tensor"),
        P("tensor", "dp"),
        P("dp", "tensor"),
        P("dp", "tensor"),
        P("tensor", "dp"),
        P(),
        P(),
        P(),
        P(None, None, "tensor"),
        P(),
        P(),
        P(None, None, "tensor"),
        P(None, None, "tensor"),
        P(None, None, "tensor"),
        P(None, None, "tensor"),
        P(),
        P(None, None, "tensor"),
        P(None, None, "tensor"),
        P(),
        P("dp"),
        P("dp", None),
        P("dp"),
    )
    return jax.shard_map(
        on_device,
        mesh=mesh,
        in_specs=placed,
        out_specs=(
            P(("dp", "tensor"), None),
            P(("dp", "tensor"), None),
            P(),
            P(),
            P(),
            P(None, None, "tensor"),
            P(),
            P(),
            P(None, None, "tensor"),
            P(None, None, "tensor"),
            P(None, None, "tensor"),
            P(None, None, "tensor"),
            P(),
            P(None, None, "tensor"),
            P(None, None, "tensor"),
            P(),
        ),
        check_vma=False,
    )
```

```python
import functools
import math

import jax
import jax.numpy as jnp
from jax import lax
from jax.experimental import pallas as pl
from jax.experimental.pallas import tpu as pltpu
from jax.sharding import PartitionSpec as P

HEAD_WIDTH = 256
ADAPTERS = 8
TINY = pl.CostEstimate(flops=1, transcendentals=0, bytes_accessed=1)


def rms_scale(value_rows, gain_row):
    inverse = lax.rsqrt(jnp.mean(value_rows * value_rows, axis=-1, keepdims=True) + 1e-06)
    return value_rows * inverse * gain_row


def rms_back(value_rows, gain_row, upstream):
    inverse = lax.rsqrt(jnp.mean(value_rows * value_rows, axis=-1, keepdims=True) + 1e-06)
    scaled = gain_row * upstream
    return inverse * scaled - value_rows * (inverse * inverse * inverse) * jnp.mean(
        value_rows * scaled, axis=-1, keepdims=True
    )


def pick_from(lookup, indices, labels):
    return jnp.sum(jnp.where(indices[:, None] == labels[None, :], lookup[None, :], 0), axis=1)


def tree_tables(segments, parents, order):
    count_seg = parents.shape[0]
    sequence_length = segments.shape[0]
    blocks = order.shape[0]
    labels = jnp.arange(count_seg, dtype=jnp.int32)
    ordered_places = jnp.arange(sequence_length, dtype=jnp.int32)
    member = segments[None, :] == labels[:, None]
    starts = jnp.min(jnp.where(member, ordered_places[None, :], sequence_length), axis=1)
    counts = jnp.sum(member.astype(jnp.int32), axis=1)
    grands = pick_from(parents, parents, labels)
    offsets = jnp.where(parents != labels, pick_from(counts, parents, labels), 0) + jnp.where(
        grands != parents, pick_from(counts, grands, labels), 0
    )
    block_rows = sequence_length // blocks
    chosen = order[:, None] == jnp.arange(blocks, dtype=jnp.int32)[None, :]
    segments = jnp.sum(
        jnp.where(chosen[:, :, None], segments.reshape(1, blocks, block_rows), 0), axis=1
    ).reshape(sequence_length)
    places = (
        order[:, None] * block_rows + jnp.arange(block_rows, dtype=jnp.int32)[None, :]
    ).reshape(sequence_length)
    tok_start = pick_from(starts, segments, labels)
    tok_offset = pick_from(offsets, segments, labels)
    tok_parent = pick_from(parents, segments, labels)
    tok_grand = pick_from(grands, segments, labels)
    positions = (places - tok_start + tok_offset).astype(jnp.float32)
    same_seg = (segments[None, :] == segments[:, None]) & (places[None, :] <= places[:, None])
    from_parent = (segments[None, :] == tok_parent[:, None]) & (tok_parent != segments)[:, None]
    from_grand = (segments[None, :] == tok_grand[:, None]) & (tok_grand != tok_parent)[:, None]
    visible = same_seg | from_parent | from_grand
    inv_freq = jnp.exp(
        jnp.arange(HEAD_WIDTH // 2, dtype=jnp.float32) * (-2.0 * math.log(10000.0) / HEAD_WIDTH)
    )
    angles = positions[:, None] * inv_freq[None, :]
    return (visible, jnp.cos(angles), jnp.sin(angles))


def product(former, latter):
    return jnp.dot(former, latter, preferred_element_type=jnp.float32)


def times_rows(former, latter):
    return lax.dot_general(
        former, latter, (((1,), (1,)), ((), ())), preferred_element_type=jnp.float32
    )


def over_rows(former, latter):
    return lax.dot_general(
        former, latter, (((0,), (0,)), ((), ())), preferred_element_type=jnp.float32
    )


def low(values):
    return values.astype(jnp.bfloat16)


def flip(values, axis_name, bit):
    size = lax.axis_size(axis_name)
    return lax.ppermute(values, axis_name, [(i, i ^ bit) for i in range(size)])


def settle(*groups):
    flat, tree = jax.tree.flatten(groups)
    return jax.tree.unflatten(tree, lax.optimization_barrier(flat))


def along_z(sent, columns_z):
    lines = [[2 * z + x for z in range(columns_z)] for x in range(2)]
    return lax.all_to_all(sent, "dp", 0, 0, axis_index_groups=lines)


def assemble(pieces, place):
    columns_z, _, columns = pieces[0][0].shape
    heights = [parts[0].shape[1] for parts in pieces]
    rows = sum(heights)

    def kernel(place_ref, *refs):
        out_ref = refs[-1]
        my_x = place_ref[0]
        for i, height in enumerate(heights):
            mine_ref, cross_ref, core_ref, core_cross_ref = refs[4 * i : 4 * i + 4]
            here = pl.ds(sum(heights[:i]), height)
            out_ref[my_x, here, :columns] = mine_ref[0]
            out_ref[my_x, here, columns:] = core_ref[0]
            out_ref[1 - my_x, here, :columns] = cross_ref[0]
            out_ref[1 - my_x, here, columns:] = core_cross_ref[0]

    out = pl.pallas_call(
        kernel,
        out_shape=jax.ShapeDtypeStruct((2 * columns_z, rows, 2 * columns), jnp.bfloat16),
        grid_spec=pltpu.PrefetchScalarGridSpec(
            num_scalar_prefetch=1,
            grid=(columns_z,),
            in_specs=[
                pl.BlockSpec((1, height, columns), lambda k, place_ref: (k, 0, 0))
                for height in heights
                for _ in range(4)
            ],
            out_specs=pl.BlockSpec((2, rows, 2 * columns), lambda k, place_ref: (k, 0, 0)),
        ),
        compiler_params=pltpu.CompilerParams(vmem_limit_bytes=32 << 20),
        cost_estimate=pl.CostEstimate(
            flops=0, transcendentals=0, bytes_accessed=16 * columns_z * rows * columns
        ),
    )(place, *[part for parts in pieces for part in parts])
    return out.reshape(2 * columns_z * rows, 2 * columns)


def beside(first, second):
    return jnp.concatenate([first, second], axis=1)


def pick_adapters(ids, whole, halved):
    rank = whole[0][0].shape[1]

    def kernel(ids_ref, *refs):
        count = len(refs) // 2
        for i in range(count):
            refs[count + i][...] = refs[i][0]

    in_specs, out_specs, shapes, stacks = [], [], [], []
    for entries, parity in ((whole, False), (halved, True)):
        for stack, near in entries:
            columns = stack.shape[2] // (2 if parity else 1)
            in_specs.append(
                pl.BlockSpec(
                    (1, rank, columns),
                    functools.partial(
                        lambda near, parity, i, ids_ref: (
                            ids_ref[1 if near else 0],
                            0,
                            ids_ref[2] if parity else 0,
                        ),
                        near,
                        parity,
                    ),
                )
            )
            out_specs.append(pl.BlockSpec((rank, columns), lambda i, ids_ref: (0, 0)))
            shapes.append(jax.ShapeDtypeStruct((rank, columns), stack.dtype))
            stacks.append(stack)
    return pl.pallas_call(
        kernel,
        out_shape=shapes,
        grid_spec=pltpu.PrefetchScalarGridSpec(
            num_scalar_prefetch=1, grid=(1,), in_specs=in_specs, out_specs=out_specs
        ),
        cost_estimate=TINY,
    )(ids, *stacks)


def fdot(former, latter, dims=((1,), (0,))):
    return lax.dot_general(former, latter, (dims, ((), ())), preferred_element_type=jnp.float32)


def turn(values, cosine, sine):
    half = values.shape[1] // 2
    front, back = values[:, :half], values[:, half:]
    return jnp.concatenate(
        [front * cosine - back * sine, back * cosine + front * sine], axis=1
    )


def project_heads(rows, weight, inner, expand, cosine, sine, queries):
    count, depth = rows.shape
    kinds = queries + 2

    def kernel(rows_ref, weight_ref, inner_ref, expand_ref, cosine_ref, sine_ref, out_ref):
        kind = pl.program_id(0) % kinds
        values = fdot(rows_ref[...], weight_ref[...]) + fdot(inner_ref[...], expand_ref[...])

        @pl.when(kind == kinds - 1)
        def _():
            out_ref[...] = low(values)

        @pl.when(kind < kinds - 1)
        def _():
            scale = jnp.where(kind < queries, HEAD_WIDTH ** (-0.5), 1.0)
            out_ref[...] = low(turn(values, cosine_ref[...], sine_ref[...]) * scale)

    whole = lambda array: pl.BlockSpec(array.shape, lambda j: (0, 0))
    return pl.pallas_call(
        kernel,
        out_shape=jax.ShapeDtypeStruct((count, weight.shape[1]), jnp.bfloat16),
        grid=(weight.shape[1] // HEAD_WIDTH,),
        in_specs=[
            whole(rows),
            pl.BlockSpec((depth, HEAD_WIDTH), lambda j: (0, j)),
            whole(inner),
            pl.BlockSpec((expand.shape[0], HEAD_WIDTH), lambda j: (0, j)),
            whole(cosine),
            whole(sine),
        ],
        out_specs=pl.BlockSpec((count, HEAD_WIDTH), lambda j: (0, j)),
        compiler_params=pltpu.CompilerParams(vmem_limit_bytes=40 << 20),
        cost_estimate=TINY,
    )(rows, weight, inner, expand, cosine, sine)


def soft_scores(query, keys, keep):
    bounded = jnp.tanh(fdot(query, keys, ((1,), (1,))) * (1.0 / 50.0))
    masked = jnp.where(keep, 50.0 * bounded, -1e30)
    exponent = jnp.exp(masked - jnp.max(masked, axis=1, keepdims=True))
    return bounded, exponent / jnp.sum(exponent, axis=1, keepdims=True)


def attend(projected, received, visible, queries):
    count = projected.shape[0]
    wide, pair = (queries + 2) * HEAD_WIDTH, 2 * HEAD_WIDTH

    def kernel(mine_ref, got_ref, visible_ref, out_ref):
        first = queries * HEAD_WIDTH
        mine = mine_ref[:, first:]
        got = got_ref[...]
        keys = jnp.concatenate([mine[:, :HEAD_WIDTH], got[:, :HEAD_WIDTH]])
        values = jnp.concatenate([mine[:, HEAD_WIDTH:], got[:, HEAD_WIDTH:]])
        keep = visible_ref[...] > 0
        for h in range(queries):
            columns = slice(h * HEAD_WIDTH, (h + 1) * HEAD_WIDTH)
            _, probs = soft_scores(mine_ref[:, columns], keys, keep)
            out_ref[:, columns] = low(fdot(low(probs), values))

    return pl.pallas_call(
        kernel,
        out_shape=jax.ShapeDtypeStruct((count, 2 * queries * HEAD_WIDTH), jnp.bfloat16),
        grid=(2,),
        in_specs=[
            pl.BlockSpec((count, wide), lambda j: (0, j)),
            pl.BlockSpec((count, pair), lambda j: (0, j)),
            pl.BlockSpec(visible.shape, lambda j: (0, 0)),
        ],
        out_specs=pl.BlockSpec((count, queries * HEAD_WIDTH), lambda j: (0, j)),
        compiler_params=pltpu.CompilerParams(vmem_limit_bytes=40 << 20),
        cost_estimate=TINY,
    )(projected, received, visible)


def attend_back(projected, received, visible, grad_mixed, cosine, sine, queries):
    count = projected.shape[0]
    wide, pair = (queries + 2) * HEAD_WIDTH, 2 * HEAD_WIDTH

    def kernel(mine_ref, got_ref, visible_ref, grad_ref, cos_ref, sin_ref, *out_refs):
        query_ref, pair_ref, send_ref = out_refs
        first = queries * HEAD_WIDTH
        mine = mine_ref[:, first:]
        got = got_ref[...]
        keys = jnp.concatenate([mine[:, :HEAD_WIDTH], got[:, :HEAD_WIDTH]])
        values = jnp.concatenate([mine[:, HEAD_WIDTH:], got[:, HEAD_WIDTH:]])
        keep = visible_ref[...] > 0
        grad_keys, grad_values = 0.0, 0.0
        for h in range(queries):
            columns = slice(h * HEAD_WIDTH, (h + 1) * HEAD_WIDTH)
            query, grad = mine_ref[:, columns], grad_ref[:, columns]
            bounded, probs = soft_scores(query, keys, keep)
            grad_values = grad_values + fdot(low(probs), grad, ((0,), (0,)))
            grad_probs = fdot(grad, values, ((1,), (1,)))
            inner = jnp.sum(probs * grad_probs, axis=1, keepdims=True)
            grad_scores = low(probs * (grad_probs - inner) * (1.0 - bounded * bounded))
            grad_query = fdot(grad_scores, keys) * HEAD_WIDTH ** (-0.5)
            query_ref[:, columns] = low(turn(grad_query, cos_ref[...], -sin_ref[...]))
            grad_keys = grad_keys + fdot(grad_scores, query, ((0,), (0,)))
        pair_ref[:, :HEAD_WIDTH] = grad_keys[:count]
        pair_ref[:, HEAD_WIDTH:] = grad_values[:count]
        send_ref[:, :HEAD_WIDTH] = low(grad_keys[count:])
        send_ref[:, HEAD_WIDTH:] = low(grad_values[count:])

    whole = lambda array: pl.BlockSpec(array.shape, lambda j: (0, 0))
    return pl.pallas_call(
        kernel,
        out_shape=[
            jax.ShapeDtypeStruct((count, 2 * queries * HEAD_WIDTH), jnp.bfloat16),
            jax.ShapeDtypeStruct((count, 2 * pair), jnp.float32),
            jax.ShapeDtypeStruct((count, 2 * pair), jnp.bfloat16),
        ],
        grid=(2,),
        in_specs=[
            pl.BlockSpec((count, wide), lambda j: (0, j)),
            pl.BlockSpec((count, pair), lambda j: (0, j)),
            whole(visible),
            pl.BlockSpec((count, queries * HEAD_WIDTH), lambda j: (0, j)),
            whole(cosine),
            whole(sine),
        ],
        out_specs=[
            pl.BlockSpec((count, queries * HEAD_WIDTH), lambda j: (0, j)),
            pl.BlockSpec((count, pair), lambda j: (0, j)),
            pl.BlockSpec((count, pair), lambda j: (0, 1 - j)),
        ],
        compiler_params=pltpu.CompilerParams(vmem_limit_bytes=48 << 20),
        cost_estimate=TINY,
    )(projected, received, visible, grad_mixed, cosine, sine)


GELU_A = math.sqrt(2.0 / math.pi)
GELU_B = 0.044715


def gate_and_up(rows, w_gate, w_up, inner, e_gate, e_up):
    count, depth = rows.shape
    units, tile = w_gate.shape[1], 256
    half = inner.shape[1] // 2
    step = count // 4

    def kernel(rows_ref, gate_w, up_w, inner_ref, gate_e, up_e, hidden_ref, gate_ref, up_ref):
        for i in range(4):
            here = slice(i * step, (i + 1) * step)
            inner_rows = inner_ref[here]
            gate = fdot(rows_ref[here], gate_w[...]) + fdot(inner_rows[:, :half], gate_e[...])
            up = fdot(rows_ref[here], up_w[...]) + fdot(inner_rows[:, half:], up_e[...])
            square = gate * gate
            bend = jnp.tanh(GELU_A * gate * (1.0 + GELU_B * square))
            half_up = 0.5 * (1.0 + bend)
            slope = half_up + 0.5 * gate * (1.0 - bend * bend) * (
                GELU_A * (1.0 + 3.0 * GELU_B * square)
            )
            bent = gate * half_up
            hidden_ref[here] = low(bent * up)
            gate_ref[here] = low(up * slope)
            up_ref[here] = low(bent)

    whole = lambda array: pl.BlockSpec(array.shape, lambda j: (0, 0))
    column = lambda array: pl.BlockSpec((array.shape[0], tile), lambda j: (0, j))
    return pl.pallas_call(
        kernel,
        out_shape=[jax.ShapeDtypeStruct((count, units), jnp.bfloat16)] * 3,
        grid=(units // tile,),
        in_specs=[whole(rows), column(w_gate), column(w_up), whole(inner), column(e_gate),
                  column(e_up)],
        out_specs=[pl.BlockSpec((count, tile), lambda j: (0, j))] * 3,
        compiler_params=pltpu.CompilerParams(vmem_limit_bytes=63 << 20),
        cost_estimate=TINY,
    )(rows, w_gate, w_up, inner, e_gate, e_up)


def square_shapes(count, depth):
    rows = count // 4
    half = rows // 2
    return [
        jax.ShapeDtypeStruct((rows, depth), jnp.float32),
        jax.ShapeDtypeStruct((half, depth), jnp.float32),
        jax.ShapeDtypeStruct((half, depth), jnp.float32),
        jax.ShapeDtypeStruct((rows, depth), jnp.bfloat16),
        jax.ShapeDtypeStruct((rows, depth), jnp.bfloat16),
    ]


def store_square(values, refs):
    rows = values.shape[0] // 4
    half = rows // 2
    mine_ref, y_ref, z_ref, send_y_ref, send_z_ref = refs
    mine_ref[...] = values[:rows]
    y_ref[...] = values[rows + half : 2 * rows]
    z_ref[...] = values[2 * rows : 2 * rows + half]
    send_y_ref[:half] = low(values[rows : rows + half])
    send_y_ref[half:] = low(values[3 * rows : 3 * rows + half])
    send_z_ref[:half] = low(values[2 * rows + half : 3 * rows])
    send_z_ref[half:] = low(values[3 * rows + half :])


def down_last(first, hidden, w_down_t):
    count, depth = first.shape
    tile = depth // 3

    def kernel(first_ref, hidden_ref, weight_ref, *out_refs):
        store_square(
            first_ref[...] + fdot(hidden_ref[...], weight_ref[...], ((1,), (1,))), out_refs
        )

    shapes = square_shapes(count, depth)
    return pl.pallas_call(
        kernel,
        out_shape=shapes,
        grid=(depth // tile,),
        in_specs=[
            pl.BlockSpec((count, tile), lambda j: (0, j)),
            pl.BlockSpec(hidden.shape, lambda j: (0, 0)),
            pl.BlockSpec((tile, w_down_t.shape[1]), lambda j: (j, 0)),
        ],
        out_specs=[pl.BlockSpec((shape.shape[0], tile), lambda j: (0, j)) for shape in shapes],
        compiler_params=pltpu.CompilerParams(vmem_limit_bytes=48 << 20),
        cost_estimate=TINY,
    )(first, hidden, w_down_t)


def feed_forward_back(grad_rows, e_down, s_gate_up, keep, chunks):
    count, depth = grad_rows.shape
    tiles = [chunk[0].shape[1] // 2 for chunk in chunks]
    columns = depth // 3
    steps = []
    for i, chunk in enumerate(chunks):
        steps += [(i, j) for j in range(chunk[0].shape[1] // tiles[i])]
    total = len(steps)
    firsts = [steps.index((i, 0)) for i in range(len(chunks))]
    counts = [chunk[0].shape[1] // tiles[i] for i, chunk in enumerate(chunks)]
    starts = [sum(chunk[0].shape[1] for chunk in chunks[:i]) for i in range(len(chunks))]
    width = sum(chunk[0].shape[1] for chunk in chunks)
    twice = e_down.shape[0]
    each = len(chunks[0])
    parts = square_shapes(count, depth)

    def kernel(grad_ref, e_down_ref, s_ref, keep_ref, *refs):
        ins = refs[: each * len(chunks)]
        out_refs = refs[each * len(chunks) :]
        rows_refs = out_refs[: len(parts)]
        inner_grad_ref, inner_ref, gates_ref, ups_ref, sums_ref = out_refs[len(parts) :]
        step = pl.program_id(0)

        @pl.when(step == 0)
        def _():
            inner_grad = fdot(grad_ref[...], e_down_ref[...], ((1,), (1,)))
            inner_grad_ref[...] = low(inner_grad * keep_ref[:, :twice])
            sums_ref[...] = jnp.zeros_like(sums_ref)

        def one(i, down, gate_in, up_in, s_down, e_gate, e_up, gate_w, up_w):
            place = pl.ds(pl.multiple_of(starts[i] + (step - firsts[i]) * tiles[i], 128), tiles[i])
            grad = fdot(grad_ref[...], down[...]) + fdot(inner_grad_ref[...], s_down[...])
            grad_gate = low(grad * gate_in[...].astype(jnp.float32))
            grad_up = low(grad * up_in[...].astype(jnp.float32))
            gates_ref[:, place] = grad_gate
            ups_ref[:, place] = grad_up
            first = fdot(grad_gate, e_gate[...], ((1,), (1,)))
            second = fdot(grad_up, e_up[...], ((1,), (1,)))
            sums_ref[:, :twice] += first
            sums_ref[:, twice:] += second

        for i in range(len(chunks)):
            within = (step >= firsts[i]) & (step < firsts[i] + counts[i])
            pl.when(within)(functools.partial(one, i, *ins[i * each : (i + 1) * each]))

        @pl.when(step == total - 1)
        def _():
            inner_ref[...] = low(sums_ref[...] * keep_ref[...])

        @pl.when(step >= total)
        def _():
            rows = fdot(inner_ref[...], s_ref[...])
            for i, chunk in enumerate(chunks):
                gate_w, up_w = ins[(i + 1) * each - 2 : (i + 1) * each]
                place = slice(starts[i], starts[i] + chunk[0].shape[1])
                rows += fdot(gates_ref[:, place], gate_w[...], ((1,), (1,)))
                rows += fdot(ups_ref[:, place], up_w[...], ((1,), (1,)))
            store_square(rows, rows_refs)

    once = pl.Buffered(1)
    whole = lambda array: pl.BlockSpec(array.shape, lambda j: (0, 0), pipeline_mode=once)
    second = lambda j: jnp.clip(j - total, 0, depth // columns - 1)

    def column(i, array):
        return pl.BlockSpec(
            (array.shape[0], tiles[i]),
            lambda j: (0, jnp.clip(j - firsts[i], 0, counts[i] - 1)),
        )

    def specs(i, chunk):
        return [column(i, array) for array in chunk[:-2]] + [
            pl.BlockSpec((columns, array.shape[1]), lambda j: (second(j), 0))
            for array in chunk[-2:]
        ]

    return pl.pallas_call(
        kernel,
        out_shape=parts
        + [
            jax.ShapeDtypeStruct((count, twice), jnp.bfloat16),
            jax.ShapeDtypeStruct((count, 2 * twice), jnp.bfloat16),
            jax.ShapeDtypeStruct((count, width), jnp.bfloat16),
            jax.ShapeDtypeStruct((count, width), jnp.bfloat16),
        ],
        grid=(total + depth // columns,),
        in_specs=[
            whole(grad_rows),
            whole(e_down),
            pl.BlockSpec((s_gate_up.shape[0], columns), lambda j: (0, second(j))),
            whole(keep),
        ]
        + [spec for i, chunk in enumerate(chunks) for spec in specs(i, chunk)],
        out_specs=[
            pl.BlockSpec((part.shape[0], columns), lambda j: (0, second(j))) for part in parts
        ]
        + [
            pl.BlockSpec((count, twice), lambda j: (0, 0)),
            pl.BlockSpec((count, 2 * twice), lambda j: (0, 0)),
            pl.BlockSpec((count, width), lambda j: (0, 0), pipeline_mode=once),
            pl.BlockSpec((count, width), lambda j: (0, 0), pipeline_mode=once),
        ],
        scratch_shapes=[pltpu.VMEM((count, 2 * twice), jnp.float32)],
        compiler_params=pltpu.CompilerParams(vmem_limit_bytes=63 << 20),
        cost_estimate=TINY,
    )(grad_rows, e_down, s_gate_up, keep, *[array for chunk in chunks for array in chunk])


def scatter_pair(part):
    rows = part.shape[0] // 2
    got = flip(low(part[rows:]), "tensor", 2)
    return part[:rows] + got.astype(jnp.float32)


def gather_pair(own):
    return jnp.concatenate([own, flip(own, "tensor", 2)])


def gather_square(own):
    half = own.shape[0] // 2
    from_y = flip(own, "tensor", 2)
    from_z = flip(own, "dp", 2)
    send_z, send_y = settle(from_y[:half], from_z[half:])
    diagonal = [flip(send_z, "dp", 2), flip(send_y, "tensor", 2)]
    return jnp.concatenate([own, from_y, from_z] + diagonal)


def sum_by_adapter(ids, gathered, shared, widths):
    count, rows, columns = gathered.shape
    cuts = [0, shared] + [shared + sum(widths[: i + 1]) for i in range(len(widths))]

    def kernel(ids_ref, gathered_ref, *refs):
        out_refs, total_ref = refs[:-1], refs[-1]
        total_refs = [total_ref] + list(out_refs[1:])
        for ref in total_refs:
            ref[...] = jnp.zeros_like(ref)
        for entry in range(count):
            adapter = ids_ref[entry]
            for i, ref in enumerate(total_refs):
                ref[adapter] += gathered_ref[entry, :, cuts[i] : cuts[i + 1]].astype(jnp.float32)
        out_refs[0][...] = low(total_ref[...])

    shapes = [jax.ShapeDtypeStruct((ADAPTERS, rows, shared), jnp.bfloat16)] + [
        jax.ShapeDtypeStruct((ADAPTERS, rows, width), jnp.float32) for width in widths
    ]
    return pl.pallas_call(
        kernel,
        out_shape=shapes,
        in_specs=[
            pl.BlockSpec(memory_space=pltpu.SMEM),
            pl.BlockSpec(gathered.shape, lambda: (0, 0, 0)),
        ],
        out_specs=[pl.BlockSpec(shape.shape, lambda: (0, 0, 0)) for shape in shapes],
        scratch_shapes=[pltpu.VMEM((ADAPTERS, rows, shared), jnp.float32)],
        compiler_params=pltpu.CompilerParams(vmem_limit_bytes=40 << 20),
        cost_estimate=TINY,
    )(ids, gathered)


def sum_unit_grads(hots, gathered, kinds):
    count, rows, columns = gathered.shape
    rank = rows // kinds
    adapters = hots.shape[2]

    def kernel(hots_ref, gathered_ref, *out_refs):
        for side in range(2):
            for kind in range(kinds):
                here = slice(kind * rank, (kind + 1) * rank)

                @pl.loop(0, adapters)
                def _(adapter):
                    total = 0.0
                    for entry in range(count):
                        total += hots_ref[side, entry, adapter] * gathered_ref[
                            entry, here
                        ].astype(jnp.float32)
                    out_refs[kind][adapter, :, side * columns : (side + 1) * columns] = total

    return pl.pallas_call(
        kernel,
        out_shape=[jax.ShapeDtypeStruct((adapters, rank, 2 * columns), jnp.float32)] * kinds,
        in_specs=[
            pl.BlockSpec(memory_space=pltpu.SMEM),
            pl.BlockSpec(gathered.shape, lambda: (0, 0, 0)),
        ],
        out_specs=[pl.BlockSpec((adapters, rank, 2 * columns), lambda: (0, 0, 0))] * kinds,
        compiler_params=pltpu.CompilerParams(vmem_limit_bytes=48 << 20),
        cost_estimate=TINY,
    )(hots, gathered)


def join_halves(core, mine, other, kinds):
    adapters, rank, columns = mine.shape
    half = columns // kinds

    def kernel(core_ref, mine_ref, other_ref, *out_refs):
        swap = core_ref[0] == 1
        for kind in range(kinds):
            here = slice(kind * half, (kind + 1) * half)
            first = mine_ref[:, :, here].astype(jnp.float32)
            second = other_ref[:, :, here].astype(jnp.float32)
            out_refs[kind][:, :, :half] = jnp.where(swap, second, first)
            out_refs[kind][:, :, half:] = jnp.where(swap, first, second)

    return pl.pallas_call(
        kernel,
        out_shape=[jax.ShapeDtypeStruct((adapters, rank, 2 * half), jnp.float32)] * kinds,
        in_specs=[pl.BlockSpec(memory_space=pltpu.SMEM)]
        + [pl.BlockSpec(mine.shape, lambda: (0, 0, 0))] * 2,
        out_specs=[pl.BlockSpec((adapters, rank, 2 * half), lambda: (0, 0, 0))] * kinds,
        compiler_params=pltpu.CompilerParams(vmem_limit_bytes=48 << 20),
        cost_estimate=TINY,
    )(core, mine, other)


def square_first(parts):
    mine, to_y, to_z, send_y, send_z = parts
    return (flip(send_y, "tensor", 2), flip(send_z, "dp", 2)), (mine, to_y, to_z)


def square_last(first, rest):
    got_y, got_z = (got.astype(jnp.float32) for got in first)
    mine, to_y, to_z = rest
    half = to_y.shape[0]
    send_y, send_z = settle(low(to_y + got_z[half:]), low(to_z + got_y[half:]))
    last_y = flip(send_y, "tensor", 2).astype(jnp.float32)
    last_z = flip(send_z, "dp", 2).astype(jnp.float32)
    return jnp.concatenate(
        [mine[:half] + got_y[:half] + last_z, mine[half:] + got_z[:half] + last_y]
    )


def tree_bits(trees):
    return [1 << b for b in range(1, trees.bit_length() - 1)][::-1] + [1]


def tree_order(trees):
    bits = tree_bits(trees)
    order = [0]
    for bit in bits[-1:] + bits[:-1]:
        order += [i ^ bit for i in order]
    return order


def on_device(
    layer_input,
    cotangent,
    norm_gains,
    w_query,
    w_key,
    w_value,
    w_output,
    w_gate,
    w_up,
    w_down,
    query_shrink,
    key_shrink,
    value_shrink,
    output_shrink,
    gate_shrink,
    up_shrink,
    down_shrink,
    query_expand,
    key_expand,
    value_expand,
    output_expand,
    gate_expand,
    up_expand,
    down_expand,
    adapter_ids,
    parent_segments,
    segment_ids,
):
    trees = lax.axis_size("dp")
    columns_z = trees // 2
    my_tree = lax.axis_index("dp")
    my_z, my_x = my_tree // 2, my_tree % 2
    my_part = lax.axis_index("tensor")
    odd = my_z % 2 == 1
    norm_gain = norm_gains.astype(jnp.float32)
    place = my_x.astype(jnp.int32)[None]

    def halves(values):
        half = values.shape[-1] // 2
        return jnp.stack([values[:, :half], values[:, half:]])

    def on_core(values):
        return flip(values, "tensor", 1)

    cut = w_query.shape[0] // 2 // 16 * 16
    qkv_parts = [
        jnp.concatenate([weight[rows] for weight in (w_query, w_key, w_value)], axis=1)
        for rows in (slice(0, cut), slice(cut, None))
    ]
    gate_halves, up_halves, down_halves = halves(w_gate), halves(w_up), halves(w_down.T)
    units = gate_halves.shape[2]
    first_units = (units // 128 + 1) // 2 * 128
    waiting = [
        qkv_parts[0][None],
        qkv_parts[1][None],
        w_output.T[None],
        gate_halves[:, :, first_units:],
        up_halves[:, :, first_units:],
        gate_halves[:, :, :first_units],
        up_halves[:, :, :first_units],
        down_halves[:, :, :first_units],
        down_halves[:, :, first_units:],
    ]
    waiting = [
        jnp.concatenate([blocks] * (columns_z // blocks.shape[0])) for blocks in waiting
    ]
    count = len(waiting)
    near, cross = {}, {}

    near_core, cross_core = {}, {}

    def transfers(step):
        if step < count:
            near[step] = along_z(waiting[step], columns_z)
        if 0 <= step - 1 < count:
            cross[step - 1] = flip(near[step - 1], "dp", 1)
            near_core[step - 1] = on_core(near[step - 1])
        if 0 <= step - 2 < count:
            cross_core[step - 2] = on_core(cross[step - 2])

    def close(step, *values):
        moved = [
            (store, key)
            for store, key in (
                (near, step),
                (cross, step - 1),
                (near_core, step - 1),
                (cross_core, step - 2),
            )
            if key in store
        ]
        following = [waiting[step + 1]] if step + 1 < count else []
        moved_values, following, values = settle(
            [store[key] for store, key in moved], following, values
        )
        for (store, key), value in zip(moved, moved_values):
            store[key] = value
        if following:
            waiting[step + 1] = following[0]
        return values

    def matrix(*keys):
        stores = (near, cross, near_core, cross_core)
        return assemble([[store[key] for store in stores] for key in keys], place)

    transfers(0)
    own_rows = layer_input.astype(jnp.float32)
    normed = low(rms_scale(own_rows, norm_gain[0]))
    normed, late_ids = settle(normed, adapter_ids)
    near_ids = flip(late_ids, "dp", 2)
    labels = jnp.arange(ADAPTERS, dtype=jnp.int32)
    order = jnp.stack([my_part, my_part ^ 2, my_part ^ 1, my_part ^ 3]).astype(jnp.int32)
    visible, cos_rows, sin_rows = tree_tables(segment_ids, parent_segments[0], order)
    row_count = 2 * normed.shape[0]
    visible = low(visible[:row_count])
    cos_rows, sin_rows = cos_rows[:row_count], sin_rows[:row_count]
    ids_parts = [late_ids, flip(late_ids, "dp", 1)]
    normed, near_ids, visible, cos_rows, sin_rows, ids_parts = close(
        0, normed, near_ids, visible, cos_rows, sin_rows, ids_parts
    )

    transfers(1)
    normed_all = gather_pair(normed)
    picks = jnp.concatenate([adapter_ids, near_ids, (my_z % 2).astype(jnp.int32)[None]])
    normed_all, picks = settle(normed_all, picks)
    picked = pick_adapters(
        picks,
        [
            (stack, False)
            for stack in (
                query_shrink,
                key_shrink,
                value_shrink,
                query_expand,
                key_expand,
                value_expand,
                output_shrink,
                output_expand,
            )
        ]
        + [
            (stack, near_tree)
            for stack in (gate_shrink, up_shrink, down_expand)
            for near_tree in (False, True)
        ],
        [
            (stack, near_tree)
            for stack in (gate_expand, up_expand, down_shrink)
            for near_tree in (False, True)
        ],
    )
    s_qkv = jnp.concatenate(picked[0:3])
    e_parts = picked[3:6]
    rank = e_parts[0].shape[0]
    widths = [part.shape[1] for part in e_parts]
    attn_mine = jnp.concatenate(picked[3:7], axis=1)
    e_output = picked[7]
    s_gate_up = jnp.concatenate(picked[8:12])
    e_down = jnp.concatenate(picked[12:14])
    ffn_mine = jnp.concatenate(picked[14:20])
    for bit in tree_bits(trees)[:-2]:
        tree_ids = jnp.concatenate(ids_parts)
        ids_parts = [tree_ids, flip(tree_ids, "dp", bit)]
    normed_all, attn_mine, e_output, s_gate_up, e_down, ffn_mine, s_qkv, ids_parts = close(
        1, normed_all, attn_mine, e_output, s_gate_up, e_down, ffn_mine, s_qkv, ids_parts
    )

    transfers(2)
    attn_other = on_core(attn_mine)
    ffn_other = on_core(ffn_mine)
    inner_qkv = low(times_rows(normed_all, s_qkv))
    tree_ids = jnp.concatenate(ids_parts)
    ids_parts = [tree_ids, flip(tree_ids, "dp", 2)]
    attn_other, ffn_other, inner_qkv, ids_parts = close(
        2, attn_other, ffn_other, inner_qkv, ids_parts
    )
    tree_ids = jnp.concatenate(ids_parts)

    transfers(3)
    heads_here = sum(widths)
    queries = widths[0] // HEAD_WIDTH
    e_mine = attn_mine[:, :heads_here]
    e_other = attn_other[:, :heads_here]
    s_output = beside(attn_mine[:, heads_here:], attn_other[:, heads_here:])
    starts = [sum(widths[:i]) for i in range(4)]
    column_kind = sum(
        (jnp.arange(heads_here, dtype=jnp.int32) >= start).astype(jnp.int32)
        for start in starts[1:3]
    )
    kind_mask = (
        jnp.arange(3 * rank, dtype=jnp.int32)[:, None] // rank
        == jnp.concatenate([column_kind, column_kind])[None, :]
    )
    e_qkv = low(jnp.where(kind_mask, jnp.tile(beside(e_mine, e_other), (3, 1)), 0.0))
    units_a = beside(ffn_mine[:, :first_units], ffn_other[:, :first_units])
    units_b = beside(ffn_mine[:, first_units:], ffn_other[:, first_units:])
    adapters_ab = [
        [block[i * 2 * rank : (i + 1) * 2 * rank] for i in range(3)] for block in (units_a, units_b)
    ]
    e_qkv, s_output, adapters_ab = close(3, e_qkv, s_output, adapters_ab)

    transfers(4)
    full_qkv = matrix(0, 1)
    projected = project_heads(
        normed_all, full_qkv, inner_qkv, e_qkv, cos_rows, sin_rows, queries
    )
    received = on_core(
        beside(projected[:, heads_here + starts[1] :], projected[:, starts[1] : heads_here])
    )
    full_qkv, projected, received = close(4, full_qkv, projected, received)

    transfers(5)
    full_out_t = matrix(2)
    mixed_heads = attend(projected, received, visible, queries)
    inner_output = low(times_rows(mixed_heads, s_output))
    attn_part = times_rows(mixed_heads, full_out_t) + product(inner_output, e_output)
    attended = scatter_pair(attn_part)
    mixed_heads, full_out_t, inner_output, attended = close(
        5, mixed_heads, full_out_t, inner_output, attended
    )

    transfers(6)
    full_gate_b = matrix(3)
    residual = own_rows + rms_scale(attended, norm_gain[1])
    normed_ffn = low(rms_scale(residual, norm_gain[2]))
    normed_y = flip(normed_ffn, "tensor", 2)
    half_rows = normed_ffn.shape[0] // 2
    normed_z_first = flip(normed_ffn[:half_rows], "dp", 2)
    residual, normed_ffn, normed_y, normed_z_first, full_gate_b = close(
        6, residual, normed_ffn, normed_y, normed_z_first, full_gate_b
    )

    transfers(7)
    normed_z_last = flip(normed_ffn[half_rows:], "dp", 2)
    full_up_b = matrix(4)
    normed_zy_first = flip(normed_z_first, "tensor", 2)
    normed_z_last, normed_zy_first, full_up_b = close(
        7, normed_z_last, normed_zy_first, full_up_b
    )

    transfers(8)
    normed_zy_last = flip(normed_z_last, "tensor", 2)
    full_gate_a = matrix(5)
    ffn_rows = jnp.concatenate(
        [normed_ffn, normed_y, normed_z_first, normed_z_last, normed_zy_first, normed_zy_last]
    )
    block_rows = residual.shape[0]
    row_block = jnp.arange(4 * block_rows, dtype=jnp.int32) // block_rows
    row_near = (row_block // 2)[:, None]
    rank_near = (jnp.arange(4 * rank, dtype=jnp.int32) // rank % 2)[None, :]
    keep_four = (row_near == rank_near).astype(jnp.float32)
    keep_two = keep_four[:, : 2 * rank]
    inner_gate_up = low(keep_four * times_rows(ffn_rows, s_gate_up))
    chunk_b = gate_and_up(
        ffn_rows, full_gate_b, full_up_b, inner_gate_up, adapters_ab[1][0], adapters_ab[1][1]
    )
    ffn_rows, inner_gate_up, chunk_b, full_gate_a = close(
        8, ffn_rows, inner_gate_up, chunk_b, full_gate_a
    )

    transfers(9)
    full_up_a = matrix(6)
    chunk_a = gate_and_up(
        ffn_rows, full_gate_a, full_up_a, inner_gate_up, adapters_ab[0][0], adapters_ab[0][1]
    )
    chunk_out = [chunk_a, chunk_b]
    hidden = [parts[0] for parts in chunk_out]
    inner_down = low(
        keep_two
        * (times_rows(hidden[0], adapters_ab[0][2]) + times_rows(hidden[1], adapters_ab[1][2]))
    )
    full_down_a = matrix(7)
    ffn_first = times_rows(hidden[0], full_down_a) + product(inner_down, e_down)
    chunk_out, inner_down, ffn_first = close(9, chunk_out, inner_down, ffn_first)
    hidden = [parts[0] for parts in chunk_out]

    cross_core[8] = on_core(cross[8])
    full_down_b = matrix(8)
    ffn_out = square_last(*square_first(down_last(ffn_first, hidden[1], full_down_b)))
    layer_output = low(residual + rms_scale(ffn_out, norm_gain[3]))

    grad_out = cotangent.astype(jnp.float32)
    grad_ffn = gather_square(low(rms_back(ffn_out, norm_gain[3], grad_out)))
    *grad_normed_parts, grad_inner_down, grad_inner_gate_up, grad_gate, grad_up = feed_forward_back(
        grad_ffn,
        e_down,
        s_gate_up,
        keep_four,
        [
            (full_down, *parts[1:], adapters[2], adapters[0], adapters[1], full_gate, full_up)
            for full_down, full_gate, full_up, parts, adapters in (
                (full_down_a, full_gate_a, full_up_a, chunk_out[0], adapters_ab[0]),
                (full_down_b, full_gate_b, full_up_b, chunk_out[1], adapters_ab[1]),
            )
        ],
    )
    def from_other_core(mine, other):
        return low(mine + on_core(low(other)).astype(jnp.float32))

    parts_first, parts_rest = square_first(grad_normed_parts)
    grad_shrink_down = jnp.concatenate(
        [over_rows(grad_inner_down, units_of) for units_of in hidden], axis=1
    )
    inner_gate, inner_up = inner_gate_up[:, : 2 * rank], inner_gate_up[:, 2 * rank :]
    grad_units = jnp.stack(
        [
            grads.reshape(2, rank, 2 * units)
            for grads in (
                over_rows(inner_gate, grad_gate),
                over_rows(inner_up, grad_up),
                grad_shrink_down,
            )
        ],
        axis=1,
    ).reshape(6 * rank, 2 * units)
    rest = units - first_units
    cuts = [0, first_units, 2 * first_units, 2 * first_units + rest, 2 * units]
    quarters = [grad_units[:, cuts[i] : cuts[i + 1]] for i in range(4)]
    mine, other = beside(quarters[0], quarters[2]), beside(quarters[1], quarters[3])
    local = from_other_core(mine, other)
    parts_first, local, grad_inner_gate_up, grad_ffn = settle(
        parts_first, local, grad_inner_gate_up, grad_ffn
    )
    local_all = jnp.stack([local, flip(local, "dp", 1)])
    grad_expand_down = over_rows(inner_down, grad_ffn)
    grad_shrink_gate_up = over_rows(grad_inner_gate_up, ffn_rows)
    grad_normed_ffn = square_last(parts_first, parts_rest)
    grad_resid = grad_out + rms_back(residual, norm_gain[2], grad_normed_ffn)
    grad_attn_mine = low(rms_back(attended, norm_gain[1], grad_resid))
    shared = jnp.concatenate([grad_shrink_gate_up, grad_expand_down]).reshape(3, 2, rank, -1)
    grad_attn_mine, grad_resid, local_all, shared = settle(
        grad_attn_mine, grad_resid, local_all, shared
    )

    def core_half(blocks):
        half = blocks.shape[-1] // 2
        kept = jnp.where(my_part % 2 == 1, blocks[..., half:], blocks[..., :half])
        return jnp.concatenate([low(block) for block in kept], axis=1)

    def with_bit(values, bit):
        return jnp.concatenate([values, flip(values, "dp", bit)])

    grad_attn = gather_pair(grad_attn_mine)
    shared_near = flip(low(shared[:, 1]), "dp", 2)
    bits = tree_bits(trees)
    for bit in bits[:-2]:
        local_all = with_bit(local_all, bit)
    grad_attn, local_all, shared, shared_near = settle(grad_attn, local_all, shared, shared_near)

    local_near = flip(local_all, "dp", bits[-2])
    grad_inner_output = low(times_rows(grad_attn, e_output))
    grad_mixed = low(product(grad_attn, full_out_t) + product(grad_inner_output, s_output))
    grad_queries, grad_pairs, to_core = attend_back(
        projected, received, visible, grad_mixed, cos_rows, sin_rows, queries
    )
    pair = 2 * HEAD_WIDTH
    from_core = on_core(to_core)
    shared = shared[:, 0] + shared_near.astype(jnp.float32)
    shared = shared + on_core(low(shared)).astype(jnp.float32)
    shared = shared + flip(low(shared), "tensor", 2).astype(jnp.float32)
    shared_mine = core_half(shared)
    from_core, grad_queries, grad_pairs, shared_mine = settle(
        from_core, grad_queries, grad_pairs, shared_mine
    )

    shared_all = shared_mine[None]
    for bit in bits[:-2]:
        shared_all = with_bit(shared_all, bit)
    grad_expand_output = over_rows(inner_output, grad_attn)
    grad_shrink_output = over_rows(grad_inner_output, mixed_heads)
    grad_pairs = grad_pairs + from_core.astype(jnp.float32)
    grad_sides = []
    for side in range(2):
        keys_values = grad_pairs[:, side * pair : (side + 1) * pair]
        grad_sides += [
            grad_queries[:, side * widths[0] : (side + 1) * widths[0]],
            low(turn(keys_values[:, :HEAD_WIDTH], cos_rows, -sin_rows)),
            low(keys_values[:, HEAD_WIDTH:]),
        ]
    grad_qkv = jnp.concatenate(grad_sides, axis=1)
    grad_inner_qkv = low(times_rows(grad_qkv, e_qkv))
    grad_expand_qkv = over_rows(inner_qkv, grad_qkv)
    last = jnp.concatenate(
        [over_rows(grad_inner_qkv, normed_all), grad_expand_output]
    ).reshape(4, rank, -1)
    pieces = []
    for side in range(2):
        for i in range(3):
            first = side * heads_here + starts[i]
            pieces.append(grad_expand_qkv[i * rank : (i + 1) * rank, first : first + widths[i]])
        pieces.append(grad_shrink_output[:, side * widths[0] : (side + 1) * widths[0]])
    local_attn = from_other_core(
        jnp.concatenate(pieces[:4], axis=1), jnp.concatenate(pieces[4:], axis=1)
    )
    last = last + on_core(low(last)).astype(jnp.float32)
    last, local_attn, grad_qkv, grad_inner_qkv, shared_all = settle(
        last, local_attn, grad_qkv, grad_inner_qkv, shared_all
    )

    last_y = flip(low(last), "tensor", 2)
    shared_all = with_bit(shared_all, bits[-2])
    part = times_rows(grad_qkv, full_qkv) + product(grad_inner_qkv, s_qkv)
    last_y, part, shared_all, local_near = settle(last_y, part, shared_all, local_near)

    last_mine = beside(core_half(last + last_y.astype(jnp.float32)), local_attn)
    last_all = lax.all_to_all(
        jnp.broadcast_to(last_mine[None], (trees,) + last_mine.shape), "dp", 0, 0
    )
    from_y = flip(low(part[block_rows:]), "tensor", 2)
    shared_all = with_bit(shared_all, 1)
    from_y, shared_all = settle(from_y, shared_all)
    grad_normed = part[:block_rows] + from_y.astype(jnp.float32)
    input_grad = grad_resid + rms_back(own_rows, norm_gain[0], grad_normed)
    local_all = jnp.concatenate([local_all, local_near])

    tree_ids = tree_ids.reshape(trees)
    hot_near = (tree_ids[:, None] == labels[None, :]).astype(jnp.float32)
    distances = my_tree ^ jnp.arange(trees, dtype=jnp.int32)
    place_of = jnp.stack(
        [jnp.asarray(tree_order(trees).index(j), jnp.int32) for j in range(trees)]
    )
    at = jnp.sum(
        jnp.where(
            distances[:, None] == jnp.arange(trees, dtype=jnp.int32)[None, :], place_of[None, :], 0
        ),
        axis=1,
    )
    ids_trees = jnp.sum(
        jnp.where(
            at[:, None] == jnp.arange(trees, dtype=jnp.int32)[None, :], tree_ids[None, :], 0
        ),
        axis=1,
    )
    order_local = [0, 1]
    for bit in bits[:-1]:
        order_local += [i ^ bit for i in order_local]
    ids_at = {tree: i for i, tree in enumerate(tree_order(trees))}
    hots, crossing = [], []
    for j in order_local:
        for near_tree in range(2):
            hots.append(hot_near[ids_at[j ^ (2 * near_tree)]])
            crossing.append((j // 2) % 2)
    hots = jnp.stack(hots)
    parity = jnp.asarray(crossing, jnp.int32) ^ (my_z % 2).astype(jnp.int32)
    local_all = local_all.reshape(2 * trees, 3 * rank, units)
    hots = jnp.stack([jnp.where(parity[:, None] == side, hots, 0.0) for side in range(2)])
    ids_shared = tree_ids.reshape(2, trees // 4, 2).transpose(2, 0, 1).reshape(trees)
    out_expand_gate, out_expand_up, out_shrink_down = sum_unit_grads(hots, local_all, 3)
    core = (my_part % 2).astype(jnp.int32)[None]
    depth_half = s_qkv.shape[1] // 2
    (sums,) = sum_by_adapter(ids_shared, shared_all, 3 * depth_half, [])
    out_shrink_gate, out_shrink_up, out_expand_down = join_halves(core, sums, on_core(sums), 3)
    (last_all, input_grad, out_expand_gate, out_expand_up, out_shrink_down, out_shrink_gate,
     out_shrink_up, out_expand_down) = settle(
        last_all, input_grad, out_expand_gate, out_expand_up, out_shrink_down, out_shrink_gate,
        out_shrink_up, out_expand_down,
    )
    sums, out_expand_query, out_expand_key, out_expand_value, out_shrink_output = sum_by_adapter(
        ids_trees, last_all, 4 * depth_half, widths + widths[:1]
    )
    out_shrink_query, out_shrink_key, out_shrink_value, out_expand_output = join_halves(
        core, sums, on_core(sums), 4
    )
    return (
        layer_output,
        input_grad,
        out_shrink_query,
        out_shrink_key,
        out_shrink_value,
        out_shrink_output,
        out_shrink_gate,
        out_shrink_up,
        out_shrink_down,
        out_expand_query,
        out_expand_key,
        out_expand_value,
        out_expand_output,
        out_expand_gate,
        out_expand_up,
        out_expand_down,
    )


def solution(mesh):
    placed = (
        P(("dp", "tensor"), None),
        P(("dp", "tensor"), None),
        P(),
        P("dp", "tensor"),
        P("dp", "tensor"),
        P("dp", "tensor"),
        P("tensor", "dp"),
        P("dp", "tensor"),
        P("dp", "tensor"),
        P("tensor", "dp"),
        P(),
        P(),
        P(),
        P(None, None, "tensor"),
        P(),
        P(),
        P(None, None, "tensor"),
        P(None, None, "tensor"),
        P(None, None, "tensor"),
        P(None, None, "tensor"),
        P(),
        P(None, None, "tensor"),
        P(None, None, "tensor"),
        P(),
        P("dp"),
        P("dp", None),
        P("dp"),
    )
    return jax.shard_map(
        on_device,
        mesh=mesh,
        in_specs=placed,
        out_specs=(
            P(("dp", "tensor"), None),
            P(("dp", "tensor"), None),
            P(),
            P(),
            P(),
            P(None, None, "tensor"),
            P(),
            P(),
            P(None, None, "tensor"),
            P(None, None, "tensor"),
            P(None, None, "tensor"),
            P(None, None, "tensor"),
            P(),
            P(None, None, "tensor"),
            P(None, None, "tensor"),
            P(),
        ),
        check_vma=False,
    )
```
